128 devices in a mesh: dp: 4 (over y_lo, core), seq: 32 (over x, y_hi, z).
Axes of the slice: x: 4, y: 4 (y_hi: 2, y_lo: 2; y = y_hi * 2 + y_lo), z: 4, core: 2. Of those that a mesh axis runs over, the one named last changes fastest.
Arguments:
- tokens: bfloat16 [4, 16384, 2048], P('dp', 'seq'), may hold values from -5 to 5, as said below
- gain_first: float32 [2048], replicated, may hold values from 0.25 to 1.75
- inputs_first: bfloat16 [2048, 3072], P(('dp', 'seq')), may hold values from -1 to 1, as said below
- output_first: bfloat16 [1024, 2048], P(('dp', 'seq')), may hold values from -0.5 to 0.5
- gain_second: float32 [2048], replicated, may hold values from 0.25 to 1.75
- inputs_second: bfloat16 [2048, 3072], P(('dp', 'seq')), may hold values from -1 to 1, as said below
- output_second: bfloat16 [1024, 2048], P(('dp', 'seq')), may hold values from -0.5 to 0.5
- starts: int32 [4, 32], P('dp'), may hold values from 0 to 32256, as said below
- band_edges: int32 [2], replicated, may hold values from 4 to 62, as said below
Outputs:
- layer_out: bfloat16 [4, 16384, 2048], P('dp', 'seq')
The draws below stay inside these ranges and needn't reach their ends.
Inputs may be any that keep to these rules, and one draw needn't show every extreme that they name: `tokens`: entries are real-valued and lie within -5 to 5. `inputs_first`: entries lie within -6 / sqrt(2048) to 6 / sqrt(2048). `inputs_second`: entries lie within -6 / sqrt(2048) to 6 / sqrt(2048). `starts`: along a sequence each start exceeds the one before by 512 to 1024; the first is at most 512. band_edges[0] < band_edges[1], with at least 4 between them; band_edges[1] is 62.
All inputs are finite; a program needn't handle non-finite values.
Results may differ from the reference program's by a relative error of at most 0.025.
Values may be sent and summed in bfloat16 or wider, within the bound.
No kernel may reach another device: no remote copies, remote signals or barrier semaphores. Data moves between devices by JAX's collectives and lax.ppermute only.
A program may use at most 128 MiB of HBM per device.

```python
import math
import jax
import jax.numpy as jnp
from jax import lax

D = 2048
HEADS = 8
HEAD = 128
C = 512
SCALE = 8
ROWS_DEV = 1
BATCH = 4
N_SEQ = 32


def draw_tokens(key, part):
    own_key = jax.random.fold_in(key, 11)
    full_shape = (BATCH, ROWS_DEV * N_SEQ * C, D)
    return (0.5 * jnp.clip(jax.random.normal(own_key, full_shape, jnp.float32), -6.0, 6.0)).astype(jnp.bfloat16)


def draw_projection(key, which):
    own_key = jax.random.fold_in(key, which)
    full_shape = (D, 3 * HEADS * HEAD)
    spread = 1.0 / math.sqrt(D)
    return (jnp.clip(jax.random.normal(own_key, full_shape, jnp.float32), -6.0, 6.0) * spread).astype(jnp.bfloat16)


def draw_inputs_first(key, part):
    return draw_projection(key, 1)


def draw_inputs_second(key, part):
    return draw_projection(key, 2)


def draw_starts(key, part):
    own_key = jax.random.fold_in(key, 21)
    block = ROWS_DEV * C
    gap_draw = jax.random.randint(own_key, (BATCH, N_SEQ), 0, block + 1)
    gap_draw = gap_draw.at[0, :].set(block)
    strides = gap_draw + block
    first_gap = gap_draw[:, 0].at[1].set(0)
    strides = strides.at[:, 0].set(first_gap)
    return jnp.cumsum(strides, axis=1).astype(jnp.int32)


def draw_band_edges(key, part):
    own_key = jax.random.fold_in(key, 31)
    lower_edge = jax.random.randint(own_key, (), 4, HEAD // 4)
    upper_edge = jnp.zeros((), jnp.int32) + (HEAD // 2 - 2)
    return jnp.stack([lower_edge, upper_edge]).astype(jnp.int32)


def shard_levels(key, shape, pieces, low, high):
    def one(axis_at, shards_of):
        draws = jax.random.uniform(jax.random.fold_in(jax.random.fold_in(key, 6), axis_at), (shards_of,), jnp.float32, low / len(pieces), high / len(pieces))
        return jnp.repeat(jnp.exp(draws), shape[axis_at] // shards_of).reshape((-1,) + (1,) * (len(shape) - axis_at - 1))

    level = one(*pieces[0])
    for cut in pieces[1:]:
        level = level * one(*cut)
    return level


def normal_values(rng, extent, deviation, limit, shards=(), kind=jnp.bfloat16):
    entries = deviation * jax.random.normal(rng, extent, jnp.float32)
    if shards:
        entries = entries * shard_levels(rng, extent, shards, -0.22, 0.18)
    return jnp.clip(entries, -limit, limit).astype(kind)


def setup_inputs(seed: int = 0) -> dict:
    arg_keys = jax.random.split(jax.random.key(seed), 10)
    tokens = draw_tokens(jax.random.fold_in(arg_keys[9], 71), 0)
    gain_first = jnp.clip(1.0 + 0.15 * jax.random.normal(arg_keys[1], (D,), jnp.float32), 0.25, 1.75)
    inputs_first = draw_inputs_first(jax.random.fold_in(arg_keys[9], 71), 0)
    output_first = normal_values(arg_keys[3], (HEADS * HEAD, D), HEAD ** -0.5, 0.5, ((0, 128),))
    gain_second = jnp.clip(1.0 + 0.15 * jax.random.normal(arg_keys[4], (D,), jnp.float32), 0.25, 1.75)
    inputs_second = draw_inputs_second(jax.random.fold_in(arg_keys[9], 71), 0)
    output_second = normal_values(arg_keys[6], (HEADS * HEAD, D), HEAD ** -0.5, 0.5, ((0, 128),))
    starts = draw_starts(jax.random.fold_in(arg_keys[9], 71), 0)
    band_edges = draw_band_edges(jax.random.fold_in(arg_keys[9], 71), 0)
    return dict(tokens=tokens, gain_first=gain_first, inputs_first=inputs_first, output_first=output_first, gain_second=gain_second, inputs_second=inputs_second, output_second=output_second, starts=starts, band_edges=band_edges)


def normed(values, gain):
    as_float = values.astype(jnp.float32)
    inv_rms = lax.rsqrt(lax.optimization_barrier(jnp.mean(as_float * as_float, axis=-1, keepdims=True)) + 1e-05)
    return (as_float * inv_rms * gain).astype(jnp.bfloat16)

def frequencies(band_edges, half_size):
    dim_index = jnp.arange(half_size, dtype=jnp.float32)
    base_freq = jnp.power(10000.0, -dim_index / half_size)
    lower_edge = band_edges[0].astype(jnp.float32)
    upper_edge = band_edges[1].astype(jnp.float32)
    ramp_share = jnp.clip((dim_index - lower_edge) / (upper_edge - lower_edge), 0.0, 1.0)
    return base_freq * (1.0 - ramp_share) + base_freq * ramp_share / SCALE

def rotary(projected, positions, frequency):
    half_size = frequency.shape[0]
    angles = positions.astype(jnp.float32)[..., None] * frequency
    mscale = 0.1 * math.log(SCALE) + 1.0
    cosine = (jnp.cos(angles) * mscale)[..., None, :]
    sine_part = (jnp.sin(angles) * mscale)[..., None, :]
    first_half = projected[..., :half_size]
    second_half = projected[..., half_size:]
    return jnp.concatenate([first_half * cosine - second_half * sine_part, second_half * cosine + first_half * sine_part], axis=-1).astype(jnp.bfloat16)

def softmax_rows(scores):
    row_max = lax.optimization_barrier(jnp.max(scores, axis=-1, keepdims=True))
    weights = jnp.exp(scores - row_max)
    return (weights / lax.optimization_barrier(jnp.sum(weights, axis=-1, keepdims=True))).astype(jnp.bfloat16)

def row_heads(triple):
    queries, key_rows, values = triple
    length = queries.shape[0]
    scores = jnp.einsum('qhd,khd->hqk', queries.astype(jnp.float32), key_rows.astype(jnp.float32)) / math.sqrt(HEAD)
    causal = jnp.arange(length)[None, :] <= jnp.arange(length)[:, None]
    scores = jnp.where(causal[None], scores, -1e+30)
    probability = softmax_rows(scores)
    return jnp.einsum('hqk,khd->qhd', probability.astype(jnp.float32), values.astype(jnp.float32)).astype(jnp.bfloat16)

def column_attention(queries, key_rows, values):
    length = queries.shape[0]
    scores = jnp.einsum('rchd,schd->chrs', queries.astype(jnp.float32), key_rows.astype(jnp.float32)) / math.sqrt(HEAD)
    causal = jnp.arange(length)[None, :] <= jnp.arange(length)[:, None]
    scores = jnp.where(causal[None, None], scores, -1e+30)
    probability = softmax_rows(scores)
    return jnp.einsum('chrs,schd->rchd', probability.astype(jnp.float32), values.astype(jnp.float32)).astype(jnp.bfloat16)

def reference(tokens, gain_first, inputs_first, output_first, gain_second, inputs_second, output_second, starts, band_edges):
    frequency = frequencies(band_edges, HEAD // 2)
    grid_rows = ROWS_DEV * N_SEQ
    attn_width = HEADS * HEAD

    def one_sequence(inputs_pair):
        residual, block_starts = inputs_pair
        positions = (block_starts[:, None] + jnp.arange(ROWS_DEV * C, dtype=jnp.int32)[None, :]).reshape(grid_rows, C)
        hidden = normed(residual, gain_first)
        projected = jnp.dot(hidden, inputs_first, preferred_element_type=jnp.float32).reshape(grid_rows, C, 3, HEADS, HEAD)
        queries = rotary(projected[:, :, 0], positions, frequency)
        key_rows = rotary(projected[:, :, 1], positions, frequency)
        values = projected[:, :, 2].astype(jnp.bfloat16)
        attended = lax.map(row_heads, (queries, key_rows, values)).reshape(grid_rows * C, attn_width)
        branch = jnp.dot(attended, output_first, preferred_element_type=jnp.float32)
        middle = (residual.astype(jnp.float32) + branch).astype(jnp.bfloat16)
        hidden = normed(middle, gain_second)
        projected = jnp.dot(hidden, inputs_second, preferred_element_type=jnp.float32).reshape(grid_rows, C, 3, HEADS, HEAD)
        queries = rotary(projected[:, :, 0], positions, frequency)
        key_rows = rotary(projected[:, :, 1], positions, frequency)
        values = projected[:, :, 2].astype(jnp.bfloat16)
        attended = column_attention(queries, key_rows, values).reshape(grid_rows * C, attn_width)
        branch = jnp.dot(attended, output_second, preferred_element_type=jnp.float32)
        return (middle.astype(jnp.float32) + branch).astype(jnp.bfloat16)
    return lax.map(one_sequence, (tokens, starts))
```

```python
import math

import jax
import jax.numpy as jnp
from jax import lax
from jax.experimental import pallas as pl
from jax.experimental.pallas import tpu as pltpu
from jax.sharding import Mesh, PartitionSpec as P

HEADS = 8
HEAD = 128
C = 512
SCALE = 8
D = 2048
WIDTH = HEADS * HEAD
N_SEQ = 32
COLS = C // N_SEQ
PAIR = 2 * HEAD
STEPS = WIDTH // PAIR
ALL_CHIPS = ("ylo", "seq")
LOG2E = 1.4426950408889634
MIB = 1 << 20


def frequencies(band_edges, half_size):
    dim_index = jnp.arange(half_size, dtype=jnp.float32)
    base_freq = jnp.power(10000.0, -dim_index / half_size)
    lower_edge = band_edges[0].astype(jnp.float32)
    upper_edge = band_edges[1].astype(jnp.float32)
    ramp_share = jnp.clip((dim_index - lower_edge) / (upper_edge - lower_edge), 0.0, 1.0)
    return base_freq * (1.0 - ramp_share) + base_freq * ramp_share / SCALE


def rotary_tables(positions, frequency):
    angles = positions.astype(jnp.float32)[:, None] * frequency
    mscale = 0.1 * math.log(SCALE) + 1.0
    cosine = jnp.cos(angles) * mscale
    sine = jnp.sin(angles) * mscale
    return jnp.concatenate([cosine, cosine], -1), jnp.concatenate([-sine, sine], -1)


def dot(a, b):
    return jnp.dot(a, b, preferred_element_type=jnp.float32)


def dot_t(a, b):
    return lax.dot_general(a, b, (((1,), (1,)), ((), ())), preferred_element_type=jnp.float32)


def slot_of(block, core):
    other = jnp.where(lax.rem(block, 2) == core, 0, 2)
    return other + block // 2


def rotate(heads, cos, sin):
    return heads * cos + pltpu.roll(heads, HEAD // 2, 1) * sin


def softmax_times(scores, keep, values):
    scores = jnp.where(keep, scores, -1e30)
    top = jnp.max(scores, axis=-1, keepdims=True)
    weights = jnp.exp2((scores - top) * (LOG2E / math.sqrt(HEAD)))
    total = jnp.sum(weights, axis=-1, keepdims=True)
    return dot(weights.astype(jnp.bfloat16), values) / total


def project(hid_ref, own_ref, other_ref):
    half = own_ref.shape[0]
    return dot(hid_ref[:, :half], own_ref[...]) + dot(hid_ref[:, half:], other_ref[...])


def row_kernel(core_ref, x_ref, gain_ref, cos_ref, sin_ref, qo, ko, vo, qs, ks, vs, out_ref, hid_ref):
    core = core_ref[0]

    @pl.when(pl.program_id(0) == 0)
    def _():
        def chunk(i, _):
            rows = pl.ds(pl.multiple_of(i * 32, 32), 32)
            x = x_ref[rows, :].astype(jnp.float32)
            inv = lax.rsqrt(jnp.mean(x * x, axis=-1, keepdims=True) + 1e-05)
            hidden = (x * inv * gain_ref[...]).astype(jnp.bfloat16)
            width = D // 4
            for block in range(4):
                lanes = pl.ds(pl.multiple_of(slot_of(block, core) * width, width), width)
                hid_ref[rows, lanes] = hidden[:, block * width : (block + 1) * width]
            return 0

        lax.fori_loop(0, C // 32, chunk, 0)

    q2 = project(hid_ref, qo, qs)
    k2 = project(hid_ref, ko, ks)
    v2 = project(hid_ref, vo, vs).astype(jnp.bfloat16)
    for h in range(2):
        lanes = slice(h * HEAD, (h + 1) * HEAD)
        q = rotate(q2[:, lanes], cos_ref[...], sin_ref[...]).astype(jnp.bfloat16)
        k = rotate(k2[:, lanes], cos_ref[...], sin_ref[...]).astype(jnp.bfloat16)
        v = v2[:, lanes]
        size = 256
        for b in range(C // size):
            end = (b + 1) * size
            scores = dot_t(q[b * size : end], k[:end])
            row = lax.broadcasted_iota(jnp.int32, scores.shape, 0) + b * size
            keep = lax.broadcasted_iota(jnp.int32, scores.shape, 1) <= row
            out_ref[b * size : end, lanes] = softmax_times(scores, keep, v[:end]).astype(jnp.bfloat16)


def column_kernel(core_ref, x_ref, cos_ref, sin_ref, qo, ko, vo, qs, ks, vs, out_ref, hid_ref):
    core = core_ref[0]

    def selection(transposed):
        a = lax.broadcasted_iota(jnp.int32, (C, C), 1 if transposed else 0)
        b = lax.broadcasted_iota(jnp.int32, (C, C), 0 if transposed else 1)
        same = (a // N_SEQ == lax.rem(b, COLS)) & (lax.rem(a, N_SEQ) == b // COLS)
        return jnp.where(same, 1.0, 0.0).astype(jnp.bfloat16)

    @pl.when(pl.program_id(0) == 0)
    def _():
        pick = selection(False)
        width = D // 4
        for block in range(4):
            lanes = pl.ds(pl.multiple_of(slot_of(block, core) * width, width), width)
            moved = dot(pick, x_ref[:, block * width : (block + 1) * width])
            hid_ref[:, lanes] = moved.astype(jnp.bfloat16)

    q2 = project(hid_ref, qo, qs)
    k2 = project(hid_ref, ko, ks)
    v2 = project(hid_ref, vo, vs).astype(jnp.bfloat16)
    size = 128
    row = lax.broadcasted_iota(jnp.int32, (size, size), 0)
    col = lax.broadcasted_iota(jnp.int32, (size, size), 1)
    keep = (row // N_SEQ == col // N_SEQ) & (col <= row)
    heads = []
    for h in range(2):
        lanes = slice(h * HEAD, (h + 1) * HEAD)
        q = rotate(q2[:, lanes], cos_ref[...], sin_ref[...]).astype(jnp.bfloat16)
        k = rotate(k2[:, lanes], cos_ref[...], sin_ref[...]).astype(jnp.bfloat16)
        v = v2[:, lanes]
        blocks = []
        for b in range(C // size):
            rows = slice(b * size, (b + 1) * size)
            blocks.append(softmax_times(dot_t(q[rows], k[rows]), keep, v[rows]).astype(jnp.bfloat16))
        heads.append(jnp.concatenate(blocks, 0))
    attended = jnp.concatenate(heads, 1)
    out_ref[...] = dot(selection(True), attended).astype(jnp.bfloat16)


def attend(kernel, core, x, gain, tables, own, other):
    half = own.shape[0]

    def weight(part):
        return pl.BlockSpec((half, PAIR), lambda i: (0, part * STEPS + i))

    whole = lambda shape: pl.BlockSpec(shape, lambda i: (0, 0), pipeline_mode=pl.Buffered(1))
    specs = [pl.BlockSpec(memory_space=pltpu.SMEM), whole((C, D))]
    args = [core, x]
    if gain is not None:
        specs.append(whole((1, D)))
        args.append(gain)
    specs += [whole((C, HEAD)), whole((C, HEAD))] + [weight(p) for p in range(3)] * 2
    args += [*tables, own, own, own, other, other, other]
    return pl.pallas_call(
        kernel,
        grid=(STEPS,),
        out_shape=jax.ShapeDtypeStruct((C, WIDTH), jnp.bfloat16),
        in_specs=specs,
        out_specs=pl.BlockSpec((C, PAIR), lambda i: (0, i)),
        scratch_shapes=[pltpu.VMEM((C, D), jnp.bfloat16)],
        compiler_params=pltpu.CompilerParams(
            dimension_semantics=("arbitrary",), vmem_limit_bytes=40 * MIB
        ),
        cost_estimate=pl.CostEstimate(
            flops=2 * C * D * 3 * WIDTH + 4 * C * C * WIDTH,
            bytes_accessed=2 * (C * D + 3 * D * WIDTH + C * WIDTH),
            transcendentals=C * C * HEADS,
        ),
    )(*args)


def branch_sum(core, att_ref, own_ref, other_ref, resid_ref):
    width = WIDTH // 4
    total = resid_ref[...].astype(jnp.float32)
    for slot in range(4):
        block = jnp.where(slot < 2, core, 1 - core) + 2 * (slot % 2)
        lanes = pl.ds(pl.multiple_of(block * width, width), width)
        ref = own_ref if slot < 2 else other_ref
        rows = slice((slot % 2) * width, (slot % 2 + 1) * width)
        total = total + dot(att_ref[:, lanes], ref[rows, :])
    return total


def middle_kernel(core_ref, att_ref, own_ref, other_ref, resid_ref, gain_ref, mid_ref, hid_ref):
    middle = branch_sum(core_ref[0], att_ref, own_ref, other_ref, resid_ref).astype(jnp.bfloat16)
    mid_ref[...] = middle
    x = middle.astype(jnp.float32)
    inv = lax.rsqrt(jnp.mean(x * x, axis=-1, keepdims=True) + 1e-05)
    hid_ref[...] = (x * inv * gain_ref[...]).astype(jnp.bfloat16)


def final_kernel(core_ref, att_ref, own_ref, other_ref, resid_ref, out_ref):
    out_ref[...] = branch_sum(core_ref[0], att_ref, own_ref, other_ref, resid_ref).astype(jnp.bfloat16)


def output_layer(kernel, core, attended, own, other, resid, gain):
    size = 128
    block = lambda width: pl.BlockSpec((size, width), lambda i: (i, 0))
    whole = lambda shape: pl.BlockSpec(shape, lambda i: (0, 0), pipeline_mode=pl.Buffered(1))
    specs = [
        pl.BlockSpec(memory_space=pltpu.SMEM),
        block(WIDTH),
        whole(own.shape),
        whole(other.shape),
        block(D),
    ]
    args = [core, attended, own, other, resid]
    outs = 1
    if gain is not None:
        specs.append(whole((1, D)))
        args.append(gain)
        outs = 2
    shape = jax.ShapeDtypeStruct((C, D), jnp.bfloat16)
    return pl.pallas_call(
        kernel,
        grid=(C // size,),
        out_shape=[shape] * outs,
        in_specs=specs,
        out_specs=[block(D)] * outs,
        compiler_params=pltpu.CompilerParams(
            dimension_semantics=("arbitrary",), vmem_limit_bytes=40 * MIB
        ),
        cost_estimate=pl.CostEstimate(
            flops=2 * C * D * WIDTH,
            bytes_accessed=2 * ((1 + outs) * C * D + D * WIDTH + C * WIDTH),
            transcendentals=0,
        ),
    )(*args)


def shards(tokens, gain_first, inputs_first, output_first, gain_second, inputs_second, output_second, starts, band_edges):
    residual = tokens[0]
    core = lax.axis_index("core")
    core_scalar = core.astype(jnp.int32).reshape(1)
    seq = lax.axis_index("seq")

    def gather(weight):
        own = lax.all_gather(weight, ALL_CHIPS, axis=0, tiled=True)
        return own, lax.ppermute(own, "core", [(0, 1), (1, 0)])

    in_first = gather(inputs_first)
    out_first = gather(output_first)
    in_second = gather(inputs_second)
    out_second = gather(output_second)

    frequency = frequencies(band_edges, HEAD // 2)
    block_starts = starts[0]
    own_start = lax.dynamic_index_in_dim(block_starts, seq, 0, keepdims=False)
    row_tables = rotary_tables(own_start + jnp.arange(C, dtype=jnp.int32), frequency)
    columns = seq.astype(jnp.int32) * COLS + jnp.arange(COLS, dtype=jnp.int32)
    column_positions = (columns[:, None] + block_starts[None, :]).reshape(C)
    column_tables = rotary_tables(column_positions, frequency)

    attended = attend(row_kernel, core_scalar, residual, gain_first.reshape(1, D), row_tables, *in_first)
    middle, hidden = output_layer(
        middle_kernel, core_scalar, attended, *out_first, residual, gain_second.reshape(1, D)
    )
    hidden = lax.all_to_all(hidden, "seq", split_axis=0, concat_axis=0, tiled=True)
    attended = attend(column_kernel, core_scalar, hidden, None, column_tables, *in_second)
    attended = lax.all_to_all(attended, "seq", split_axis=0, concat_axis=0, tiled=True)
    (out,) = output_layer(final_kernel, core_scalar, attended, *out_second, middle, None)
    return out[None]


def solution(mesh):
    split = Mesh(mesh.devices.reshape(2, 2, N_SEQ), ("ylo", "core", "seq"))
    dp = ("ylo", "core")
    every = ("ylo", "core", "seq")
    return jax.shard_map(
        shards,
        mesh=split,
        in_specs=(
            P(dp, "seq", None),
            P(),
            P(every, None),
            P(every, None),
            P(),
            P(every, None),
            P(every, None),
            P(dp, None),
            P(),
        ),
        out_specs=P(dp, "seq", None),
        check_vma=False,
    )
```

```python
import math

import jax
import jax.numpy as jnp
from jax import lax
from jax.experimental import pallas as pl
from jax.experimental.pallas import tpu as pltpu
from jax.sharding import Mesh, PartitionSpec as P

HEADS = 8
HEAD = 128
C = 512
SCALE = 8
D = 2048
WIDTH = HEADS * HEAD
N_SEQ = 32
COLS = C // N_SEQ
PAIR = 2 * HEAD
STEPS = WIDTH // PAIR
SEQ = ("x", "yhi", "z")
QKV_PART = 3 * WIDTH // 2
PART = 2 * WIDTH
RELATIVE = ((0, 0, PART), (3, 0, PART), (1, 0, PART), (2, 0, PART // 2), (2, PART // 2, PART))
STACKED = (0, 3, 1, 2)
LOG2E = 1.4426950408889634
MIB = 1 << 20


def frequencies(band_edges, half_size):
    dim_index = jnp.arange(half_size, dtype=jnp.float32)
    base_freq = jnp.power(10000.0, -dim_index / half_size)
    lower_edge = band_edges[0].astype(jnp.float32)
    upper_edge = band_edges[1].astype(jnp.float32)
    ramp_share = jnp.clip((dim_index - lower_edge) / (upper_edge - lower_edge), 0.0, 1.0)
    return base_freq * (1.0 - ramp_share) + base_freq * ramp_share / SCALE


def rotary_tables(positions, frequency):
    angles = positions.astype(jnp.float32)[:, None] * frequency
    mscale = 0.1 * math.log(SCALE) + 1.0
    cosine = jnp.cos(angles) * mscale
    sine = jnp.sin(angles) * mscale
    return jnp.concatenate([cosine, cosine], -1), jnp.concatenate([-sine, sine], -1)


def dot(a, b):
    return jnp.dot(a, b, preferred_element_type=jnp.float32)


def dot_t(a, b):
    return lax.dot_general(a, b, (((1,), (1,)), ((), ())), preferred_element_type=jnp.float32)


def slot_of(block, core):
    other = jnp.where(lax.rem(block, 2) == core, 0, 2)
    return other + block // 2


def rotate(heads, cos, sin):
    return heads * cos + pltpu.roll(heads, HEAD // 2, 1) * sin


def softmax_times(scores, keep, values):
    scores = jnp.where(keep, scores, -1e30)
    top = jnp.max(scores, axis=-1, keepdims=True)
    weights = jnp.exp2((scores - top) * (LOG2E / math.sqrt(HEAD)))
    total = jnp.sum(weights, axis=-1, keepdims=True)
    return dot(weights.astype(jnp.bfloat16), values) / total


def project(hid_ref, own_ref, other_ref):
    half = own_ref.shape[0]
    return dot(hid_ref[:, :half], own_ref[...]) + dot(hid_ref[:, half:], other_ref[...])


def norm_kernel(core_ref, x_ref, gain_ref, hid_ref):
    core = core_ref[0]

    def chunk(i, _):
        rows = pl.ds(pl.multiple_of(i * 32, 32), 32)
        x = x_ref[rows, :].astype(jnp.float32)
        inv = lax.rsqrt(jnp.mean(x * x, axis=-1, keepdims=True) + 1e-05)
        hidden = (x * inv * gain_ref[...]).astype(jnp.bfloat16)
        width = D // 4
        for block in range(4):
            lanes = pl.ds(pl.multiple_of(slot_of(block, core) * width, width), width)
            hid_ref[rows, lanes] = hidden[:, block * width : (block + 1) * width]
        return 0

    lax.fori_loop(0, C // 32, chunk, 0)


def normed_slots(core, x, gain):
    vmem = pl.BlockSpec(memory_space=pltpu.VMEM)
    return pl.pallas_call(
        norm_kernel,
        out_shape=jax.ShapeDtypeStruct((C, D), jnp.bfloat16),
        in_specs=[pl.BlockSpec(memory_space=pltpu.SMEM), vmem, vmem],
        out_specs=vmem,
        compiler_params=pltpu.CompilerParams(vmem_limit_bytes=16 * MIB),
        cost_estimate=pl.CostEstimate(flops=4 * C * D, bytes_accessed=4 * C * D, transcendentals=C),
    )(core, x, gain)


def row_kernel(place_ref, x_ref, hid_ref, gain_ref, cos_ref, sin_ref, *refs):
    pieces = refs[: 4 * len(RELATIVE)]
    mid_ref, next_ref, w_ref, o_ref, att_ref, sems = refs[4 * len(RELATIVE) :]
    core, my_x, my_y = place_ref[0], place_ref[1], place_ref[2]

    def block_of(part, stacked, ring):
        x, y = (stacked, ring) if part == 0 else (ring, stacked)
        x = lax.rem(my_x + x, 4)
        y = lax.rem(my_y + y, 4)
        return lax.rem(y, 2) * 8 + x * 2 + y // 2

    def copies(slot, part, outputs):
        first = (slot * 2 + part) * len(RELATIVE)
        for index, (ring, low, high) in enumerate(RELATIVE):
            src = pieces[first + index]
            if outputs:
                if high < PART:
                    continue
                lanes, target = pl.ds(QKV_PART - low, PART - QKV_PART), None
            else:
                end = min(high, QKV_PART)
                lanes, target = pl.ds(0, end - low), pl.ds(low, end - low)
            for k, stacked in enumerate(STACKED):
                block = block_of(part, stacked, ring)
                if outputs:
                    width = PART - QKV_PART
                    dst = o_ref.at[slot, block, :, :, pl.ds(part * width, width)]
                else:
                    dst = w_ref.at[slot, part, block, :, :, target]
                sem = sems.at[4 + slot if outputs else slot * 2 + part]
                pltpu.make_async_copy(src.at[k, :, :, lanes], dst, sem).start()

    for part in range(2):
        for slot in range(2):
            copies(slot, part, False)
    for part in range(2):
        for slot in range(2):
            copies(slot, part, True)

    def arrived(ref, sem):
        pltpu.make_async_copy(ref, ref, sem).wait()

    half = D // 2

    def step(g, _):
        part = g // 2
        for p in range(2):

            @pl.when(g == 2 * p)
            def _():
                for slot in range(2):
                    arrived(w_ref.at[slot, p], sems.at[slot * 2 + p])

        base = lax.rem(g, 2) * (3 * PAIR)

        def weight(slot, kind):
            lanes = pl.ds(pl.multiple_of(base + kind * PAIR, PAIR), PAIR)
            return w_ref[slot, part, :, :, :, lanes].reshape(half, PAIR)

        def projected(kind):
            return dot(hid_ref[:, :half], weight(0, kind)) + dot(hid_ref[:, half:], weight(1, kind))

        q2 = projected(0)
        k2 = projected(1)
        v2 = projected(2).astype(jnp.bfloat16)
        for h in range(2):
            lanes = slice(h * HEAD, (h + 1) * HEAD)
            q = rotate(q2[:, lanes], cos_ref[...], sin_ref[...]).astype(jnp.bfloat16)
            k = rotate(k2[:, lanes], cos_ref[...], sin_ref[...]).astype(jnp.bfloat16)
            v = v2[:, lanes]
            size = 256
            for b in range(C // size):
                end = (b + 1) * size
                scores = dot_t(q[b * size : end], k[:end])
                row = lax.broadcasted_iota(jnp.int32, scores.shape, 0) + b * size
                keep = lax.broadcasted_iota(jnp.int32, scores.shape, 1) <= row
                att_ref[g, b * size : end, lanes] = softmax_times(scores, keep, v[:end]).astype(jnp.bfloat16)
        return 0

    lax.fori_loop(0, STEPS, step, 0)
    for slot in range(2):
        arrived(o_ref.at[slot], sems.at[4 + slot])

    def finish(i, _):
        rows = pl.ds(pl.multiple_of(i * 128, 128), 128)
        halves = []
        squares = jnp.zeros((128, 1), jnp.float32)
        for h in range(2):
            lanes = slice(h * half, (h + 1) * half)
            total = x_ref[rows, lanes].astype(jnp.float32)
            for slot in range(2):
                for j in range(2):
                    block = (core if slot == 0 else 1 - core) + 2 * j
                    weight = o_ref[slot, j * 8 : (j + 1) * 8, h].reshape(PAIR, half)
                    total = total + dot(att_ref[block, rows, :], weight)
            middle = total.astype(jnp.bfloat16)
            mid_ref[rows, lanes] = middle
            middle = middle.astype(jnp.float32)
            squares = squares + jnp.sum(middle * middle, axis=-1, keepdims=True)
            halves.append(middle)
        inv = lax.rsqrt(squares / D + 1e-05)
        for h in range(2):
            lanes = slice(h * half, (h + 1) * half)
            next_ref[rows, lanes] = (halves[h] * inv * gain_ref[:, lanes]).astype(jnp.bfloat16)
        return 0

    lax.fori_loop(0, C // 128, finish, 0)


def row_layer(place, x, hidden, gain, tables, pieces):
    vmem = pl.BlockSpec(memory_space=pltpu.VMEM)
    shape = jax.ShapeDtypeStruct((C, D), jnp.bfloat16)
    return pl.pallas_call(
        row_kernel,
        out_shape=[shape, shape],
        in_specs=[pl.BlockSpec(memory_space=pltpu.SMEM)]
        + [vmem] * 5
        + [pl.BlockSpec(memory_space=pl.ANY)] * len(pieces),
        out_specs=[vmem, vmem],
        scratch_shapes=[
            pltpu.VMEM((2, 2, 16, 2, 32, QKV_PART), jnp.bfloat16),
            pltpu.VMEM((2, 16, 2, 32, D // 2), jnp.bfloat16),
            pltpu.VMEM((STEPS, C, PAIR), jnp.bfloat16),
            pltpu.SemaphoreType.DMA((6,)),
        ],
        compiler_params=pltpu.CompilerParams(vmem_limit_bytes=48 * MIB),
        cost_estimate=pl.CostEstimate(
            flops=2 * C * D * 4 * WIDTH + 4 * C * C * WIDTH,
            bytes_accessed=2 * (4 * C * D + 4 * D * WIDTH),
            transcendentals=C * C * HEADS,
        ),
    )(place, x, hidden, gain, *tables, *pieces)


def column_kernel(core_ref, x_ref, cos_ref, sin_ref, qo, ko, vo, qs, ks, vs, out_ref, hid_ref):
    core = core_ref[0]

    def selection(transposed):
        a = lax.broadcasted_iota(jnp.int32, (C, C), 1 if transposed else 0)
        b = lax.broadcasted_iota(jnp.int32, (C, C), 0 if transposed else 1)
        same = (a // N_SEQ == lax.rem(b, COLS)) & (lax.rem(a, N_SEQ) == b // COLS)
        return jnp.where(same, 1.0, 0.0).astype(jnp.bfloat16)

    @pl.when(pl.program_id(0) == 0)
    def _():
        pick = selection(False)
        width = D // 4
        for block in range(4):
            lanes = pl.ds(pl.multiple_of(slot_of(block, core) * width, width), width)
            moved = dot(pick, x_ref[:, block * width : (block + 1) * width])
            hid_ref[:, lanes] = moved.astype(jnp.bfloat16)

    q2 = project(hid_ref, qo, qs)
    k2 = project(hid_ref, ko, ks)
    v2 = project(hid_ref, vo, vs).astype(jnp.bfloat16)
    size = 128
    row = lax.broadcasted_iota(jnp.int32, (size, size), 0)
    col = lax.broadcasted_iota(jnp.int32, (size, size), 1)
    keep = (row // N_SEQ == col // N_SEQ) & (col <= row)
    heads = []
    for h in range(2):
        lanes = slice(h * HEAD, (h + 1) * HEAD)
        q = rotate(q2[:, lanes], cos_ref[...], sin_ref[...]).astype(jnp.bfloat16)
        k = rotate(k2[:, lanes], cos_ref[...], sin_ref[...]).astype(jnp.bfloat16)
        v = v2[:, lanes]
        blocks = []
        for b in range(C // size):
            rows = slice(b * size, (b + 1) * size)
            blocks.append(softmax_times(dot_t(q[rows], k[rows]), keep, v[rows]).astype(jnp.bfloat16))
        heads.append(jnp.concatenate(blocks, 0))
    attended = jnp.concatenate(heads, 1)
    out_ref[...] = dot(selection(True), attended).astype(jnp.bfloat16)


def attend(kernel, core, x, tables, own, other):
    half = own.shape[0]

    def weight(part):
        return pl.BlockSpec((half, PAIR), lambda i: (0, part * STEPS + i))

    whole = lambda shape: pl.BlockSpec(shape, lambda i: (0, 0), pipeline_mode=pl.Buffered(1))
    specs = [pl.BlockSpec(memory_space=pltpu.SMEM), whole((C, D))]
    args = [core, x]
    specs += [whole((C, HEAD)), whole((C, HEAD))] + [weight(p) for p in range(3)] * 2
    args += [*tables, own, own, own, other, other, other]
    return pl.pallas_call(
        kernel,
        grid=(STEPS,),
        out_shape=jax.ShapeDtypeStruct((C, WIDTH), jnp.bfloat16),
        in_specs=specs,
        out_specs=pl.BlockSpec((C, PAIR), lambda i: (0, i)),
        scratch_shapes=[pltpu.VMEM((C, D), jnp.bfloat16)],
        compiler_params=pltpu.CompilerParams(
            dimension_semantics=("arbitrary",), vmem_limit_bytes=40 * MIB
        ),
        cost_estimate=pl.CostEstimate(
            flops=2 * C * D * 3 * WIDTH + 4 * C * C * WIDTH,
            bytes_accessed=2 * (C * D + 3 * D * WIDTH + C * WIDTH),
            transcendentals=C * C * HEADS,
        ),
    )(*args)


def branch_sum(core, att_ref, own_ref, other_ref, resid_ref):
    width = WIDTH // 4
    total = resid_ref[...].astype(jnp.float32)
    for slot in range(4):
        block = jnp.where(slot < 2, core, 1 - core) + 2 * (slot % 2)
        lanes = pl.ds(pl.multiple_of(block * width, width), width)
        ref = own_ref if slot < 2 else other_ref
        rows = slice((slot % 2) * width, (slot % 2 + 1) * width)
        total = total + dot(att_ref[:, lanes], ref[rows, :])
    return total


def final_kernel(core_ref, att_ref, own_ref, other_ref, resid_ref, out_ref):
    out_ref[...] = branch_sum(core_ref[0], att_ref, own_ref, other_ref, resid_ref).astype(jnp.bfloat16)


def output_layer(core, attended, own, other, resid):
    size = 128
    block = lambda width: pl.BlockSpec((size, width), lambda i: (i, 0))
    whole = lambda shape: pl.BlockSpec(shape, lambda i: (0, 0), pipeline_mode=pl.Buffered(1))
    return pl.pallas_call(
        final_kernel,
        grid=(C // size,),
        out_shape=jax.ShapeDtypeStruct((C, D), jnp.bfloat16),
        in_specs=[
            pl.BlockSpec(memory_space=pltpu.SMEM),
            block(WIDTH),
            whole(own.shape),
            whole(other.shape),
            block(D),
        ],
        out_specs=block(D),
        compiler_params=pltpu.CompilerParams(
            dimension_semantics=("arbitrary",), vmem_limit_bytes=40 * MIB
        ),
        cost_estimate=pl.CostEstimate(
            flops=2 * C * D * WIDTH,
            bytes_accessed=2 * (2 * C * D + D * WIDTH + C * WIDTH),
            transcendentals=0,
        ),
    )(core, attended, own, other, resid)


def shift(value, axis, by):
    if axis == "y":
        where = lambda y: (y % 2) * 2 + y // 2
        return lax.ppermute(value, ("ylo", "yhi"), [(where(y), where((y + by) % 4)) for y in range(4)])
    return lax.ppermute(value, axis, [(i, (i + by) % 4) for i in range(4)])


def ring(value, axis):
    half = value.shape[-1] // 2
    left = shift(value, axis, 1)
    right = shift(value, axis, -1)
    return [value, left, right, shift(left[..., :half], axis, 1), shift(right[..., half:], axis, -1)]


def stack(pieces):
    own, left, right, low, high = pieces
    return jnp.stack([own, left, right, jnp.concatenate([low, high], -1)])


def swap(value):
    return lax.ppermute(value, "core", [(0, 1), (1, 0)])


def fold_output(output):
    return jnp.concatenate([output[:, : D // 2], output[:, D // 2 :]], 0)


def row_weights(inputs, output):
    by_step = inputs.reshape(-1, 3, STEPS, PAIR).transpose(0, 2, 1, 3).reshape(-1, 3 * WIDTH)
    shard = jnp.concatenate([by_step, fold_output(output)], 1)
    line = lax.all_gather(shard, "z", axis=0)
    qkv = line[:, :, : 3 * WIDTH].reshape(2, 32, 3 * WIDTH)
    out = line[:, :, 3 * WIDTH :].reshape(4, 2, 8, WIDTH).transpose(1, 0, 2, 3).reshape(2, 32, WIDTH)
    parts = []
    for p in range(2):
        lanes = slice(p * QKV_PART, (p + 1) * QKV_PART)
        rest = slice(p * WIDTH // 2, (p + 1) * WIDTH // 2)
        parts.append(jnp.concatenate([qkv[:, :, lanes], out[:, :, rest]], -1))
    stacks = [stack(ring(parts[0], "x")), stack(ring(parts[1], "y"))]
    stacks = lax.optimization_barrier(stacks)
    own = [ring(stacks[0], "y"), ring(stacks[1], "x")]
    return own, stacks


def column_weights(inputs, output):
    shard = jnp.concatenate([inputs, fold_output(output)], 1)
    line = lax.all_gather(shard, ("ylo", "yhi"), axis=0)
    plane = lax.all_gather(line, ("x", "z"), axis=0)
    plane = plane.reshape(4, 4, 2, 2, 16, 4 * WIDTH).transpose(2, 0, 3, 1, 4, 5)
    qkv = plane[..., : 3 * WIDTH].reshape(D // 2, 3 * WIDTH)
    out = plane[..., 3 * WIDTH :].reshape(64, 2, 8, WIDTH).transpose(0, 2, 1, 3).reshape(WIDTH // 2, D)
    return (qkv, swap(qkv)), (out, swap(out))


def shards(tokens, gain_first, inputs_first, output_first, gain_second, inputs_second, output_second, starts, band_edges):
    residual = tokens[0]
    core = lax.axis_index("core").astype(jnp.int32)
    core_scalar = core.reshape(1)
    seq = lax.axis_index(SEQ)
    my_y = lax.axis_index("yhi") * 2 + lax.axis_index("ylo")
    place = jnp.stack([core, lax.axis_index("x").astype(jnp.int32), my_y.astype(jnp.int32)])

    own, stacks = row_weights(inputs_first, output_first)
    inputs_second, output_second, stacks = lax.optimization_barrier((inputs_second, output_second, stacks))
    in_second, out_second = column_weights(inputs_second, output_second)
    pieces = [piece for part in own for piece in part]
    pieces = pieces + [swap(piece) for piece in pieces]

    frequency = frequencies(band_edges, HEAD // 2)
    block_starts = starts[0]
    own_start = lax.dynamic_index_in_dim(block_starts, seq, 0, keepdims=False)
    row_tables = rotary_tables(own_start + jnp.arange(C, dtype=jnp.int32), frequency)
    columns = seq.astype(jnp.int32) * COLS + jnp.arange(COLS, dtype=jnp.int32)
    column_positions = (columns[:, None] + block_starts[None, :]).reshape(C)
    column_tables = rotary_tables(column_positions, frequency)

    hidden = normed_slots(core_scalar, residual, gain_first.reshape(1, D))
    middle, hidden = row_layer(place, residual, hidden, gain_second.reshape(1, D), row_tables, pieces)
    hidden = lax.all_to_all(hidden, SEQ, split_axis=0, concat_axis=0, tiled=True)
    attended = attend(column_kernel, core_scalar, hidden, column_tables, *in_second)
    attended = lax.all_to_all(attended, SEQ, split_axis=0, concat_axis=0, tiled=True)
    return output_layer(core_scalar, attended, *out_second, middle)[None]


def solution(mesh):
    split = Mesh(mesh.devices.reshape(2, 2, 4, 2, 4), ("ylo", "core") + SEQ)
    dp = ("ylo", "core")
    every = dp + SEQ
    return jax.shard_map(
        shards,
        mesh=split,
        in_specs=(
            P(dp, SEQ, None),
            P(),
            P(every, None),
            P(every, None),
            P(),
            P(every, None),
            P(every, None),
            P(dp, None),
            P(),
        ),
        out_specs=P(dp, SEQ, None),
        check_vma=False,
    )
```

```python
import math

import jax
import jax.numpy as jnp
from jax import lax
from jax.experimental import pallas as pl
from jax.experimental.pallas import tpu as pltpu
from jax.sharding import Mesh, PartitionSpec as P

HEADS = 8
HEAD = 128
C = 512
SCALE = 8
D = 2048
WIDTH = HEADS * HEAD
N_SEQ = 32
COLS = C // N_SEQ
PAIR = 2 * HEAD
STEPS = WIDTH // PAIR
SEQ = ("x", "yhi", "z")
QKV_PART = 3 * WIDTH // 2
PART = 2 * WIDTH
RELATIVE = ((0, 0, PART), (3, 0, PART), (1, 0, PART), (2, 0, PART // 2), (2, PART // 2, PART))
STACKED = (0, 3, 1, 2)
LOG2E = 1.4426950408889634
MIB = 1 << 20


def frequencies(band_edges, half_size):
    dim_index = jnp.arange(half_size, dtype=jnp.float32)
    base_freq = jnp.power(10000.0, -dim_index / half_size)
    lower_edge = band_edges[0].astype(jnp.float32)
    upper_edge = band_edges[1].astype(jnp.float32)
    ramp_share = jnp.clip((dim_index - lower_edge) / (upper_edge - lower_edge), 0.0, 1.0)
    return base_freq * (1.0 - ramp_share) + base_freq * ramp_share / SCALE


def rotary_tables(positions, frequency):
    angles = positions.astype(jnp.float32)[:, None] * frequency
    mscale = 0.1 * math.log(SCALE) + 1.0
    cosine = jnp.cos(angles) * mscale
    sine = jnp.sin(angles) * mscale
    return jnp.concatenate([cosine, cosine], -1), jnp.concatenate([-sine, sine], -1)


def dot(a, b):
    return jnp.dot(a, b, preferred_element_type=jnp.float32)


def dot_t(a, b):
    return lax.dot_general(a, b, (((1,), (1,)), ((), ())), preferred_element_type=jnp.float32)


def slot_of(block, core):
    other = jnp.where(lax.rem(block, 2) == core, 0, 2)
    return other + block // 2


def rotate(heads, cos, sin):
    return heads * cos + pltpu.roll(heads, HEAD // 2, 1) * sin


def softmax_times(scores, keep, values):
    scores = jnp.where(keep, scores, -1e30)
    top = jnp.max(scores, axis=-1, keepdims=True)
    weights = jnp.exp2((scores - top) * (LOG2E / math.sqrt(HEAD)))
    total = jnp.sum(weights, axis=-1, keepdims=True)
    return dot(weights.astype(jnp.bfloat16), values) / total


def norm_kernel(core_ref, x_ref, gain_ref, hid_ref):
    core = core_ref[0]

    def chunk(i, _):
        rows = pl.ds(pl.multiple_of(i * 32, 32), 32)
        x = x_ref[rows, :].astype(jnp.float32)
        inv = lax.rsqrt(jnp.mean(x * x, axis=-1, keepdims=True) + 1e-05)
        hidden = (x * inv * gain_ref[...]).astype(jnp.bfloat16)
        width = D // 4
        for block in range(4):
            lanes = pl.ds(pl.multiple_of(slot_of(block, core) * width, width), width)
            hid_ref[rows, lanes] = hidden[:, block * width : (block + 1) * width]
        return 0

    lax.fori_loop(0, C // 32, chunk, 0)


def normed_slots(core, x, gain):
    vmem = pl.BlockSpec(memory_space=pltpu.VMEM)
    return pl.pallas_call(
        norm_kernel,
        out_shape=jax.ShapeDtypeStruct((C, D), jnp.bfloat16),
        in_specs=[pl.BlockSpec(memory_space=pltpu.SMEM), vmem, vmem],
        out_specs=vmem,
        compiler_params=pltpu.CompilerParams(vmem_limit_bytes=16 * MIB),
        cost_estimate=pl.CostEstimate(flops=4 * C * D, bytes_accessed=4 * C * D, transcendentals=C),
    )(core, x, gain)


def row_kernel(place_ref, x_ref, hid_ref, gain_ref, cos_ref, sin_ref, *refs):
    pieces = refs[: 4 * len(RELATIVE)]
    mid_ref, next_ref, w_ref, o_ref, att_ref, sems = refs[4 * len(RELATIVE) :]
    core, my_x, my_y = place_ref[0], place_ref[1], place_ref[2]

    def block_of(part, stacked, ring):
        x, y = (stacked, ring) if part == 0 else (ring, stacked)
        x = lax.rem(my_x + x, 4)
        y = lax.rem(my_y + y, 4)
        return lax.rem(y, 2) * 8 + x * 2 + y // 2

    def copies(slot, part, outputs):
        first = (slot * 2 + part) * len(RELATIVE)
        for index, (ring, low, high) in enumerate(RELATIVE):
            src = pieces[first + index]
            if outputs:
                if high < PART:
                    continue
                lanes, target = pl.ds(QKV_PART - low, PART - QKV_PART), None
            else:
                end = min(high, QKV_PART)
                lanes, target = pl.ds(0, end - low), pl.ds(low, end - low)
            for k, stacked in enumerate(STACKED):
                block = block_of(part, stacked, ring)
                if outputs:
                    width = PART - QKV_PART
                    dst = o_ref.at[slot, block, :, :, pl.ds(part * width, width)]
                else:
                    dst = w_ref.at[slot, part, block, :, :, target]
                sem = sems.at[4 + slot if outputs else slot * 2 + part]
                pltpu.make_async_copy(src.at[k, :, :, lanes], dst, sem).start()

    for part in range(2):
        for slot in range(2):
            copies(slot, part, False)
    for part in range(2):
        for slot in range(2):
            copies(slot, part, True)

    def arrived(ref, sem):
        pltpu.make_async_copy(ref, ref, sem).wait()

    half = D // 2

    def step(g, _):
        part = g // 2
        for p in range(2):

            @pl.when(g == 2 * p)
            def _():
                for slot in range(2):
                    arrived(w_ref.at[slot, p], sems.at[slot * 2 + p])

        base = lax.rem(g, 2) * (3 * PAIR)

        def weight(slot, kind):
            lanes = pl.ds(pl.multiple_of(base + kind * PAIR, PAIR), PAIR)
            return w_ref[slot, part, :, :, :, lanes].reshape(half, PAIR)

        def projected(kind):
            return dot(hid_ref[:, :half], weight(0, kind)) + dot(hid_ref[:, half:], weight(1, kind))

        q2 = projected(0)
        k2 = projected(1)
        v2 = projected(2).astype(jnp.bfloat16)
        for h in range(2):
            lanes = slice(h * HEAD, (h + 1) * HEAD)
            q = rotate(q2[:, lanes], cos_ref[...], sin_ref[...]).astype(jnp.bfloat16)
            k = rotate(k2[:, lanes], cos_ref[...], sin_ref[...]).astype(jnp.bfloat16)
            v = v2[:, lanes]
            size = 256
            for b in range(C // size):
                end = (b + 1) * size
                scores = dot_t(q[b * size : end], k[:end])
                row = lax.broadcasted_iota(jnp.int32, scores.shape, 0) + b * size
                keep = lax.broadcasted_iota(jnp.int32, scores.shape, 1) <= row
                att_ref[g, b * size : end, lanes] = softmax_times(scores, keep, v[:end]).astype(jnp.bfloat16)
        return 0

    lax.fori_loop(0, STEPS, step, 0)
    for slot in range(2):
        arrived(o_ref.at[slot], sems.at[4 + slot])

    def finish(i, _):
        rows = pl.ds(pl.multiple_of(i * 128, 128), 128)
        halves = []
        squares = jnp.zeros((128, 1), jnp.float32)
        for h in range(2):
            lanes = slice(h * half, (h + 1) * half)
            total = x_ref[rows, lanes].astype(jnp.float32)
            for slot in range(2):
                for j in range(2):
                    block = (core if slot == 0 else 1 - core) + 2 * j
                    weight = o_ref[slot, j * 8 : (j + 1) * 8, h].reshape(PAIR, half)
                    total = total + dot(att_ref[block, rows, :], weight)
            middle = total.astype(jnp.bfloat16)
            mid_ref[rows, lanes] = middle
            middle = middle.astype(jnp.float32)
            squares = squares + jnp.sum(middle * middle, axis=-1, keepdims=True)
            halves.append(middle)
        inv = lax.rsqrt(squares / D + 1e-05)
        for h in range(2):
            lanes = slice(h * half, (h + 1) * half)
            next_ref[rows, lanes] = (halves[h] * inv * gain_ref[:, lanes]).astype(jnp.bfloat16)
        return 0

    lax.fori_loop(0, C // 128, finish, 0)


def row_layer(place, x, hidden, gain, tables, pieces):
    vmem = pl.BlockSpec(memory_space=pltpu.VMEM)
    shape = jax.ShapeDtypeStruct((C, D), jnp.bfloat16)
    return pl.pallas_call(
        row_kernel,
        out_shape=[shape, shape],
        in_specs=[pl.BlockSpec(memory_space=pltpu.SMEM)]
        + [vmem] * 5
        + [pl.BlockSpec(memory_space=pl.ANY)] * len(pieces),
        out_specs=[vmem, vmem],
        scratch_shapes=[
            pltpu.VMEM((2, 2, 16, 2, 32, QKV_PART), jnp.bfloat16),
            pltpu.VMEM((2, 16, 2, 32, D // 2), jnp.bfloat16),
            pltpu.VMEM((STEPS, C, PAIR), jnp.bfloat16),
            pltpu.SemaphoreType.DMA((6,)),
        ],
        compiler_params=pltpu.CompilerParams(vmem_limit_bytes=48 * MIB),
        cost_estimate=pl.CostEstimate(
            flops=2 * C * D * 4 * WIDTH + 4 * C * C * WIDTH,
            bytes_accessed=2 * (4 * C * D + 4 * D * WIDTH),
            transcendentals=C * C * HEADS,
        ),
    )(place, x, hidden, gain, *tables, *pieces)


def column_kernel(core_ref, x_ref, cos_ref, sin_ref, own_plane, other_plane, out_ref, w_ref, hid_ref, sems):
    core = core_ref[0]
    half = D // 2
    triple = 3 * PAIR

    for g in range(STEPS):
        lanes = pl.ds(g * triple, triple)
        for slot, plane in enumerate((own_plane, other_plane)):
            for ylo in range(2):
                for yhi in range(2):
                    src = plane.at[:, :, ylo, yhi, :, lanes]
                    dst = w_ref.at[g, slot, ylo, :, yhi]
                    pltpu.make_async_copy(src, dst, sems.at[g]).start()

    def selection(transposed):
        a = lax.broadcasted_iota(jnp.int32, (C, C), 1 if transposed else 0)
        b = lax.broadcasted_iota(jnp.int32, (C, C), 0 if transposed else 1)
        same = (a // N_SEQ == lax.rem(b, COLS)) & (lax.rem(a, N_SEQ) == b // COLS)
        return jnp.where(same, 1.0, 0.0).astype(jnp.bfloat16)

    pick = selection(False)
    width = D // 4
    for block in range(4):
        lanes = pl.ds(pl.multiple_of(slot_of(block, core) * width, width), width)
        moved = dot(pick, x_ref[:, block * width : (block + 1) * width])
        hid_ref[:, lanes] = moved.astype(jnp.bfloat16)

    back = selection(True)
    size = 128
    row = lax.broadcasted_iota(jnp.int32, (size, size), 0)
    col = lax.broadcasted_iota(jnp.int32, (size, size), 1)
    keep = (row // N_SEQ == col // N_SEQ) & (col <= row)

    def step(g, _):
        pltpu.make_async_copy(w_ref.at[g], w_ref.at[g], sems.at[g]).wait()

        def weight(slot, kind):
            lanes = slice(kind * PAIR, (kind + 1) * PAIR)
            return w_ref[g, slot, :, :, :, :, :, lanes].reshape(half, PAIR)

        def projected(kind):
            return dot(hid_ref[:, :half], weight(0, kind)) + dot(hid_ref[:, half:], weight(1, kind))

        q2 = projected(0)
        k2 = projected(1)
        v2 = projected(2).astype(jnp.bfloat16)
        heads = []
        for h in range(2):
            lanes = slice(h * HEAD, (h + 1) * HEAD)
            q = rotate(q2[:, lanes], cos_ref[...], sin_ref[...]).astype(jnp.bfloat16)
            k = rotate(k2[:, lanes], cos_ref[...], sin_ref[...]).astype(jnp.bfloat16)
            v = v2[:, lanes]
            blocks = []
            for b in range(C // size):
                rows = slice(b * size, (b + 1) * size)
                blocks.append(softmax_times(dot_t(q[rows], k[rows]), keep, v[rows]).astype(jnp.bfloat16))
            heads.append(jnp.concatenate(blocks, 0))
        attended = jnp.concatenate(heads, 1)
        lanes = pl.ds(pl.multiple_of(g * PAIR, PAIR), PAIR)
        out_ref[:, lanes] = dot(back, attended).astype(jnp.bfloat16)
        return 0

    lax.fori_loop(0, STEPS, step, 0)


def column_layer(core, x, tables, planes):
    vmem = pl.BlockSpec(memory_space=pltpu.VMEM)
    return pl.pallas_call(
        column_kernel,
        out_shape=jax.ShapeDtypeStruct((C, WIDTH), jnp.bfloat16),
        in_specs=[pl.BlockSpec(memory_space=pltpu.SMEM)] + [vmem] * 3 + [pl.BlockSpec(memory_space=pl.ANY)] * 2,
        out_specs=vmem,
        scratch_shapes=[
            pltpu.VMEM((STEPS, 2, 2, 4, 2, 4, 16, 3 * PAIR), jnp.bfloat16),
            pltpu.VMEM((C, D), jnp.bfloat16),
            pltpu.SemaphoreType.DMA((STEPS,)),
        ],
        compiler_params=pltpu.CompilerParams(vmem_limit_bytes=40 * MIB),
        cost_estimate=pl.CostEstimate(
            flops=2 * C * D * 3 * WIDTH + 4 * C * C * WIDTH,
            bytes_accessed=2 * (C * D + 3 * D * WIDTH + C * WIDTH),
            transcendentals=C * C * HEADS,
        ),
    )(core, x, *tables, *planes)


def branch_sum(core, att_ref, own_ref, other_ref, resid_ref):
    width = WIDTH // 4
    total = resid_ref[...].astype(jnp.float32)
    for slot in range(4):
        block = jnp.where(slot < 2, core, 1 - core) + 2 * (slot % 2)
        lanes = pl.ds(pl.multiple_of(block * width, width), width)
        ref = own_ref if slot < 2 else other_ref
        rows = slice((slot % 2) * width, (slot % 2 + 1) * width)
        total = total + dot(att_ref[:, lanes], ref[rows, :])
    return total


def final_kernel(core_ref, att_ref, own_ref, other_ref, resid_ref, out_ref):
    out_ref[...] = branch_sum(core_ref[0], att_ref, own_ref, other_ref, resid_ref).astype(jnp.bfloat16)


def output_layer(core, attended, own, other, resid):
    size = 128
    block = lambda width: pl.BlockSpec((size, width), lambda i: (i, 0))
    whole = lambda shape: pl.BlockSpec(shape, lambda i: (0, 0), pipeline_mode=pl.Buffered(1))
    return pl.pallas_call(
        final_kernel,
        grid=(C // size,),
        out_shape=jax.ShapeDtypeStruct((C, D), jnp.bfloat16),
        in_specs=[
            pl.BlockSpec(memory_space=pltpu.SMEM),
            block(WIDTH),
            whole(own.shape),
            whole(other.shape),
            block(D),
        ],
        out_specs=block(D),
        compiler_params=pltpu.CompilerParams(
            dimension_semantics=("arbitrary",), vmem_limit_bytes=40 * MIB
        ),
        cost_estimate=pl.CostEstimate(
            flops=2 * C * D * WIDTH,
            bytes_accessed=2 * (2 * C * D + D * WIDTH + C * WIDTH),
            transcendentals=0,
        ),
    )(core, attended, own, other, resid)


def shift(value, axis, by):
    if axis == "y":
        where = lambda y: (y % 2) * 2 + y // 2
        return lax.ppermute(value, ("ylo", "yhi"), [(where(y), where((y + by) % 4)) for y in range(4)])
    return lax.ppermute(value, axis, [(i, (i + by) % 4) for i in range(4)])


def ring(value, axis):
    half = value.shape[-1] // 2
    left = shift(value, axis, 1)
    right = shift(value, axis, -1)
    return [value, left, right, shift(left[..., :half], axis, 1), shift(right[..., half:], axis, -1)]


def stack(pieces):
    own, left, right, low, high = pieces
    return jnp.stack([own, left, right, jnp.concatenate([low, high], -1)])


def swap(value):
    return lax.ppermute(value, "core", [(0, 1), (1, 0)])


def fold_output(output):
    return jnp.concatenate([output[:, : D // 2], output[:, D // 2 :]], 0)


def by_step(inputs):
    return inputs.reshape(-1, 3, STEPS, PAIR).transpose(0, 2, 1, 3).reshape(-1, 3 * WIDTH)


def row_weights(inputs, output, line):
    shard = jnp.concatenate([by_step(inputs), fold_output(output)], 1)
    rows = lax.all_gather(shard, "z", axis=0)
    qkv = rows[:, :, : 3 * WIDTH].reshape(2, 32, 3 * WIDTH)
    out = rows[:, :, 3 * WIDTH :].reshape(4, 2, 8, WIDTH).transpose(1, 0, 2, 3).reshape(2, 32, WIDTH)
    parts = []
    for p in range(2):
        lanes = slice(p * QKV_PART, (p + 1) * QKV_PART)
        rest = slice(p * WIDTH // 2, (p + 1) * WIDTH // 2)
        parts.append(jnp.concatenate([qkv[:, :, lanes], out[:, :, rest]], -1))
    stacks = [stack(ring(parts[0], "x")), stack(ring(parts[1], "y"))]
    stacks, line = lax.optimization_barrier((stacks, line))
    own = [ring(stacks[0], "y"), ring(stacks[1], "x")]
    return own, line


def column_line(inputs, output):
    shard = jnp.concatenate([by_step(inputs), fold_output(output)], 1)
    return lax.all_gather(jnp.concatenate([shard, shard], 1), ("ylo", "yhi"), axis=0)


def column_plane(line):
    return lax.all_gather(line[:, :, : 4 * WIDTH], ("x", "z"), axis=0).reshape(4, 4, 2, 2, 16, 4 * WIDTH)


def column_output(plane):
    out = plane[..., 3 * WIDTH :].transpose(2, 0, 3, 1, 4, 5)
    return out.reshape(64, 2, 8, WIDTH).transpose(0, 2, 1, 3).reshape(WIDTH // 2, D)


def shards(tokens, gain_first, inputs_first, output_first, gain_second, inputs_second, output_second, starts, band_edges):
    residual = tokens[0]
    core = lax.axis_index("core").astype(jnp.int32)
    core_scalar = core.reshape(1)
    seq = lax.axis_index(SEQ)
    my_y = lax.axis_index("yhi") * 2 + lax.axis_index("ylo")
    place = jnp.stack([core, lax.axis_index("x").astype(jnp.int32), my_y.astype(jnp.int32)])

    line = column_line(inputs_second, output_second)
    own, line = row_weights(inputs_first, output_first, line)
    plane = column_plane(line)
    pieces = [piece for part in own for piece in part]
    pieces = pieces + [swap(piece) for piece in pieces]

    frequency = frequencies(band_edges, HEAD // 2)
    block_starts = starts[0]
    own_start = lax.dynamic_index_in_dim(block_starts, seq, 0, keepdims=False)
    row_tables = rotary_tables(own_start + jnp.arange(C, dtype=jnp.int32), frequency)
    columns = seq.astype(jnp.int32) * COLS + jnp.arange(COLS, dtype=jnp.int32)
    column_positions = (columns[:, None] + block_starts[None, :]).reshape(C)
    column_tables = rotary_tables(column_positions, frequency)

    hidden = normed_slots(core_scalar, residual, gain_first.reshape(1, D))
    middle, hidden = row_layer(place, residual, hidden, gain_second.reshape(1, D), row_tables, pieces)
    plane, hidden = lax.optimization_barrier((plane, hidden))
    planes = (plane, swap(plane))
    hidden = lax.all_to_all(hidden, SEQ, split_axis=0, concat_axis=0, tiled=True)
    attended = column_layer(core_scalar, hidden, column_tables, planes)
    attended = lax.all_to_all(attended, SEQ, split_axis=0, concat_axis=0, tiled=True)
    return output_layer(core_scalar, attended, *[column_output(p) for p in planes], middle)[None]


def solution(mesh):
    split = Mesh(mesh.devices.reshape(2, 2, 4, 2, 4), ("ylo", "core") + SEQ)
    dp = ("ylo", "core")
    every = dp + SEQ
    return jax.shard_map(
        shards,
        mesh=split,
        in_specs=(
            P(dp, SEQ, None),
            P(),
            P(every, None),
            P(every, None),
            P(),
            P(every, None),
            P(every, None),
            P(dp, None),
            P(),
        ),
        out_specs=P(dp, SEQ, None),
        check_vma=False,
    )
```

```python
import math

import jax
import jax.numpy as jnp
from jax import lax
from jax.experimental import pallas as pl
from jax.experimental.pallas import tpu as pltpu
from jax.sharding import Mesh, PartitionSpec as P

HEADS = 8
HEAD = 128
C = 512
SCALE = 8
D = 2048
WIDTH = HEADS * HEAD
N_SEQ = 32
COLS = C // N_SEQ
PAIR = 2 * HEAD
STEPS = WIDTH // PAIR
SEQ = ("x", "yhi", "z")
QKV_PART = 3 * WIDTH // 2
PART = 2 * WIDTH
RELATIVE = ((0, 0, PART), (3, 0, PART), (1, 0, PART), (2, 0, PART // 2), (2, PART // 2, PART))
STACKED = (0, 3, 1, 2)
LOG2E = 1.4426950408889634
MIB = 1 << 20


def frequencies(band_edges, half_size):
    dim_index = jnp.arange(half_size, dtype=jnp.float32)
    base_freq = jnp.power(10000.0, -dim_index / half_size)
    lower_edge = band_edges[0].astype(jnp.float32)
    upper_edge = band_edges[1].astype(jnp.float32)
    ramp_share = jnp.clip((dim_index - lower_edge) / (upper_edge - lower_edge), 0.0, 1.0)
    return base_freq * (1.0 - ramp_share) + base_freq * ramp_share / SCALE


def rotary_tables(positions, frequency):
    angles = positions.astype(jnp.float32)[:, None] * frequency
    mscale = 0.1 * math.log(SCALE) + 1.0
    cosine = jnp.cos(angles) * mscale
    sine = jnp.sin(angles) * mscale
    return jnp.concatenate([cosine, cosine], -1), jnp.concatenate([-sine, sine], -1)


def dot(a, b):
    return jnp.dot(a, b, preferred_element_type=jnp.float32)


def dot_t(a, b):
    return lax.dot_general(a, b, (((1,), (1,)), ((), ())), preferred_element_type=jnp.float32)


def slot_of(block, core):
    other = jnp.where(lax.rem(block, 2) == core, 0, 2)
    return other + block // 2


def rotate(heads, cos, sin):
    return heads * cos + pltpu.roll(heads, HEAD // 2, 1) * sin


def softmax_times(scores, keep, values):
    scores = jnp.where(keep, scores, -1e30)
    top = jnp.max(scores, axis=-1, keepdims=True)
    weights = jnp.exp2((scores - top) * (LOG2E / math.sqrt(HEAD)))
    total = jnp.sum(weights, axis=-1, keepdims=True)
    return dot(weights.astype(jnp.bfloat16), values) / total


def norm_kernel(core_ref, x_ref, gain_ref, hid_ref):
    core = core_ref[0]

    def chunk(i, _):
        rows = pl.ds(pl.multiple_of(i * 32, 32), 32)
        x = x_ref[rows, :].astype(jnp.float32)
        inv = lax.rsqrt(jnp.mean(x * x, axis=-1, keepdims=True) + 1e-05)
        hidden = (x * inv * gain_ref[...]).astype(jnp.bfloat16)
        width = D // 4
        for block in range(4):
            lanes = pl.ds(pl.multiple_of(slot_of(block, core) * width, width), width)
            hid_ref[rows, lanes] = hidden[:, block * width : (block + 1) * width]
        return 0

    lax.fori_loop(0, C // 32, chunk, 0)


def normed_slots(core, x, gain):
    vmem = pl.BlockSpec(memory_space=pltpu.VMEM)
    hbm = pl.BlockSpec(memory_space=pltpu.HBM)
    return pl.pallas_call(
        norm_kernel,
        out_shape=jax.ShapeDtypeStruct((C, D), jnp.bfloat16),
        in_specs=[pl.BlockSpec(memory_space=pltpu.SMEM), vmem, vmem],
        out_specs=vmem,
        compiler_params=pltpu.CompilerParams(vmem_limit_bytes=16 * MIB),
        cost_estimate=pl.CostEstimate(flops=4 * C * D, bytes_accessed=4 * C * D, transcendentals=C),
    )(core, x, gain)


def start_copies(place_ref, pieces, sems, w_ref=None, o_ref=None):
    my_x, my_y = place_ref[1], place_ref[2]

    def block_of(part, stacked, ring):
        x, y = (stacked, ring) if part == 0 else (ring, stacked)
        x = lax.rem(my_x + x, 4)
        y = lax.rem(my_y + y, 4)
        return lax.rem(y, 2) * 8 + x * 2 + y // 2

    def move(slot, part, outputs):
        first = (slot * 2 + part) * len(RELATIVE)
        for index, (ring, low, high) in enumerate(RELATIVE):
            src = pieces[first + index]
            if outputs:
                if high < PART:
                    continue
                lanes, target = pl.ds(QKV_PART - low, PART - QKV_PART), None
            else:
                end = min(high, QKV_PART)
                lanes, target = pl.ds(0, end - low), pl.ds(low, end - low)
            for k, stacked in enumerate(STACKED):
                block = block_of(part, stacked, ring)
                if outputs:
                    width = PART - QKV_PART
                    dst = o_ref.at[slot, block, :, :, pl.ds(part * width, width)]
                else:
                    dst = w_ref.at[slot, part, block, :, :, target]
                sem = sems.at[4 + slot if outputs else slot * 2 + part]
                pltpu.make_async_copy(src.at[k, :, :, lanes], dst, sem).start()

    for outputs, ref in ((False, w_ref), (True, o_ref)):
        if ref is not None:
            for part in range(2):
                for slot in range(2):
                    move(slot, part, outputs)


def arrived(ref, sem):
    pltpu.make_async_copy(ref, ref, sem).wait()


def step_weights(w_ref, sems, g):
    part = g // 2
    for p in range(2):

        @pl.when(g == 2 * p)
        def _():
            for slot in range(2):
                arrived(w_ref.at[slot, p], sems.at[slot * 2 + p])

    base = lax.rem(g, 2) * (3 * PAIR)

    def weight(slot, kind):
        lanes = pl.ds(pl.multiple_of(base + kind * PAIR, PAIR), PAIR)
        return w_ref[slot, part, :, :, :, lanes].reshape(D // 2, PAIR)

    return weight


def output_sum(core, att_ref, rows, o_ref, h, total):
    for slot in range(2):
        for j in range(2):
            block = (core if slot == 0 else 1 - core) + 2 * j
            lanes = pl.ds(pl.multiple_of(block * PAIR, PAIR), PAIR)
            weight = o_ref[slot, j * 8 : (j + 1) * 8, h].reshape(PAIR, D // 2)
            total = total + dot(att_ref[rows, lanes], weight)
    return total


def row_kernel(place_ref, x_ref, hid_ref, gain_ref, cos_ref, sin_ref, *refs):
    pieces = refs[: 4 * len(RELATIVE)]
    mid_ref, next_ref, w_ref, o_ref, att_ref, sems = refs[4 * len(RELATIVE) :]
    core = place_ref[0]
    start_copies(place_ref, pieces, sems, w_ref, o_ref)
    half = D // 2

    def step(g, _):
        weight = step_weights(w_ref, sems, g)

        def projected(kind):
            return dot(hid_ref[:, :half], weight(0, kind)) + dot(hid_ref[:, half:], weight(1, kind))

        q2 = projected(0)
        k2 = projected(1)
        v2 = projected(2).astype(jnp.bfloat16)
        for h in range(2):
            lanes = slice(h * HEAD, (h + 1) * HEAD)
            q = rotate(q2[:, lanes], cos_ref[...], sin_ref[...]).astype(jnp.bfloat16)
            k = rotate(k2[:, lanes], cos_ref[...], sin_ref[...]).astype(jnp.bfloat16)
            v = v2[:, lanes]
            size = 256
            for b in range(C // size):
                end = (b + 1) * size
                scores = dot_t(q[b * size : end], k[:end])
                row = lax.broadcasted_iota(jnp.int32, scores.shape, 0) + b * size
                keep = lax.broadcasted_iota(jnp.int32, scores.shape, 1) <= row
                target = pl.ds(pl.multiple_of(g * PAIR + h * HEAD, HEAD), HEAD)
                att_ref[b * size : end, target] = softmax_times(scores, keep, v[:end]).astype(jnp.bfloat16)
        return 0

    lax.fori_loop(0, STEPS, step, 0)
    for slot in range(2):
        arrived(o_ref.at[slot], sems.at[4 + slot])

    def finish(i, _):
        rows = pl.ds(pl.multiple_of(i * 128, 128), 128)
        halves = []
        squares = jnp.zeros((128, 1), jnp.float32)
        for h in range(2):
            lanes = slice(h * half, (h + 1) * half)
            total = output_sum(core, att_ref, rows, o_ref, h, x_ref[rows, lanes].astype(jnp.float32))
            middle = total.astype(jnp.bfloat16)
            mid_ref[rows, lanes] = middle
            middle = middle.astype(jnp.float32)
            squares = squares + jnp.sum(middle * middle, axis=-1, keepdims=True)
            halves.append(middle)
        inv = lax.rsqrt(squares / D + 1e-05)
        for h in range(2):
            lanes = slice(h * half, (h + 1) * half)
            next_ref[rows, lanes] = (halves[h] * inv * gain_ref[:, lanes]).astype(jnp.bfloat16)
        return 0

    lax.fori_loop(0, C // 128, finish, 0)


def row_layer(place, x, hidden, gain, tables, pieces):
    vmem = pl.BlockSpec(memory_space=pltpu.VMEM)
    hbm = pl.BlockSpec(memory_space=pltpu.HBM)
    shape = jax.ShapeDtypeStruct((C, D), jnp.bfloat16)
    return pl.pallas_call(
        row_kernel,
        out_shape=[shape, shape],
        in_specs=[pl.BlockSpec(memory_space=pltpu.SMEM)]
        + [vmem] * 5
        + [hbm] * len(pieces),
        out_specs=[vmem, vmem],
        scratch_shapes=[
            pltpu.VMEM((2, 2, 16, 2, 32, QKV_PART), jnp.bfloat16),
            pltpu.VMEM((2, 16, 2, 32, D // 2), jnp.bfloat16),
            pltpu.VMEM((C, WIDTH), jnp.bfloat16),
            pltpu.SemaphoreType.DMA((6,)),
        ],
        compiler_params=pltpu.CompilerParams(vmem_limit_bytes=48 * MIB),
        cost_estimate=pl.CostEstimate(
            flops=2 * C * D * 4 * WIDTH + 4 * C * C * WIDTH,
            bytes_accessed=2 * (4 * C * D + 4 * D * WIDTH),
            transcendentals=C * C * HEADS,
        ),
    )(place, x, hidden, gain, *tables, *pieces)


def column_kernel(place_ref, x_ref, cos_ref, sin_ref, *refs):
    pieces = refs[: 4 * len(RELATIVE)]
    out_ref, w_ref, hid_ref, sems = refs[4 * len(RELATIVE) :]
    core = place_ref[0]
    half = D // 2
    start_copies(place_ref, pieces, sems, w_ref)

    def selection(transposed):
        a = lax.broadcasted_iota(jnp.int32, (C, C), 1 if transposed else 0)
        b = lax.broadcasted_iota(jnp.int32, (C, C), 0 if transposed else 1)
        same = (a // N_SEQ == lax.rem(b, COLS)) & (lax.rem(a, N_SEQ) == b // COLS)
        return jnp.where(same, 1.0, 0.0).astype(jnp.bfloat16)

    pick = selection(False)
    width = D // 4
    for block in range(4):
        lanes = pl.ds(pl.multiple_of(slot_of(block, core) * width, width), width)
        moved = dot(pick, x_ref[:, block * width : (block + 1) * width])
        hid_ref[:, lanes] = moved.astype(jnp.bfloat16)

    back = selection(True)
    size = 128
    row = lax.broadcasted_iota(jnp.int32, (size, size), 0)
    col = lax.broadcasted_iota(jnp.int32, (size, size), 1)
    keep = (row // N_SEQ == col // N_SEQ) & (col <= row)

    def step(g, _):
        weight = step_weights(w_ref, sems, g)

        def projected(kind):
            return dot(hid_ref[:, :half], weight(0, kind)) + dot(hid_ref[:, half:], weight(1, kind))

        q2 = projected(0)
        k2 = projected(1)
        v2 = projected(2).astype(jnp.bfloat16)
        heads = []
        for h in range(2):
            lanes = slice(h * HEAD, (h + 1) * HEAD)
            q = rotate(q2[:, lanes], cos_ref[...], sin_ref[...]).astype(jnp.bfloat16)
            k = rotate(k2[:, lanes], cos_ref[...], sin_ref[...]).astype(jnp.bfloat16)
            v = v2[:, lanes]
            blocks = []
            for b in range(C // size):
                rows = slice(b * size, (b + 1) * size)
                blocks.append(softmax_times(dot_t(q[rows], k[rows]), keep, v[rows]).astype(jnp.bfloat16))
            heads.append(jnp.concatenate(blocks, 0))
        attended = jnp.concatenate(heads, 1)
        lanes = pl.ds(pl.multiple_of(g * PAIR, PAIR), PAIR)
        out_ref[:, lanes] = dot(back, attended).astype(jnp.bfloat16)
        return 0

    lax.fori_loop(0, STEPS, step, 0)


def column_layer(place, x, tables, pieces):
    vmem = pl.BlockSpec(memory_space=pltpu.VMEM)
    hbm = pl.BlockSpec(memory_space=pltpu.HBM)
    return pl.pallas_call(
        column_kernel,
        out_shape=jax.ShapeDtypeStruct((C, WIDTH), jnp.bfloat16),
        in_specs=[pl.BlockSpec(memory_space=pltpu.SMEM)] + [vmem] * 3 + [hbm] * len(pieces),
        out_specs=vmem,
        scratch_shapes=[
            pltpu.VMEM((2, 2, 16, 2, 32, QKV_PART), jnp.bfloat16),
            pltpu.VMEM((C, D), jnp.bfloat16),
            pltpu.SemaphoreType.DMA((4,)),
        ],
        compiler_params=pltpu.CompilerParams(vmem_limit_bytes=40 * MIB),
        cost_estimate=pl.CostEstimate(
            flops=2 * C * D * 3 * WIDTH + 4 * C * C * WIDTH,
            bytes_accessed=2 * (C * D + 3 * D * WIDTH + C * WIDTH),
            transcendentals=C * C * HEADS,
        ),
    )(place, x, *tables, *pieces)


def final_kernel(place_ref, att_ref, x_ref, *refs):
    pieces = refs[: 4 * len(RELATIVE)]
    out_ref, o_ref, sems = refs[4 * len(RELATIVE) :]
    core = place_ref[0]
    half = D // 2

    @pl.when(pl.program_id(0) == 0)
    def _():
        start_copies(place_ref, pieces, sems, o_ref=o_ref)
        for slot in range(2):
            arrived(o_ref.at[slot], sems.at[4 + slot])

    for h in range(2):
        lanes = slice(h * half, (h + 1) * half)
        total = x_ref[:, lanes].astype(jnp.float32)
        out_ref[:, lanes] = output_sum(core, att_ref, slice(None), o_ref, h, total).astype(jnp.bfloat16)


def final_layer(place, attended, x, pieces):
    size = 128
    block = lambda width: pl.BlockSpec((size, width), lambda i: (i, 0))
    hbm = pl.BlockSpec(memory_space=pltpu.HBM)
    return pl.pallas_call(
        final_kernel,
        grid=(C // size,),
        out_shape=jax.ShapeDtypeStruct((C, D), jnp.bfloat16),
        in_specs=[pl.BlockSpec(memory_space=pltpu.SMEM), block(WIDTH), block(D)] + [hbm] * len(pieces),
        out_specs=block(D),
        scratch_shapes=[
            pltpu.VMEM((2, 16, 2, 32, D // 2), jnp.bfloat16),
            pltpu.SemaphoreType.DMA((6,)),
        ],
        compiler_params=pltpu.CompilerParams(
            dimension_semantics=("arbitrary",), vmem_limit_bytes=24 * MIB
        ),
        cost_estimate=pl.CostEstimate(
            flops=2 * C * D * WIDTH,
            bytes_accessed=2 * (2 * C * D + D * WIDTH + C * WIDTH),
            transcendentals=0,
        ),
    )(place, attended, x, *pieces)


def shift(value, axis, by):
    if axis == "y":
        where = lambda y: (y % 2) * 2 + y // 2
        return lax.ppermute(value, ("ylo", "yhi"), [(where(y), where((y + by) % 4)) for y in range(4)])
    return lax.ppermute(value, axis, [(i, (i + by) % 4) for i in range(4)])


def first_hops(value, axis):
    return [value, shift(value, axis, 1), shift(value, axis, -1)]


def forwards(hops, axis):
    own, left, right = hops
    half = own.shape[-1] // 2
    return hops + [shift(left[..., :half], axis, 1), shift(right[..., half:], axis, -1)]


def stack(pieces):
    own, left, right, low, high = pieces
    return jnp.stack([own, left, right, jnp.concatenate([low, high], -1)])


def swap(value):
    return lax.ppermute(value, "core", [(0, 1), (1, 0)])


def fold_output(output):
    return jnp.concatenate([output[:, : D // 2], output[:, D // 2 :]], 0)


def by_step(inputs):
    return inputs.reshape(-1, 3, STEPS, PAIR).transpose(0, 2, 1, 3).reshape(-1, 3 * WIDTH)


def lines(inputs, output):
    shard = jnp.concatenate([by_step(inputs), fold_output(output)], 1)
    rows = lax.all_gather(shard, "z", axis=0)
    qkv = rows[:, :, : 3 * WIDTH].reshape(2, 32, 3 * WIDTH)
    out = rows[:, :, 3 * WIDTH :].reshape(4, 2, 8, WIDTH).transpose(1, 0, 2, 3).reshape(2, 32, WIDTH)
    parts = []
    for p in range(2):
        lanes = slice(p * QKV_PART, (p + 1) * QKV_PART)
        rest = slice(p * WIDTH // 2, (p + 1) * WIDTH // 2)
        parts.append(jnp.concatenate([qkv[:, :, lanes], out[:, :, rest]], -1))
    return parts


def inner_rings(parts):
    hops = [first_hops(part, axis) for part, axis in zip(parts, "xy")]
    return [stack(forwards(hop, axis)) for hop, axis in zip(hops, "xy")]


def outer_hops(stacks):
    return [first_hops(part, axis) for part, axis in zip(stacks, "yx")]


def outer_forwards(hops):
    return [forwards(hop, axis) for hop, axis in zip(hops, "yx")]


def both_cores(parts, swapped):
    own = [piece for part in parts for piece in part]
    other = [swapped[index] if index in swapped else swap(piece) for index, piece in enumerate(own)]
    return own + other


def shards(tokens, gain_first, inputs_first, output_first, gain_second, inputs_second, output_second, starts, band_edges):
    residual = tokens[0]
    core = lax.axis_index("core").astype(jnp.int32)
    core_scalar = core.reshape(1)
    seq = lax.axis_index(SEQ)
    my_y = lax.axis_index("yhi") * 2 + lax.axis_index("ylo")
    place = jnp.stack([core, lax.axis_index("x").astype(jnp.int32), my_y.astype(jnp.int32)])

    frequency = frequencies(band_edges, HEAD // 2)
    block_starts = starts[0]
    own_start = lax.dynamic_index_in_dim(block_starts, seq, 0, keepdims=False)
    row_tables = rotary_tables(own_start + jnp.arange(C, dtype=jnp.int32), frequency)
    columns = seq.astype(jnp.int32) * COLS + jnp.arange(COLS, dtype=jnp.int32)
    column_positions = (columns[:, None] + block_starts[None, :]).reshape(C)
    column_tables = rotary_tables(column_positions, frequency)

    hidden = normed_slots(core_scalar, residual, gain_first.reshape(1, D))

    first = inner_rings(lines(inputs_first, output_first))
    first, hidden, row_tables, column_tables = lax.optimization_barrier((first, hidden, row_tables, column_tables))
    first_hop = outer_hops(first)
    swapped = {0: swap(first[0]), 5: swap(first[1])}
    inputs_second, output_second, swapped = lax.optimization_barrier((inputs_second, output_second, swapped))
    second = lines(inputs_second, output_second)
    pieces = both_cores(outer_forwards(first_hop), swapped)
    second = inner_rings(second)
    second, place = lax.optimization_barrier((second, place))
    second_hop = outer_hops(second)

    middle, hidden = row_layer(place, residual, hidden, gain_second.reshape(1, D), row_tables, pieces)
    second_hop, hidden = lax.optimization_barrier((second_hop, hidden))
    pieces = both_cores(outer_forwards(second_hop), {})
    hidden = lax.all_to_all(hidden, SEQ, split_axis=0, concat_axis=0, tiled=True)
    attended = column_layer(place, hidden, column_tables, pieces)
    attended = lax.all_to_all(attended, SEQ, split_axis=0, concat_axis=0, tiled=True)
    return final_layer(place, attended, middle, pieces)[None]


def solution(mesh):
    split = Mesh(mesh.devices.reshape(2, 2, 4, 2, 4), ("ylo", "core") + SEQ)
    dp = ("ylo", "core")
    every = dp + SEQ
    return jax.shard_map(
        shards,
        mesh=split,
        in_specs=(
            P(dp, SEQ, None),
            P(),
            P(every, None),
            P(every, None),
            P(),
            P(every, None),
            P(every, None),
            P(dp, None),
            P(),
        ),
        out_specs=P(dp, SEQ, None),
        check_vma=False,
    )
```

```python
import math

import jax
import jax.numpy as jnp
from jax import lax
from jax.experimental import pallas as pl
from jax.experimental.pallas import tpu as pltpu
from jax.sharding import Mesh, PartitionSpec as P

HEADS = 8
HEAD = 128
C = 512
SCALE = 8
D = 2048
WIDTH = HEADS * HEAD
N_SEQ = 32
COLS = C // N_SEQ
PAIR = 2 * HEAD
STEPS = WIDTH // PAIR
SEQ = ("x", "yhi", "z")
QKV_PART = 3 * WIDTH // 2
PART = 2 * WIDTH
RELATIVE = ((0, 0, PART), (3, 0, PART), (1, 0, PART), (2, 0, PART // 2), (2, PART // 2, PART))
STACKED = (0, 3, 1, 2)
LOG2E = 1.4426950408889634
MIB = 1 << 20


def frequencies(band_edges, half_size):
    dim_index = jnp.arange(half_size, dtype=jnp.float32)
    base_freq = jnp.power(10000.0, -dim_index / half_size)
    lower_edge = band_edges[0].astype(jnp.float32)
    upper_edge = band_edges[1].astype(jnp.float32)
    ramp_share = jnp.clip((dim_index - lower_edge) / (upper_edge - lower_edge), 0.0, 1.0)
    return base_freq * (1.0 - ramp_share) + base_freq * ramp_share / SCALE


def rotary_tables(positions, frequency):
    angles = positions.astype(jnp.float32)[:, None] * frequency
    mscale = 0.1 * math.log(SCALE) + 1.0
    cosine = jnp.cos(angles) * mscale
    sine = jnp.sin(angles) * mscale
    return jnp.concatenate([cosine, cosine], -1), jnp.concatenate([-sine, sine], -1)


def dot(a, b):
    return jnp.dot(a, b, preferred_element_type=jnp.float32)


def dot_t(a, b):
    return lax.dot_general(a, b, (((1,), (1,)), ((), ())), preferred_element_type=jnp.float32)


def slot_of(block, core):
    other = jnp.where(lax.rem(block, 2) == core, 0, 2)
    return other + block // 2


def rotate(heads, cos, sin):
    return heads * cos + pltpu.roll(heads, HEAD // 2, 1) * sin


def softmax_times(scores, keep, values):
    scores = jnp.where(keep, scores, -1e30)
    top = jnp.max(scores, axis=-1, keepdims=True)
    weights = jnp.exp2((scores - top) * (LOG2E / math.sqrt(HEAD)))
    total = jnp.sum(weights, axis=-1, keepdims=True)
    return dot(weights.astype(jnp.bfloat16), values) / total


def norm_kernel(core_ref, x_ref, gain_ref, hid_ref):
    core = core_ref[0]

    def chunk(i, _):
        rows = pl.ds(pl.multiple_of(i * 32, 32), 32)
        x = x_ref[rows, :].astype(jnp.float32)
        inv = lax.rsqrt(jnp.mean(x * x, axis=-1, keepdims=True) + 1e-05)
        hidden = (x * inv * gain_ref[...]).astype(jnp.bfloat16)
        width = D // 4
        for block in range(4):
            lanes = pl.ds(pl.multiple_of(slot_of(block, core) * width, width), width)
            hid_ref[rows, lanes] = hidden[:, block * width : (block + 1) * width]
        return 0

    lax.fori_loop(0, C // 32, chunk, 0)


def normed_slots(core, x, gain):
    vmem = pl.BlockSpec(memory_space=pltpu.VMEM)
    hbm = pl.BlockSpec(memory_space=pltpu.HBM)
    return pl.pallas_call(
        norm_kernel,
        out_shape=jax.ShapeDtypeStruct((C, D), jnp.bfloat16),
        in_specs=[pl.BlockSpec(memory_space=pltpu.SMEM), vmem, vmem],
        out_specs=vmem,
        compiler_params=pltpu.CompilerParams(vmem_limit_bytes=16 * MIB),
        cost_estimate=pl.CostEstimate(flops=4 * C * D, bytes_accessed=4 * C * D, transcendentals=C),
    )(core, x, gain)


def start_copies(place_ref, pieces, sems, w_ref=None, o_ref=None):
    my_x, my_y = place_ref[1], place_ref[2]

    def block_of(part, stacked, ring):
        x, y = (stacked, ring) if part == 0 else (ring, stacked)
        x = lax.rem(my_x + x, 4)
        y = lax.rem(my_y + y, 4)
        return lax.rem(y, 2) * 8 + x * 2 + y // 2

    def move(slot, part, outputs):
        first = (slot * 2 + part) * len(RELATIVE)
        for index, (ring, low, high) in enumerate(RELATIVE):
            src = pieces[first + index]
            if outputs:
                if high < PART:
                    continue
                lanes, target = pl.ds(QKV_PART - low, PART - QKV_PART), None
            else:
                end = min(high, QKV_PART)
                lanes, target = pl.ds(0, end - low), pl.ds(low, end - low)
            for k, stacked in enumerate(STACKED):
                block = block_of(part, stacked, ring)
                if outputs:
                    width = PART - QKV_PART
                    dst = o_ref.at[slot, block, :, :, pl.ds(part * width, width)]
                else:
                    dst = w_ref.at[slot, part, block, :, :, target]
                sem = sems.at[4 + slot if outputs else slot * 2 + part]
                pltpu.make_async_copy(src.at[k, :, :, lanes], dst, sem).start()

    for outputs, ref in ((False, w_ref), (True, o_ref)):
        if ref is not None:
            for part in range(2):
                for slot in range(2):
                    move(slot, part, outputs)


def arrived(ref, sem):
    pltpu.make_async_copy(ref, ref, sem).wait()


def step_weights(w_ref, sems, g):
    part = g // 2
    for p in range(2):

        @pl.when(g == 2 * p)
        def _():
            for slot in range(2):
                arrived(w_ref.at[slot, p], sems.at[slot * 2 + p])

    base = lax.rem(g, 2) * (3 * PAIR)

    def weight(slot, kind):
        lanes = pl.ds(pl.multiple_of(base + kind * PAIR, PAIR), PAIR)
        return w_ref[slot, part, :, :, :, lanes].reshape(D // 2, PAIR)

    return weight


def output_sum(core, att_ref, rows, o_ref, h, total):
    for slot in range(2):
        for j in range(2):
            block = (core if slot == 0 else 1 - core) + 2 * j
            lanes = pl.ds(pl.multiple_of(block * PAIR, PAIR), PAIR)
            weight = o_ref[slot, j * 8 : (j + 1) * 8, h].reshape(PAIR, D // 2)
            total = total + dot(att_ref[rows, lanes], weight)
    return total


def row_kernel(place_ref, x_ref, hid_ref, gain_ref, cos_ref, sin_ref, *refs):
    pieces = refs[: 4 * len(RELATIVE)]
    mid_ref, next_ref, w_ref, o_ref, att_ref, sems = refs[4 * len(RELATIVE) :]
    core = place_ref[0]
    start_copies(place_ref, pieces, sems, w_ref, o_ref)
    half = D // 2

    def step(g, _):
        weight = step_weights(w_ref, sems, g)

        def projected(kind):
            return dot(hid_ref[:, :half], weight(0, kind)) + dot(hid_ref[:, half:], weight(1, kind))

        q2 = projected(0)
        k2 = projected(1)
        v2 = projected(2).astype(jnp.bfloat16)
        for h in range(2):
            lanes = slice(h * HEAD, (h + 1) * HEAD)
            q = rotate(q2[:, lanes], cos_ref[...], sin_ref[...]).astype(jnp.bfloat16)
            k = rotate(k2[:, lanes], cos_ref[...], sin_ref[...]).astype(jnp.bfloat16)
            v = v2[:, lanes]
            size = 256
            for b in range(C // size):
                end = (b + 1) * size
                scores = dot_t(q[b * size : end], k[:end])
                row = lax.broadcasted_iota(jnp.int32, scores.shape, 0) + b * size
                keep = lax.broadcasted_iota(jnp.int32, scores.shape, 1) <= row
                target = pl.ds(pl.multiple_of(g * PAIR + h * HEAD, HEAD), HEAD)
                att_ref[b * size : end, target] = softmax_times(scores, keep, v[:end]).astype(jnp.bfloat16)
        return 0

    lax.fori_loop(0, STEPS, step, 0)
    for slot in range(2):
        arrived(o_ref.at[slot], sems.at[4 + slot])

    def finish(i, _):
        rows = pl.ds(pl.multiple_of(i * 128, 128), 128)
        halves = []
        squares = jnp.zeros((128, 1), jnp.float32)
        for h in range(2):
            lanes = slice(h * half, (h + 1) * half)
            total = output_sum(core, att_ref, rows, o_ref, h, x_ref[rows, lanes].astype(jnp.float32))
            middle = total.astype(jnp.bfloat16)
            mid_ref[rows, lanes] = middle
            middle = middle.astype(jnp.float32)
            squares = squares + jnp.sum(middle * middle, axis=-1, keepdims=True)
            halves.append(middle)
        inv = lax.rsqrt(squares / D + 1e-05)
        for h in range(2):
            lanes = slice(h * half, (h + 1) * half)
            next_ref[rows, lanes] = (halves[h] * inv * gain_ref[:, lanes]).astype(jnp.bfloat16)
        return 0

    lax.fori_loop(0, C // 128, finish, 0)


def row_layer(place, x, hidden, gain, tables, pieces):
    vmem = pl.BlockSpec(memory_space=pltpu.VMEM)
    hbm = pl.BlockSpec(memory_space=pltpu.HBM)
    shape = jax.ShapeDtypeStruct((C, D), jnp.bfloat16)
    return pl.pallas_call(
        row_kernel,
        out_shape=[shape, shape],
        in_specs=[pl.BlockSpec(memory_space=pltpu.SMEM)]
        + [vmem] * 5
        + [hbm] * len(pieces),
        out_specs=[vmem, vmem],
        scratch_shapes=[
            pltpu.VMEM((2, 2, 16, 2, 32, QKV_PART), jnp.bfloat16),
            pltpu.VMEM((2, 16, 2, 32, D // 2), jnp.bfloat16),
            pltpu.VMEM((C, WIDTH), jnp.bfloat16),
            pltpu.SemaphoreType.DMA((6,)),
        ],
        compiler_params=pltpu.CompilerParams(vmem_limit_bytes=48 * MIB),
        cost_estimate=pl.CostEstimate(
            flops=2 * C * D * 4 * WIDTH + 4 * C * C * WIDTH,
            bytes_accessed=2 * (4 * C * D + 4 * D * WIDTH),
            transcendentals=C * C * HEADS,
        ),
    )(place, x, hidden, gain, *tables, *pieces)


def column_kernel(core_ref, x_ref, cos_ref, sin_ref, own_plane, other_plane, out_ref, w_ref, hid_ref, sems):
    core = core_ref[0]
    half = D // 2
    triple = 3 * PAIR

    for g in range(STEPS):
        lanes = pl.ds(g * triple, triple)
        for slot, plane in enumerate((own_plane, other_plane)):
            for ylo in range(2):
                for yhi in range(2):
                    src = plane.at[:, :, ylo, yhi, :, lanes]
                    dst = w_ref.at[g, slot, ylo, :, yhi]
                    pltpu.make_async_copy(src, dst, sems.at[g]).start()

    def selection(transposed):
        a = lax.broadcasted_iota(jnp.int32, (C, C), 1 if transposed else 0)
        b = lax.broadcasted_iota(jnp.int32, (C, C), 0 if transposed else 1)
        same = (a // N_SEQ == lax.rem(b, COLS)) & (lax.rem(a, N_SEQ) == b // COLS)
        return jnp.where(same, 1.0, 0.0).astype(jnp.bfloat16)

    pick = selection(False)
    width = D // 4
    for block in range(4):
        lanes = pl.ds(pl.multiple_of(slot_of(block, core) * width, width), width)
        moved = dot(pick, x_ref[:, block * width : (block + 1) * width])
        hid_ref[:, lanes] = moved.astype(jnp.bfloat16)

    back = selection(True)
    size = 128
    row = lax.broadcasted_iota(jnp.int32, (size, size), 0)
    col = lax.broadcasted_iota(jnp.int32, (size, size), 1)
    keep = (row // N_SEQ == col // N_SEQ) & (col <= row)

    def step(g, _):
        pltpu.make_async_copy(w_ref.at[g], w_ref.at[g], sems.at[g]).wait()

        def weight(slot, kind):
            lanes = slice(kind * PAIR, (kind + 1) * PAIR)
            return w_ref[g, slot, :, :, :, :, :, lanes].reshape(half, PAIR)

        def projected(kind):
            return dot(hid_ref[:, :half], weight(0, kind)) + dot(hid_ref[:, half:], weight(1, kind))

        q2 = projected(0)
        k2 = projected(1)
        v2 = projected(2).astype(jnp.bfloat16)
        heads = []
        for h in range(2):
            lanes = slice(h * HEAD, (h + 1) * HEAD)
            q = rotate(q2[:, lanes], cos_ref[...], sin_ref[...]).astype(jnp.bfloat16)
            k = rotate(k2[:, lanes], cos_ref[...], sin_ref[...]).astype(jnp.bfloat16)
            v = v2[:, lanes]
            blocks = []
            for b in range(C // size):
                rows = slice(b * size, (b + 1) * size)
                blocks.append(softmax_times(dot_t(q[rows], k[rows]), keep, v[rows]).astype(jnp.bfloat16))
            heads.append(jnp.concatenate(blocks, 0))
        attended = jnp.concatenate(heads, 1)
        lanes = pl.ds(pl.multiple_of(g * PAIR, PAIR), PAIR)
        out_ref[:, lanes] = dot(back, attended).astype(jnp.bfloat16)
        return 0

    lax.fori_loop(0, STEPS, step, 0)


def column_layer(core, x, tables, planes):
    vmem = pl.BlockSpec(memory_space=pltpu.VMEM)
    hbm = pl.BlockSpec(memory_space=pltpu.HBM)
    return pl.pallas_call(
        column_kernel,
        out_shape=jax.ShapeDtypeStruct((C, WIDTH), jnp.bfloat16),
        in_specs=[pl.BlockSpec(memory_space=pltpu.SMEM)] + [vmem] * 3 + [hbm] * 2,
        out_specs=vmem,
        scratch_shapes=[
            pltpu.VMEM((STEPS, 2, 2, 4, 2, 4, 16, 3 * PAIR), jnp.bfloat16),
            pltpu.VMEM((C, D), jnp.bfloat16),
            pltpu.SemaphoreType.DMA((STEPS,)),
        ],
        compiler_params=pltpu.CompilerParams(vmem_limit_bytes=56 * MIB),
        cost_estimate=pl.CostEstimate(
            flops=2 * C * D * 3 * WIDTH + 4 * C * C * WIDTH,
            bytes_accessed=2 * (C * D + 3 * D * WIDTH + C * WIDTH),
            transcendentals=C * C * HEADS,
        ),
    )(core, x, *tables, *planes)


def branch_sum(core, att_ref, own_ref, other_ref, resid_ref):
    width = WIDTH // 4
    total = resid_ref[...].astype(jnp.float32)
    for slot in range(4):
        block = jnp.where(slot < 2, core, 1 - core) + 2 * (slot % 2)
        lanes = pl.ds(pl.multiple_of(block * width, width), width)
        ref = own_ref if slot < 2 else other_ref
        rows = slice((slot % 2) * width, (slot % 2 + 1) * width)
        total = total + dot(att_ref[:, lanes], ref[rows, :])
    return total


def final_kernel(core_ref, att_ref, own_ref, other_ref, resid_ref, out_ref):
    out_ref[...] = branch_sum(core_ref[0], att_ref, own_ref, other_ref, resid_ref).astype(jnp.bfloat16)


def output_layer(core, attended, own, other, resid):
    size = 128
    block = lambda width: pl.BlockSpec((size, width), lambda i: (i, 0))
    whole = lambda shape: pl.BlockSpec(shape, lambda i: (0, 0), pipeline_mode=pl.Buffered(1))
    return pl.pallas_call(
        final_kernel,
        grid=(C // size,),
        out_shape=jax.ShapeDtypeStruct((C, D), jnp.bfloat16),
        in_specs=[
            pl.BlockSpec(memory_space=pltpu.SMEM),
            block(WIDTH),
            whole(own.shape),
            whole(other.shape),
            block(D),
        ],
        out_specs=block(D),
        compiler_params=pltpu.CompilerParams(
            dimension_semantics=("arbitrary",), vmem_limit_bytes=54 * MIB
        ),
        cost_estimate=pl.CostEstimate(
            flops=2 * C * D * WIDTH,
            bytes_accessed=2 * (2 * C * D + D * WIDTH + C * WIDTH),
            transcendentals=0,
        ),
    )(core, attended, own, other, resid)


def shift(value, axis, by):
    if axis == "y":
        where = lambda y: (y % 2) * 2 + y // 2
        return lax.ppermute(value, ("ylo", "yhi"), [(where(y), where((y + by) % 4)) for y in range(4)])
    return lax.ppermute(value, axis, [(i, (i + by) % 4) for i in range(4)])


def first_hops(value, axis):
    return [value, shift(value, axis, 1), shift(value, axis, -1)]


def forwards(hops, axis):
    own, left, right = hops
    half = own.shape[-1] // 2
    return hops + [shift(left[..., :half], axis, 1), shift(right[..., half:], axis, -1)]


def stack(pieces):
    own, left, right, low, high = pieces
    return jnp.stack([own, left, right, jnp.concatenate([low, high], -1)])


def swap(value):
    return lax.ppermute(value, "core", [(0, 1), (1, 0)])


def fold_output(output):
    return jnp.concatenate([output[:, : D // 2], output[:, D // 2 :]], 0)


def by_step(inputs):
    return inputs.reshape(-1, 3, STEPS, PAIR).transpose(0, 2, 1, 3).reshape(-1, 3 * WIDTH)


def lines(inputs, output):
    shard = jnp.concatenate([by_step(inputs), fold_output(output)], 1)
    rows = lax.all_gather(shard, "z", axis=0)
    qkv = rows[:, :, : 3 * WIDTH].reshape(2, 32, 3 * WIDTH)
    out = rows[:, :, 3 * WIDTH :].reshape(4, 2, 8, WIDTH).transpose(1, 0, 2, 3).reshape(2, 32, WIDTH)
    parts = []
    for p in range(2):
        lanes = slice(p * QKV_PART, (p + 1) * QKV_PART)
        rest = slice(p * WIDTH // 2, (p + 1) * WIDTH // 2)
        parts.append(jnp.concatenate([qkv[:, :, lanes], out[:, :, rest]], -1))
    return parts


def inner_rings(parts):
    hops = [first_hops(part, axis) for part, axis in zip(parts, "xy")]
    return [stack(forwards(hop, axis)) for hop, axis in zip(hops, "xy")]


def outer_hops(stacks):
    return [first_hops(part, axis) for part, axis in zip(stacks, "yx")]


def outer_forwards(hops):
    return [forwards(hop, axis) for hop, axis in zip(hops, "yx")]


def both_cores(parts):
    own = [piece for part in parts for piece in part]
    return own + [swap(piece) for piece in own]


def column_line(inputs, output):
    shard = jnp.concatenate([by_step(inputs), fold_output(output)], 1)
    return lax.all_gather(shard, ("ylo", "yhi"), axis=0)


def column_plane(line):
    return lax.all_gather(line, ("x", "z"), axis=0).reshape(4, 4, 2, 2, 16, 4 * WIDTH)


def column_output(plane):
    out = plane[..., 3 * WIDTH :].transpose(2, 0, 3, 1, 4, 5)
    return out.reshape(64, 2, 8, WIDTH).transpose(0, 2, 1, 3).reshape(WIDTH // 2, D)


def shards(tokens, gain_first, inputs_first, output_first, gain_second, inputs_second, output_second, starts, band_edges):
    residual = tokens[0]
    core = lax.axis_index("core").astype(jnp.int32)
    core_scalar = core.reshape(1)
    seq = lax.axis_index(SEQ)
    my_y = lax.axis_index("yhi") * 2 + lax.axis_index("ylo")
    place = jnp.stack([core, lax.axis_index("x").astype(jnp.int32), my_y.astype(jnp.int32)])

    frequency = frequencies(band_edges, HEAD // 2)
    block_starts = starts[0]
    own_start = lax.dynamic_index_in_dim(block_starts, seq, 0, keepdims=False)
    row_tables = rotary_tables(own_start + jnp.arange(C, dtype=jnp.int32), frequency)
    columns = seq.astype(jnp.int32) * COLS + jnp.arange(COLS, dtype=jnp.int32)
    column_positions = (columns[:, None] + block_starts[None, :]).reshape(C)
    column_tables = rotary_tables(column_positions, frequency)

    hidden = normed_slots(core_scalar, residual, gain_first.reshape(1, D))

    line = column_line(inputs_second, output_second)
    first = inner_rings(lines(inputs_first, output_first))
    first, hidden, row_tables, column_tables = lax.optimization_barrier((first, hidden, row_tables, column_tables))
    first_hop = outer_hops(first)
    line, _ = lax.optimization_barrier((line, first_hop))
    plane = column_plane(line)
    pieces = both_cores(outer_forwards(first_hop))

    middle, hidden = row_layer(place, residual, hidden, gain_second.reshape(1, D), row_tables, pieces)
    plane, hidden = lax.optimization_barrier((plane, hidden))
    planes = (plane, swap(plane))
    hidden = lax.all_to_all(hidden, SEQ, split_axis=0, concat_axis=0, tiled=True)
    attended = column_layer(core_scalar, hidden, column_tables, planes)
    attended = lax.all_to_all(attended, SEQ, split_axis=0, concat_axis=0, tiled=True)
    return output_layer(core_scalar, attended, *[column_output(p) for p in planes], middle)[None]


def solution(mesh):
    split = Mesh(mesh.devices.reshape(2, 2, 4, 2, 4), ("ylo", "core") + SEQ)
    dp = ("ylo", "core")
    every = dp + SEQ
    return jax.shard_map(
        shards,
        mesh=split,
        in_specs=(
            P(dp, SEQ, None),
            P(),
            P(every, None),
            P(every, None),
            P(),
            P(every, None),
            P(every, None),
            P(dp, None),
            P(),
        ),
        out_specs=P(dp, SEQ, None),
        check_vma=False,
    )
```

```python
import math

import jax
import jax.numpy as jnp
from jax import lax
from jax.experimental import pallas as pl
from jax.experimental.pallas import tpu as pltpu
from jax.sharding import Mesh, PartitionSpec as P

HEADS = 8
HEAD = 128
C = 512
SCALE = 8
D = 2048
WIDTH = HEADS * HEAD
N_SEQ = 32
COLS = C // N_SEQ
PAIR = 2 * HEAD
STEPS = WIDTH // PAIR
SEQ = ("x", "yhi", "z")
QKV_PART = 3 * WIDTH // 2
OUT_PART = WIDTH // 2
PART = QKV_PART + 2 * OUT_PART
RELATIVE = ((0, 0, PART), (3, 0, PART), (1, 0, PART), (2, 0, PART // 2), (2, PART // 2, PART))
STACKED = (0, 3, 1, 2)
LOG2E = 1.4426950408889634
MIB = 1 << 20


def frequencies(band_edges, half_size):
    dim_index = jnp.arange(half_size, dtype=jnp.float32)
    base_freq = jnp.power(10000.0, -dim_index / half_size)
    lower_edge = band_edges[0].astype(jnp.float32)
    upper_edge = band_edges[1].astype(jnp.float32)
    ramp_share = jnp.clip((dim_index - lower_edge) / (upper_edge - lower_edge), 0.0, 1.0)
    return base_freq * (1.0 - ramp_share) + base_freq * ramp_share / SCALE


def rotary_tables(positions, frequency):
    angles = positions.astype(jnp.float32)[:, None] * frequency
    mscale = 0.1 * math.log(SCALE) + 1.0
    cosine = jnp.cos(angles) * mscale
    sine = jnp.sin(angles) * mscale
    return jnp.concatenate([cosine, cosine], -1), jnp.concatenate([-sine, sine], -1)


def dot(a, b):
    return jnp.dot(a, b, preferred_element_type=jnp.float32)


def dot_t(a, b):
    return lax.dot_general(a, b, (((1,), (1,)), ((), ())), preferred_element_type=jnp.float32)


def slot_of(block, core):
    other = jnp.where(lax.rem(block, 2) == core, 0, 2)
    return other + block // 2


def rotate(heads, cos, sin):
    return heads * cos + pltpu.roll(heads, HEAD // 2, 1) * sin


def softmax_times(scores, keep, values):
    scores = jnp.where(keep, scores, -1e30)
    top = jnp.max(scores, axis=-1, keepdims=True)
    weights = jnp.exp2((scores - top) * (LOG2E / math.sqrt(HEAD)))
    total = jnp.sum(weights, axis=-1, keepdims=True)
    return dot(weights.astype(jnp.bfloat16), values) / total


def norm_kernel(core_ref, x_ref, gain_ref, hid_ref):
    core = core_ref[0]

    def chunk(i, _):
        rows = pl.ds(pl.multiple_of(i * 32, 32), 32)
        x = x_ref[rows, :].astype(jnp.float32)
        inv = lax.rsqrt(jnp.mean(x * x, axis=-1, keepdims=True) + 1e-05)
        hidden = (x * inv * gain_ref[...]).astype(jnp.bfloat16)
        width = D // 4
        for block in range(4):
            lanes = pl.ds(pl.multiple_of(slot_of(block, core) * width, width), width)
            hid_ref[rows, lanes] = hidden[:, block * width : (block + 1) * width]
        return 0

    lax.fori_loop(0, C // 32, chunk, 0)


def normed_slots(core, x, gain):
    vmem = pl.BlockSpec(memory_space=pltpu.VMEM)
    hbm = pl.BlockSpec(memory_space=pltpu.HBM)
    return pl.pallas_call(
        norm_kernel,
        out_shape=jax.ShapeDtypeStruct((C, D), jnp.bfloat16),
        in_specs=[pl.BlockSpec(memory_space=pltpu.SMEM), vmem, vmem],
        out_specs=vmem,
        compiler_params=pltpu.CompilerParams(vmem_limit_bytes=16 * MIB),
        cost_estimate=pl.CostEstimate(flops=4 * C * D, bytes_accessed=4 * C * D, transcendentals=C),
    )(core, x, gain)


def start_copies(place_ref, pieces, sems, w_ref=None, o_ref=None, base=None):
    my_x, my_y = place_ref[1], place_ref[2]

    def block_of(part, stacked, ring):
        x, y = (stacked, ring) if part == 0 else (ring, stacked)
        x = lax.rem(my_x + x, 4)
        y = lax.rem(my_y + y, 4)
        return lax.rem(y, 2) * 8 + x * 2 + y // 2

    def move(slot, part, outputs):
        first = (slot * 2 + part) * len(RELATIVE)
        for index, (ring, low, high) in enumerate(RELATIVE):
            src = pieces[first + index]
            if outputs:
                if high < PART:
                    continue
                lanes, target = pl.ds(base - low, OUT_PART), None
            else:
                end = min(high, QKV_PART)
                lanes, target = pl.ds(0, end - low), pl.ds(low, end - low)
            for k, stacked in enumerate(STACKED):
                block = block_of(part, stacked, ring)
                if outputs:
                    dst = o_ref.at[slot, block, :, :, pl.ds(part * OUT_PART, OUT_PART)]
                else:
                    dst = w_ref.at[slot, part, block, :, :, target]
                sem = sems.at[slot if outputs else slot * 2 + part]
                pltpu.make_async_copy(src.at[k, :, :, lanes], dst, sem).start()

    for outputs, ref in ((False, w_ref), (True, o_ref)):
        if ref is not None:
            for part in range(2):
                for slot in range(2):
                    move(slot, part, outputs)


def arrived(ref, sem):
    pltpu.make_async_copy(ref, ref, sem).wait()


def step_weights(w_ref, sems, g):
    part = g // 2
    for p in range(2):

        @pl.when(g == 2 * p)
        def _():
            for slot in range(2):
                arrived(w_ref.at[slot, p], sems.at[slot * 2 + p])

    base = lax.rem(g, 2) * (3 * PAIR)

    def weight(slot, kind):
        lanes = pl.ds(pl.multiple_of(base + kind * PAIR, PAIR), PAIR)
        return w_ref[slot, part, :, :, :, lanes].reshape(D // 2, PAIR)

    return weight


def output_sum(core, att_ref, rows, o_ref, h, total):
    for slot in range(2):
        for j in range(2):
            block = (core if slot == 0 else 1 - core) + 2 * j
            lanes = pl.ds(pl.multiple_of(block * PAIR, PAIR), PAIR)
            weight = o_ref[slot, j * 8 : (j + 1) * 8, h].reshape(PAIR, D // 2)
            total = total + dot(att_ref[rows, lanes], weight)
    return total


def row_kernel(hid_ref, cos_ref, sin_ref, own_plane, other_plane, out_ref, w_ref, sems):
    half = D // 2
    triple = 3 * PAIR
    for g in range(STEPS):
        lanes = pl.ds(g * triple, triple)
        for slot, plane in enumerate((own_plane, other_plane)):
            for ylo in range(2):
                for yhi in range(2):
                    src = plane.at[:, :, ylo, yhi, :, lanes]
                    dst = w_ref.at[g, slot, ylo, :, yhi]
                    pltpu.make_async_copy(src, dst, sems.at[g]).start()

    def step(g, _):
        arrived(w_ref.at[g], sems.at[g])

        def weight(slot, kind):
            lanes = slice(kind * PAIR, (kind + 1) * PAIR)
            return w_ref[g, slot, :, :, :, :, :, lanes].reshape(half, PAIR)

        def projected(kind):
            return dot(hid_ref[:, :half], weight(0, kind)) + dot(hid_ref[:, half:], weight(1, kind))

        q2 = projected(0)
        k2 = projected(1)
        v2 = projected(2).astype(jnp.bfloat16)
        for h in range(2):
            lanes = slice(h * HEAD, (h + 1) * HEAD)
            q = rotate(q2[:, lanes], cos_ref[...], sin_ref[...]).astype(jnp.bfloat16)
            k = rotate(k2[:, lanes], cos_ref[...], sin_ref[...]).astype(jnp.bfloat16)
            v = v2[:, lanes]
            size = 256
            for b in range(C // size):
                end = (b + 1) * size
                scores = dot_t(q[b * size : end], k[:end])
                row = lax.broadcasted_iota(jnp.int32, scores.shape, 0) + b * size
                keep = lax.broadcasted_iota(jnp.int32, scores.shape, 1) <= row
                target = pl.ds(pl.multiple_of(g * PAIR + h * HEAD, HEAD), HEAD)
                out_ref[b * size : end, target] = softmax_times(scores, keep, v[:end]).astype(jnp.bfloat16)
        return 0

    lax.fori_loop(0, STEPS, step, 0)


def row_layer(hidden, tables, planes):
    vmem = pl.BlockSpec(memory_space=pltpu.VMEM)
    hbm = pl.BlockSpec(memory_space=pltpu.HBM)
    return pl.pallas_call(
        row_kernel,
        out_shape=jax.ShapeDtypeStruct((C, WIDTH), jnp.bfloat16),
        in_specs=[vmem] * 3 + [hbm] * 2,
        out_specs=vmem,
        scratch_shapes=[
            pltpu.VMEM((STEPS, 2, 2, 4, 2, 4, 16, 3 * PAIR), jnp.bfloat16),
            pltpu.SemaphoreType.DMA((STEPS,)),
        ],
        compiler_params=pltpu.CompilerParams(vmem_limit_bytes=56 * MIB),
        cost_estimate=pl.CostEstimate(
            flops=2 * C * D * 3 * WIDTH + 4 * C * C * WIDTH,
            bytes_accessed=2 * (C * D + 3 * D * WIDTH + C * WIDTH),
            transcendentals=C * C * HEADS,
        ),
    )(hidden, *tables, *planes)


def middle_kernel(place_ref, att_ref, x_ref, gain_ref, *refs):
    pieces = refs[: 4 * len(RELATIVE)]
    mid_ref, next_ref, o_ref, sems = refs[4 * len(RELATIVE) :]
    core = place_ref[0]
    half = D // 2
    start_copies(place_ref, pieces, sems, o_ref=o_ref, base=QKV_PART + OUT_PART)
    for slot in range(2):
        arrived(o_ref.at[slot], sems.at[slot])

    def finish(i, _):
        rows = pl.ds(pl.multiple_of(i * 128, 128), 128)
        halves = []
        squares = jnp.zeros((128, 1), jnp.float32)
        for h in range(2):
            lanes = slice(h * half, (h + 1) * half)
            total = output_sum(core, att_ref, rows, o_ref, h, x_ref[rows, lanes].astype(jnp.float32))
            middle = total.astype(jnp.bfloat16)
            mid_ref[rows, lanes] = middle
            middle = middle.astype(jnp.float32)
            squares = squares + jnp.sum(middle * middle, axis=-1, keepdims=True)
            halves.append(middle)
        inv = lax.rsqrt(squares / D + 1e-05)
        for h in range(2):
            lanes = slice(h * half, (h + 1) * half)
            next_ref[rows, lanes] = (halves[h] * inv * gain_ref[:, lanes]).astype(jnp.bfloat16)
        return 0

    lax.fori_loop(0, C // 128, finish, 0)


def middle_layer(place, attended, x, gain, pieces):
    vmem = pl.BlockSpec(memory_space=pltpu.VMEM)
    hbm = pl.BlockSpec(memory_space=pltpu.HBM)
    shape = jax.ShapeDtypeStruct((C, D), jnp.bfloat16)
    return pl.pallas_call(
        middle_kernel,
        out_shape=[shape, shape],
        in_specs=[pl.BlockSpec(memory_space=pltpu.SMEM)] + [vmem] * 3 + [hbm] * len(pieces),
        out_specs=[vmem, vmem],
        scratch_shapes=[
            pltpu.VMEM((2, 16, 2, 32, D // 2), jnp.bfloat16),
            pltpu.SemaphoreType.DMA((2,)),
        ],
        compiler_params=pltpu.CompilerParams(vmem_limit_bytes=54 * MIB),
        cost_estimate=pl.CostEstimate(
            flops=2 * C * D * WIDTH,
            bytes_accessed=2 * (3 * C * D + D * WIDTH + C * WIDTH),
            transcendentals=0,
        ),
    )(place, attended, x, gain, *pieces)


def column_kernel(place_ref, x_ref, cos_ref, sin_ref, *refs):
    pieces = refs[: 4 * len(RELATIVE)]
    out_ref, w_ref, hid_ref, sems = refs[4 * len(RELATIVE) :]
    core = place_ref[0]
    half = D // 2
    start_copies(place_ref, pieces, sems, w_ref)

    def selection(transposed):
        a = lax.broadcasted_iota(jnp.int32, (C, C), 1 if transposed else 0)
        b = lax.broadcasted_iota(jnp.int32, (C, C), 0 if transposed else 1)
        same = (a // N_SEQ == lax.rem(b, COLS)) & (lax.rem(a, N_SEQ) == b // COLS)
        return jnp.where(same, 1.0, 0.0).astype(jnp.bfloat16)

    pick = selection(False)
    width = D // 4
    for block in range(4):
        lanes = pl.ds(pl.multiple_of(slot_of(block, core) * width, width), width)
        moved = dot(pick, x_ref[:, block * width : (block + 1) * width])
        hid_ref[:, lanes] = moved.astype(jnp.bfloat16)

    back = selection(True)
    size = 128
    row = lax.broadcasted_iota(jnp.int32, (size, size), 0)
    col = lax.broadcasted_iota(jnp.int32, (size, size), 1)
    keep = (row // N_SEQ == col // N_SEQ) & (col <= row)

    def step(g, _):
        weight = step_weights(w_ref, sems, g)

        def projected(kind):
            return dot(hid_ref[:, :half], weight(0, kind)) + dot(hid_ref[:, half:], weight(1, kind))

        q2 = projected(0)
        k2 = projected(1)
        v2 = projected(2).astype(jnp.bfloat16)
        heads = []
        for h in range(2):
            lanes = slice(h * HEAD, (h + 1) * HEAD)
            q = rotate(q2[:, lanes], cos_ref[...], sin_ref[...]).astype(jnp.bfloat16)
            k = rotate(k2[:, lanes], cos_ref[...], sin_ref[...]).astype(jnp.bfloat16)
            v = v2[:, lanes]
            blocks = []
            for b in range(C // size):
                rows = slice(b * size, (b + 1) * size)
                blocks.append(softmax_times(dot_t(q[rows], k[rows]), keep, v[rows]).astype(jnp.bfloat16))
            heads.append(jnp.concatenate(blocks, 0))
        attended = jnp.concatenate(heads, 1)
        lanes = pl.ds(pl.multiple_of(g * PAIR, PAIR), PAIR)
        out_ref[:, lanes] = dot(back, attended).astype(jnp.bfloat16)
        return 0

    lax.fori_loop(0, STEPS, step, 0)


def column_layer(place, x, tables, pieces):
    vmem = pl.BlockSpec(memory_space=pltpu.VMEM)
    hbm = pl.BlockSpec(memory_space=pltpu.HBM)
    return pl.pallas_call(
        column_kernel,
        out_shape=jax.ShapeDtypeStruct((C, WIDTH), jnp.bfloat16),
        in_specs=[pl.BlockSpec(memory_space=pltpu.SMEM)] + [vmem] * 3 + [hbm] * len(pieces),
        out_specs=vmem,
        scratch_shapes=[
            pltpu.VMEM((2, 2, 16, 2, 32, QKV_PART), jnp.bfloat16),
            pltpu.VMEM((C, D), jnp.bfloat16),
            pltpu.SemaphoreType.DMA((4,)),
        ],
        compiler_params=pltpu.CompilerParams(vmem_limit_bytes=56 * MIB),
        cost_estimate=pl.CostEstimate(
            flops=2 * C * D * 3 * WIDTH + 4 * C * C * WIDTH,
            bytes_accessed=2 * (C * D + 3 * D * WIDTH + C * WIDTH),
            transcendentals=C * C * HEADS,
        ),
    )(place, x, *tables, *pieces)


def final_kernel(place_ref, att_ref, x_ref, *refs):
    pieces = refs[: 4 * len(RELATIVE)]
    out_ref, o_ref, sems = refs[4 * len(RELATIVE) :]
    core = place_ref[0]
    half = D // 2

    @pl.when(pl.program_id(0) == 0)
    def _():
        start_copies(place_ref, pieces, sems, o_ref=o_ref, base=QKV_PART)
        for slot in range(2):
            arrived(o_ref.at[slot], sems.at[slot])

    for h in range(2):
        lanes = slice(h * half, (h + 1) * half)
        total = x_ref[:, lanes].astype(jnp.float32)
        out_ref[:, lanes] = output_sum(core, att_ref, slice(None), o_ref, h, total).astype(jnp.bfloat16)


def final_layer(place, attended, x, pieces):
    size = 128
    block = lambda width: pl.BlockSpec((size, width), lambda i: (i, 0))
    hbm = pl.BlockSpec(memory_space=pltpu.HBM)
    return pl.pallas_call(
        final_kernel,
        grid=(C // size,),
        out_shape=jax.ShapeDtypeStruct((C, D), jnp.bfloat16),
        in_specs=[pl.BlockSpec(memory_space=pltpu.SMEM), block(WIDTH), block(D)] + [hbm] * len(pieces),
        out_specs=block(D),
        scratch_shapes=[
            pltpu.VMEM((2, 16, 2, 32, D // 2), jnp.bfloat16),
            pltpu.SemaphoreType.DMA((2,)),
        ],
        compiler_params=pltpu.CompilerParams(
            dimension_semantics=("arbitrary",), vmem_limit_bytes=54 * MIB
        ),
        cost_estimate=pl.CostEstimate(
            flops=2 * C * D * WIDTH,
            bytes_accessed=2 * (2 * C * D + D * WIDTH + C * WIDTH),
            transcendentals=0,
        ),
    )(place, attended, x, *pieces)


def shift(value, axis, by):
    if axis == "y":
        where = lambda y: (y % 2) * 2 + y // 2
        return lax.ppermute(value, ("ylo", "yhi"), [(where(y), where((y + by) % 4)) for y in range(4)])
    return lax.ppermute(value, axis, [(i, (i + by) % 4) for i in range(4)])


def first_hops(value, axis):
    return [value, shift(value, axis, 1), shift(value, axis, -1)]


def forwards(hops, axis):
    own, left, right = hops
    half = own.shape[-1] // 2
    return hops + [shift(left[..., :half], axis, 1), shift(right[..., half:], axis, -1)]


def stack(pieces):
    own, left, right, low, high = pieces
    return jnp.stack([own, left, right, jnp.concatenate([low, high], -1)])


def swap(value):
    return lax.ppermute(value, "core", [(0, 1), (1, 0)])


def fold_output(output):
    return jnp.concatenate([output[:, : D // 2], output[:, D // 2 :]], 0)


def by_step(inputs):
    return inputs.reshape(-1, 3, STEPS, PAIR).transpose(0, 2, 1, 3).reshape(-1, 3 * WIDTH)


def lines(inputs, *outputs):
    shard = jnp.concatenate([by_step(inputs)] + [fold_output(output) for output in outputs], 1)
    rows = lax.all_gather(shard, "z", axis=0)
    qkv = rows[:, :, : 3 * WIDTH].reshape(2, 32, 3 * WIDTH)
    outs = rows[:, :, 3 * WIDTH :].reshape(4, 2, 8, len(outputs), WIDTH).transpose(3, 1, 0, 2, 4)
    outs = outs.reshape(len(outputs), 2, 32, WIDTH)
    parts = []
    for p in range(2):
        lanes = slice(p * QKV_PART, (p + 1) * QKV_PART)
        rest = slice(p * OUT_PART, (p + 1) * OUT_PART)
        parts.append(jnp.concatenate([qkv[:, :, lanes]] + [out[:, :, rest] for out in outs], -1))
    return parts


def row_plane(inputs):
    line = lax.all_gather(by_step(inputs), ("ylo", "yhi"), axis=0)
    return line, lax.all_gather(line, ("x", "z"), axis=0).reshape(4, 4, 2, 2, 16, 3 * WIDTH)


def inner_rings(parts):
    hops = [first_hops(part, axis) for part, axis in zip(parts, "xy")]
    return [stack(forwards(hop, axis)) for hop, axis in zip(hops, "xy")]


def outer_hops(stacks):
    return [first_hops(part, axis) for part, axis in zip(stacks, "yx")]


def outer_forwards(hops):
    return [forwards(hop, axis) for hop, axis in zip(hops, "yx")]


def both_cores(parts):
    own = [piece for part in parts for piece in part]
    return own + [swap(piece) for piece in own]


def shards(tokens, gain_first, inputs_first, output_first, gain_second, inputs_second, output_second, starts, band_edges):
    residual = tokens[0]
    core = lax.axis_index("core").astype(jnp.int32)
    core_scalar = core.reshape(1)
    seq = lax.axis_index(SEQ)
    my_y = lax.axis_index("yhi") * 2 + lax.axis_index("ylo")
    place = jnp.stack([core, lax.axis_index("x").astype(jnp.int32), my_y.astype(jnp.int32)])

    frequency = frequencies(band_edges, HEAD // 2)
    block_starts = starts[0]
    own_start = lax.dynamic_index_in_dim(block_starts, seq, 0, keepdims=False)
    row_tables = rotary_tables(own_start + jnp.arange(C, dtype=jnp.int32), frequency)
    columns = seq.astype(jnp.int32) * COLS + jnp.arange(COLS, dtype=jnp.int32)
    column_positions = (columns[:, None] + block_starts[None, :]).reshape(C)
    column_tables = rotary_tables(column_positions, frequency)

    hidden = normed_slots(core_scalar, residual, gain_first.reshape(1, D))

    line, plane = row_plane(inputs_first)
    output_first, output_second, inputs_second, line = lax.optimization_barrier(
        (output_first, output_second, inputs_second, line)
    )
    stacks = inner_rings(lines(inputs_second, output_second, output_first))
    hops = outer_hops(stacks)
    plane, hidden, row_tables, column_tables, _ = lax.optimization_barrier(
        (plane, hidden, row_tables, column_tables, hops)
    )
    planes = (plane, swap(plane))
    pieces = both_cores(outer_forwards(hops))

    attended = row_layer(hidden, row_tables, planes)
    middle, hidden = middle_layer(place, attended, residual, gain_second.reshape(1, D), pieces)
    hidden = lax.all_to_all(hidden, SEQ, split_axis=0, concat_axis=0, tiled=True)
    attended = column_layer(place, hidden, column_tables, pieces)
    attended = lax.all_to_all(attended, SEQ, split_axis=0, concat_axis=0, tiled=True)
    return final_layer(place, attended, middle, pieces)[None]


def solution(mesh):
    split = Mesh(mesh.devices.reshape(2, 2, 4, 2, 4), ("ylo", "core") + SEQ)
    dp = ("ylo", "core")
    every = dp + SEQ
    return jax.shard_map(
        shards,
        mesh=split,
        in_specs=(
            P(dp, SEQ, None),
            P(),
            P(every, None),
            P(every, None),
            P(),
            P(every, None),
            P(every, None),
            P(dp, None),
            P(),
        ),
        out_specs=P(dp, SEQ, None),
        check_vma=False,
    )
```

```python
import math

import jax
import jax.numpy as jnp
from jax import lax
from jax.experimental import pallas as pl
from jax.experimental.pallas import tpu as pltpu
from jax.sharding import Mesh, PartitionSpec as P

HEADS = 8
HEAD = 128
C = 512
SCALE = 8
D = 2048
WIDTH = HEADS * HEAD
N_SEQ = 32
COLS = C // N_SEQ
PAIR = 2 * HEAD
STEPS = WIDTH // PAIR
SEQ = ("x", "yhi", "z")
QKV_PART = 3 * WIDTH // 2
PART = 2 * WIDTH
RELATIVE = (0, 3, 1, 2)
PIECES = 2 * 2 * 2 * len(RELATIVE)
LOG2E = 1.4426950408889634
MIB = 1 << 20


def frequencies(band_edges, half_size):
    dim_index = jnp.arange(half_size, dtype=jnp.float32)
    base_freq = jnp.power(10000.0, -dim_index / half_size)
    lower_edge = band_edges[0].astype(jnp.float32)
    upper_edge = band_edges[1].astype(jnp.float32)
    ramp_share = jnp.clip((dim_index - lower_edge) / (upper_edge - lower_edge), 0.0, 1.0)
    return base_freq * (1.0 - ramp_share) + base_freq * ramp_share / SCALE


def rotary_tables(positions, frequency):
    angles = positions.astype(jnp.float32)[:, None] * frequency
    mscale = 0.1 * math.log(SCALE) + 1.0
    cosine = jnp.cos(angles) * mscale
    sine = jnp.sin(angles) * mscale
    return jnp.concatenate([cosine, cosine], -1), jnp.concatenate([-sine, sine], -1)


def dot(a, b):
    return jnp.dot(a, b, preferred_element_type=jnp.float32)


def dot_t(a, b):
    return lax.dot_general(a, b, (((1,), (1,)), ((), ())), preferred_element_type=jnp.float32)


def slot_of(block, core):
    other = jnp.where(lax.rem(block, 2) == core, 0, 2)
    return other + block // 2


def rotate(heads, cos, sin):
    return heads * cos + pltpu.roll(heads, HEAD // 2, 1) * sin


def softmax_times(scores, keep, values):
    scores = jnp.where(keep, scores, -1e30)
    top = jnp.max(scores, axis=-1, keepdims=True)
    weights = jnp.exp2((scores - top) * (LOG2E / math.sqrt(HEAD)))
    total = jnp.sum(weights, axis=-1, keepdims=True)
    return dot(weights.astype(jnp.bfloat16), values) / total


def norm_kernel(core_ref, x_ref, gain_ref, hid_ref):
    core = core_ref[0]

    def chunk(i, _):
        rows = pl.ds(pl.multiple_of(i * 32, 32), 32)
        x = x_ref[rows, :].astype(jnp.float32)
        inv = lax.rsqrt(jnp.mean(x * x, axis=-1, keepdims=True) + 1e-05)
        hidden = (x * inv * gain_ref[...]).astype(jnp.bfloat16)
        width = D // 4
        for block in range(4):
            lanes = pl.ds(pl.multiple_of(slot_of(block, core) * width, width), width)
            hid_ref[rows, lanes] = hidden[:, block * width : (block + 1) * width]
        return 0

    lax.fori_loop(0, C // 32, chunk, 0)


def normed_slots(core, x, gain):
    vmem = pl.BlockSpec(memory_space=pltpu.VMEM)
    hbm = pl.BlockSpec(memory_space=pltpu.HBM)
    return pl.pallas_call(
        norm_kernel,
        out_shape=jax.ShapeDtypeStruct((C, D), jnp.bfloat16),
        in_specs=[pl.BlockSpec(memory_space=pltpu.SMEM), vmem, vmem],
        out_specs=vmem,
        compiler_params=pltpu.CompilerParams(vmem_limit_bytes=16 * MIB),
        cost_estimate=pl.CostEstimate(flops=4 * C * D, bytes_accessed=4 * C * D, transcendentals=C),
    )(core, x, gain)


def start_copies(place_ref, pieces, sems, w_ref=None, o_ref=None):
    my_x, my_y = place_ref[1], place_ref[2]

    def block_of(part, stacked, ring):
        x, y = (stacked, ring) if part == 0 else (ring, stacked)
        x = lax.rem(my_x + x, 4)
        y = lax.rem(my_y + y, 4)
        return lax.rem(y, 2) * 8 + x * 2 + y // 2

    def move(slot, part, outputs):
        cut = QKV_PART - WIDTH
        for half in range(2):
            first = ((slot * 2 + part) * 2 + half) * len(RELATIVE)
            for index, ring in enumerate(RELATIVE):
                src = pieces[first + index]
                if outputs:
                    if half == 0:
                        continue
                    lanes = pl.ds(cut, WIDTH - cut)
                else:
                    width = cut if half else WIDTH
                    lanes, target = pl.ds(0, width), pl.ds(half * WIDTH, width)
                for k, stacked in enumerate(RELATIVE):
                    block = block_of(part, stacked, ring)
                    if outputs:
                        width = WIDTH - cut
                        dst = o_ref.at[slot, block, :, :, pl.ds(part * width, width)]
                    else:
                        dst = w_ref.at[slot, part, block, :, :, target]
                    sem = sems.at[4 + slot if outputs else slot * 2 + part]
                    pltpu.make_async_copy(src.at[k, :, :, lanes], dst, sem).start()

    for outputs, ref in ((False, w_ref), (True, o_ref)):
        if ref is not None:
            for part in range(2):
                for slot in range(2):
                    move(slot, part, outputs)


def arrived(ref, sem):
    pltpu.make_async_copy(ref, ref, sem).wait()


def step_weights(w_ref, sems, g):
    part = g // 2
    for p in range(2):

        @pl.when(g == 2 * p)
        def _():
            for slot in range(2):
                arrived(w_ref.at[slot, p], sems.at[slot * 2 + p])

    base = lax.rem(g, 2) * (3 * PAIR)

    def weight(slot, kind):
        lanes = pl.ds(pl.multiple_of(base + kind * PAIR, PAIR), PAIR)
        return w_ref[slot, part, :, :, :, lanes].reshape(D // 2, PAIR)

    return weight


def output_sum(core, att_ref, rows, o_ref, h, total):
    for slot in range(2):
        for j in range(2):
            block = (core if slot == 0 else 1 - core) + 2 * j
            lanes = pl.ds(pl.multiple_of(block * PAIR, PAIR), PAIR)
            weight = o_ref[slot, j * 8 : (j + 1) * 8, h].reshape(PAIR, D // 2)
            total = total + dot(att_ref[rows, lanes], weight)
    return total


def row_kernel(place_ref, x_ref, hid_ref, gain_ref, cos_ref, sin_ref, *refs):
    pieces = refs[: PIECES]
    mid_ref, next_ref, w_ref, o_ref, att_ref, sems = refs[PIECES :]
    core = place_ref[0]
    start_copies(place_ref, pieces, sems, w_ref, o_ref)
    half = D // 2

    def step(g, _):
        weight = step_weights(w_ref, sems, g)

        def projected(kind):
            return dot(hid_ref[:, :half], weight(0, kind)) + dot(hid_ref[:, half:], weight(1, kind))

        q2 = projected(0)
        k2 = projected(1)
        v2 = projected(2).astype(jnp.bfloat16)
        for h in range(2):
            lanes = slice(h * HEAD, (h + 1) * HEAD)
            q = rotate(q2[:, lanes], cos_ref[...], sin_ref[...]).astype(jnp.bfloat16)
            k = rotate(k2[:, lanes], cos_ref[...], sin_ref[...]).astype(jnp.bfloat16)
            v = v2[:, lanes]
            size = 256
            for b in range(C // size):
                end = (b + 1) * size
                scores = dot_t(q[b * size : end], k[:end])
                row = lax.broadcasted_iota(jnp.int32, scores.shape, 0) + b * size
                keep = lax.broadcasted_iota(jnp.int32, scores.shape, 1) <= row
                target = pl.ds(pl.multiple_of(g * PAIR + h * HEAD, HEAD), HEAD)
                att_ref[b * size : end, target] = softmax_times(scores, keep, v[:end]).astype(jnp.bfloat16)
        return 0

    lax.fori_loop(0, STEPS, step, 0)
    for slot in range(2):
        arrived(o_ref.at[slot], sems.at[4 + slot])

    def finish(i, _):
        rows = pl.ds(pl.multiple_of(i * 128, 128), 128)
        halves = []
        squares = jnp.zeros((128, 1), jnp.float32)
        for h in range(2):
            lanes = slice(h * half, (h + 1) * half)
            total = output_sum(core, att_ref, rows, o_ref, h, x_ref[rows, lanes].astype(jnp.float32))
            middle = total.astype(jnp.bfloat16)
            mid_ref[rows, lanes] = middle
            middle = middle.astype(jnp.float32)
            squares = squares + jnp.sum(middle * middle, axis=-1, keepdims=True)
            halves.append(middle)
        inv = lax.rsqrt(squares / D + 1e-05)
        for h in range(2):
            lanes = slice(h * half, (h + 1) * half)
            next_ref[rows, lanes] = (halves[h] * inv * gain_ref[:, lanes]).astype(jnp.bfloat16)
        return 0

    lax.fori_loop(0, C // 128, finish, 0)


def row_layer(place, x, hidden, gain, tables, pieces):
    vmem = pl.BlockSpec(memory_space=pltpu.VMEM)
    hbm = pl.BlockSpec(memory_space=pltpu.HBM)
    shape = jax.ShapeDtypeStruct((C, D), jnp.bfloat16)
    return pl.pallas_call(
        row_kernel,
        out_shape=[shape, shape],
        in_specs=[pl.BlockSpec(memory_space=pltpu.SMEM)]
        + [vmem] * 5
        + [hbm] * len(pieces),
        out_specs=[vmem, vmem],
        scratch_shapes=[
            pltpu.VMEM((2, 2, 16, 2, 32, QKV_PART), jnp.bfloat16),
            pltpu.VMEM((2, 16, 2, 32, D // 2), jnp.bfloat16),
            pltpu.VMEM((C, WIDTH), jnp.bfloat16),
            pltpu.SemaphoreType.DMA((6,)),
        ],
        compiler_params=pltpu.CompilerParams(vmem_limit_bytes=48 * MIB),
        cost_estimate=pl.CostEstimate(
            flops=2 * C * D * 4 * WIDTH + 4 * C * C * WIDTH,
            bytes_accessed=2 * (4 * C * D + 4 * D * WIDTH),
            transcendentals=C * C * HEADS,
        ),
    )(place, x, hidden, gain, *tables, *pieces)


def column_kernel(core_ref, x_ref, cos_ref, sin_ref, own_plane, other_plane, out_ref, w_ref, hid_ref, sems):
    core = core_ref[0]
    half = D // 2
    triple = 3 * PAIR

    for g in range(STEPS):
        lanes = pl.ds(g * triple, triple)
        for slot, plane in enumerate((own_plane, other_plane)):
            for ylo in range(2):
                for yhi in range(2):
                    src = plane.at[:, :, ylo, yhi, :, lanes]
                    dst = w_ref.at[g, slot, ylo, :, yhi]
                    pltpu.make_async_copy(src, dst, sems.at[g]).start()

    def selection(transposed):
        a = lax.broadcasted_iota(jnp.int32, (C, C), 1 if transposed else 0)
        b = lax.broadcasted_iota(jnp.int32, (C, C), 0 if transposed else 1)
        same = (a // N_SEQ == lax.rem(b, COLS)) & (lax.rem(a, N_SEQ) == b // COLS)
        return jnp.where(same, 1.0, 0.0).astype(jnp.bfloat16)

    pick = selection(False)
    width = D // 4
    for block in range(4):
        lanes = pl.ds(pl.multiple_of(slot_of(block, core) * width, width), width)
        moved = dot(pick, x_ref[:, block * width : (block + 1) * width])
        hid_ref[:, lanes] = moved.astype(jnp.bfloat16)

    back = selection(True)
    size = 128
    row = lax.broadcasted_iota(jnp.int32, (size, size), 0)
    col = lax.broadcasted_iota(jnp.int32, (size, size), 1)
    keep = (row // N_SEQ == col // N_SEQ) & (col <= row)

    def step(g, _):
        pltpu.make_async_copy(w_ref.at[g], w_ref.at[g], sems.at[g]).wait()

        def weight(slot, kind):
            lanes = slice(kind * PAIR, (kind + 1) * PAIR)
            return w_ref[g, slot, :, :, :, :, :, lanes].reshape(half, PAIR)

        def projected(kind):
            return dot(hid_ref[:, :half], weight(0, kind)) + dot(hid_ref[:, half:], weight(1, kind))

        q2 = projected(0)
        k2 = projected(1)
        v2 = projected(2).astype(jnp.bfloat16)
        heads = []
        for h in range(2):
            lanes = slice(h * HEAD, (h + 1) * HEAD)
            q = rotate(q2[:, lanes], cos_ref[...], sin_ref[...]).astype(jnp.bfloat16)
            k = rotate(k2[:, lanes], cos_ref[...], sin_ref[...]).astype(jnp.bfloat16)
            v = v2[:, lanes]
            blocks = []
            for b in range(C // size):
                rows = slice(b * size, (b + 1) * size)
                blocks.append(softmax_times(dot_t(q[rows], k[rows]), keep, v[rows]).astype(jnp.bfloat16))
            heads.append(jnp.concatenate(blocks, 0))
        attended = jnp.concatenate(heads, 1)
        lanes = pl.ds(pl.multiple_of(g * PAIR, PAIR), PAIR)
        out_ref[:, lanes] = dot(back, attended).astype(jnp.bfloat16)
        return 0

    lax.fori_loop(0, STEPS, step, 0)


def column_layer(core, x, tables, planes):
    vmem = pl.BlockSpec(memory_space=pltpu.VMEM)
    hbm = pl.BlockSpec(memory_space=pltpu.HBM)
    return pl.pallas_call(
        column_kernel,
        out_shape=jax.ShapeDtypeStruct((C, WIDTH), jnp.bfloat16),
        in_specs=[pl.BlockSpec(memory_space=pltpu.SMEM)] + [vmem] * 3 + [hbm] * 2,
        out_specs=vmem,
        scratch_shapes=[
            pltpu.VMEM((STEPS, 2, 2, 4, 2, 4, 16, 3 * PAIR), jnp.bfloat16),
            pltpu.VMEM((C, D), jnp.bfloat16),
            pltpu.SemaphoreType.DMA((STEPS,)),
        ],
        compiler_params=pltpu.CompilerParams(vmem_limit_bytes=56 * MIB),
        cost_estimate=pl.CostEstimate(
            flops=2 * C * D * 3 * WIDTH + 4 * C * C * WIDTH,
            bytes_accessed=2 * (C * D + 3 * D * WIDTH + C * WIDTH),
            transcendentals=C * C * HEADS,
        ),
    )(core, x, *tables, *planes)


def branch_sum(core, att_ref, own_ref, other_ref, resid_ref):
    width = WIDTH // 4
    total = resid_ref[...].astype(jnp.float32)
    for slot in range(4):
        block = jnp.where(slot < 2, core, 1 - core) + 2 * (slot % 2)
        lanes = pl.ds(pl.multiple_of(block * width, width), width)
        ref = own_ref if slot < 2 else other_ref
        rows = slice((slot % 2) * width, (slot % 2 + 1) * width)
        total = total + dot(att_ref[:, lanes], ref[rows, :])
    return total


def final_kernel(core_ref, att_ref, own_ref, other_ref, resid_ref, out_ref):
    out_ref[...] = branch_sum(core_ref[0], att_ref, own_ref, other_ref, resid_ref).astype(jnp.bfloat16)


def output_layer(core, attended, own, other, resid):
    size = 128
    block = lambda width: pl.BlockSpec((size, width), lambda i: (i, 0))
    whole = lambda shape: pl.BlockSpec(shape, lambda i: (0, 0), pipeline_mode=pl.Buffered(1))
    return pl.pallas_call(
        final_kernel,
        grid=(C // size,),
        out_shape=jax.ShapeDtypeStruct((C, D), jnp.bfloat16),
        in_specs=[
            pl.BlockSpec(memory_space=pltpu.SMEM),
            block(WIDTH),
            whole(own.shape),
            whole(other.shape),
            block(D),
        ],
        out_specs=block(D),
        compiler_params=pltpu.CompilerParams(
            dimension_semantics=("arbitrary",), vmem_limit_bytes=54 * MIB
        ),
        cost_estimate=pl.CostEstimate(
            flops=2 * C * D * WIDTH,
            bytes_accessed=2 * (2 * C * D + D * WIDTH + C * WIDTH),
            transcendentals=0,
        ),
    )(core, attended, own, other, resid)


def shift(value, axis, by):
    if axis == "y":
        where = lambda y: (y % 2) * 2 + y // 2
        return lax.ppermute(value, ("ylo", "yhi"), [(where(y), where((y + by) % 4)) for y in range(4)])
    return lax.ppermute(value, axis, [(i, (i + by) % 4) for i in range(4)])


def inner_ring(part, axis):
    half = part.shape[-1] // 2
    left = shift(part, axis, 1)
    right = shift(part, axis, -1)
    opposite = (shift(left[..., :half], axis, 1), shift(right[..., half:], axis, -1))
    lanes = (slice(0, half), slice(half, 2 * half))
    return [
        jnp.stack([part[..., lanes[h]], left[..., lanes[h]], right[..., lanes[h]], opposite[h]])
        for h in range(2)
    ]


def outer_hops(stacks):
    return [
        [(stack, shift(stack, axis, 1), shift(stack, axis, -1)) for stack in part]
        for part, axis in zip(stacks, "yx")
    ]


def outer_pieces(hops):
    pieces = []
    for part, axis in zip(hops, "yx"):
        for half, (own, left, right) in enumerate(part):
            far = shift(right, axis, -1) if half else shift(left, axis, 1)
            pieces += [own, left, right, far]
    return pieces


def swap(value):
    return lax.ppermute(value, "core", [(0, 1), (1, 0)])


def fold_output(output):
    return jnp.concatenate([output[:, : D // 2], output[:, D // 2 :]], 0)


def by_step(inputs):
    return inputs.reshape(-1, 3, STEPS, PAIR).transpose(0, 2, 1, 3).reshape(-1, 3 * WIDTH)


def lines(inputs, output):
    shard = jnp.concatenate([by_step(inputs), fold_output(output)], 1)
    rows = lax.all_gather(shard, "z", axis=0)
    qkv = rows[:, :, : 3 * WIDTH].reshape(2, 32, 3 * WIDTH)
    out = rows[:, :, 3 * WIDTH :].reshape(4, 2, 8, WIDTH).transpose(1, 0, 2, 3).reshape(2, 32, WIDTH)
    parts = []
    for p in range(2):
        lanes = slice(p * QKV_PART, (p + 1) * QKV_PART)
        rest = slice(p * WIDTH // 2, (p + 1) * WIDTH // 2)
        parts.append(jnp.concatenate([qkv[:, :, lanes], out[:, :, rest]], -1))
    return parts


def column_line(inputs, output):
    shard = jnp.concatenate([by_step(inputs), fold_output(output)], 1)
    return lax.all_gather(jnp.concatenate([shard, shard], 1), ("ylo", "yhi"), axis=0)[:, :, : 4 * WIDTH]


def column_plane(line):
    return lax.all_gather(line, ("x", "z"), axis=0).reshape(4, 4, 2, 2, 16, 4 * WIDTH)


def column_output(plane):
    out = plane[..., 3 * WIDTH :].transpose(2, 0, 3, 1, 4, 5)
    return out.reshape(64, 2, 8, WIDTH).transpose(0, 2, 1, 3).reshape(WIDTH // 2, D)


def shards(tokens, gain_first, inputs_first, output_first, gain_second, inputs_second, output_second, starts, band_edges):
    residual = tokens[0]
    core = lax.axis_index("core").astype(jnp.int32)
    core_scalar = core.reshape(1)
    seq = lax.axis_index(SEQ)
    my_y = lax.axis_index("yhi") * 2 + lax.axis_index("ylo")
    place = jnp.stack([core, lax.axis_index("x").astype(jnp.int32), my_y.astype(jnp.int32)])

    frequency = frequencies(band_edges, HEAD // 2)
    block_starts = starts[0]
    own_start = lax.dynamic_index_in_dim(block_starts, seq, 0, keepdims=False)
    row_tables = rotary_tables(own_start + jnp.arange(C, dtype=jnp.int32), frequency)
    columns = seq.astype(jnp.int32) * COLS + jnp.arange(COLS, dtype=jnp.int32)
    column_positions = (columns[:, None] + block_starts[None, :]).reshape(C)
    column_tables = rotary_tables(column_positions, frequency)

    hidden = normed_slots(core_scalar, residual, gain_first.reshape(1, D))

    line = column_line(inputs_second, output_second)
    first = [inner_ring(part, axis) for part, axis in zip(lines(inputs_first, output_first), "xy")]
    first, hidden, row_tables, column_tables = lax.optimization_barrier((first, hidden, row_tables, column_tables))
    first_hop = outer_hops(first)
    line, _ = lax.optimization_barrier((line, first_hop))
    plane = column_plane(line)
    pieces = outer_pieces(first_hop)
    pieces = pieces + [swap(piece) for piece in pieces]

    middle, hidden = row_layer(place, residual, hidden, gain_second.reshape(1, D), row_tables, pieces)
    plane, hidden = lax.optimization_barrier((plane, hidden))
    planes = (plane, swap(plane))
    hidden = lax.all_to_all(hidden, SEQ, split_axis=0, concat_axis=0, tiled=True)
    attended = column_layer(core_scalar, hidden, column_tables, planes)
    attended = lax.all_to_all(attended, SEQ, split_axis=0, concat_axis=0, tiled=True)
    return output_layer(core_scalar, attended, *[column_output(p) for p in planes], middle)[None]


def solution(mesh):
    split = Mesh(mesh.devices.reshape(2, 2, 4, 2, 4), ("ylo", "core") + SEQ)
    dp = ("ylo", "core")
    every = dp + SEQ
    return jax.shard_map(
        shards,
        mesh=split,
        in_specs=(
            P(dp, SEQ, None),
            P(),
            P(every, None),
            P(every, None),
            P(),
            P(every, None),
            P(every, None),
            P(dp, None),
            P(),
        ),
        out_specs=P(dp, SEQ, None),
        check_vma=False,
    )
```

```python
import functools
import math

import jax
import jax.numpy as jnp
from jax import lax
from jax.experimental import pallas as pl
from jax.experimental.pallas import tpu as pltpu
from jax.sharding import Mesh, PartitionSpec as P

HEADS = 8
HEAD = 128
C = 512
SCALE = 8
D = 2048
WIDTH = HEADS * HEAD
N_SEQ = 32
ROWS = C // 2
COLS = ROWS // N_SEQ
PAIR = 2 * HEAD
STEPS = WIDTH // PAIR
SEQ = ("x", "yhi", "z")
QKV_PART = 3 * WIDTH // 2
PART = 2 * WIDTH
RELATIVE = ((0, 0, PART), (3, 0, PART), (1, 0, PART), (2, 0, PART // 2), (2, PART // 2, PART))
STACKED = (0, 3, 1, 2)
LOG2E = 1.4426950408889634
MIB = 1 << 20


def frequencies(band_edges, half_size):
    dim_index = jnp.arange(half_size, dtype=jnp.float32)
    base_freq = jnp.power(10000.0, -dim_index / half_size)
    lower_edge = band_edges[0].astype(jnp.float32)
    upper_edge = band_edges[1].astype(jnp.float32)
    ramp_share = jnp.clip((dim_index - lower_edge) / (upper_edge - lower_edge), 0.0, 1.0)
    return base_freq * (1.0 - ramp_share) + base_freq * ramp_share / SCALE


def rotary_tables(positions, frequency):
    angles = positions.astype(jnp.float32)[:, None] * frequency
    mscale = 0.1 * math.log(SCALE) + 1.0
    cosine = jnp.cos(angles) * mscale
    sine = jnp.sin(angles) * mscale
    return jnp.concatenate([cosine, cosine], -1), jnp.concatenate([-sine, sine], -1)


def dot(a, b):
    return jnp.dot(a, b, preferred_element_type=jnp.float32)


def dot_t(a, b):
    return lax.dot_general(a, b, (((1,), (1,)), ((), ())), preferred_element_type=jnp.float32)


def slot_of(block, core):
    other = jnp.where(lax.rem(block, 2) == core, 0, 2)
    return other + block // 2


def rotate(heads, cos, sin):
    return heads * cos + pltpu.roll(heads, HEAD // 2, 1) * sin


def softmax_times(scores, keep, values):
    scores = jnp.where(keep, scores, -1e30)
    top = jnp.max(scores, axis=-1, keepdims=True)
    weights = jnp.exp2((scores - top) * (LOG2E / math.sqrt(HEAD)))
    total = jnp.sum(weights, axis=-1, keepdims=True)
    return dot(weights.astype(jnp.bfloat16), values) / total


def norm_kernel(core_ref, x_ref, gain_ref, hid_ref):
    core = core_ref[0]

    def chunk(i, _):
        rows = pl.ds(pl.multiple_of(i * 32, 32), 32)
        x = x_ref[rows, :].astype(jnp.float32)
        inv = lax.rsqrt(jnp.mean(x * x, axis=-1, keepdims=True) + 1e-05)
        hidden = (x * inv * gain_ref[...]).astype(jnp.bfloat16)
        width = D // 4
        for block in range(4):
            lanes = pl.ds(pl.multiple_of(slot_of(block, core) * width, width), width)
            hid_ref[rows, lanes] = hidden[:, block * width : (block + 1) * width]
        return 0

    lax.fori_loop(0, C // 32, chunk, 0)


def normed_slots(core, x, gain):
    vmem = pl.BlockSpec(memory_space=pltpu.VMEM)
    hbm = pl.BlockSpec(memory_space=pltpu.HBM)
    return pl.pallas_call(
        norm_kernel,
        out_shape=jax.ShapeDtypeStruct((C, D), jnp.bfloat16),
        in_specs=[pl.BlockSpec(memory_space=pltpu.SMEM), vmem, vmem],
        out_specs=vmem,
        compiler_params=pltpu.CompilerParams(vmem_limit_bytes=16 * MIB),
        cost_estimate=pl.CostEstimate(flops=4 * C * D, bytes_accessed=4 * C * D, transcendentals=C),
    )(core, x, gain)


def start_copies(place_ref, pieces, sems, w_ref=None, o_ref=None):
    my_x, my_y = place_ref[1], place_ref[2]

    def block_of(part, stacked, ring):
        x, y = (stacked, ring) if part == 0 else (ring, stacked)
        x = lax.rem(my_x + x, 4)
        y = lax.rem(my_y + y, 4)
        return lax.rem(y, 2) * 8 + x * 2 + y // 2

    def move(slot, part, outputs):
        first = (slot * 2 + part) * len(RELATIVE)
        for index, (ring, low, high) in enumerate(RELATIVE):
            src = pieces[first + index]
            if outputs:
                if high < PART:
                    continue
                lanes, target = pl.ds(QKV_PART - low, PART - QKV_PART), None
            else:
                end = min(high, QKV_PART)
                lanes, target = pl.ds(0, end - low), pl.ds(low, end - low)
            for k, stacked in enumerate(STACKED):
                block = block_of(part, stacked, ring)
                if outputs:
                    width = PART - QKV_PART
                    dst = o_ref.at[slot, block, :, :, pl.ds(part * width, width)]
                else:
                    dst = w_ref.at[slot, part, block, :, :, target]
                sem = sems.at[4 + slot if outputs else slot * 2 + part]
                pltpu.make_async_copy(src.at[k, :, :, lanes], dst, sem).start()

    for outputs, ref in ((False, w_ref), (True, o_ref)):
        if ref is not None:
            for part in range(2):
                for slot in range(2):
                    move(slot, part, outputs)


def arrived(ref, sem):
    pltpu.make_async_copy(ref, ref, sem).wait()


def step_weights(w_ref, sems, g):
    part = g // 2
    for p in range(2):

        @pl.when(g == 2 * p)
        def _():
            for slot in range(2):
                arrived(w_ref.at[slot, p], sems.at[slot * 2 + p])

    base = lax.rem(g, 2) * (3 * PAIR)

    def weight(slot, kind):
        lanes = pl.ds(pl.multiple_of(base + kind * PAIR, PAIR), PAIR)
        return w_ref[slot, part, :, :, :, lanes].reshape(D // 2, PAIR)

    return weight


def output_sum(core, att_ref, rows, o_ref, h, total):
    for slot in range(2):
        for j in range(2):
            block = (core if slot == 0 else 1 - core) + 2 * j
            lanes = pl.ds(pl.multiple_of(block * PAIR, PAIR), PAIR)
            weight = o_ref[slot, j * 8 : (j + 1) * 8, h].reshape(PAIR, D // 2)
            total = total + dot(att_ref[rows, lanes], weight)
    return total


def row_kernel(first, place_ref, x_ref, hid_ref, gain_ref, cos_ref, sin_ref, *refs):
    pieces = refs[: 4 * len(RELATIVE)]
    key_ref, value_ref, mid_ref, next_ref = refs[4 * len(RELATIVE) : -4]
    if first:
        mid_ref, next_ref, key_ref, value_ref = refs[4 * len(RELATIVE) : -4]
    w_ref, o_ref, att_ref, sems = refs[-4:]
    core = place_ref[0]
    start_copies(place_ref, pieces, sems, w_ref, o_ref)
    half = D // 2

    def step(g, _):
        weight = step_weights(w_ref, sems, g)

        def projected(kind):
            return dot(hid_ref[:, :half], weight(0, kind)) + dot(hid_ref[:, half:], weight(1, kind))

        q2 = projected(0)
        k2 = projected(1)
        v2 = projected(2).astype(jnp.bfloat16)
        for h in range(2):
            lanes = slice(h * HEAD, (h + 1) * HEAD)
            q = rotate(q2[:, lanes], cos_ref[...], sin_ref[...]).astype(jnp.bfloat16)
            k = rotate(k2[:, lanes], cos_ref[...], sin_ref[...]).astype(jnp.bfloat16)
            v = v2[:, lanes]
            target = pl.ds(pl.multiple_of(g * PAIR + h * HEAD, HEAD), HEAD)
            if first:
                key_ref[:, target] = k
                value_ref[:, target] = v
            else:
                k = jnp.concatenate([key_ref[:, target], k], 0)
                v = jnp.concatenate([value_ref[:, target], v], 0)
            scores = dot_t(q, k)
            row = lax.broadcasted_iota(jnp.int32, scores.shape, 0) + (k.shape[0] - ROWS)
            keep = lax.broadcasted_iota(jnp.int32, scores.shape, 1) <= row
            att_ref[:, target] = softmax_times(scores, keep, v).astype(jnp.bfloat16)
        return 0

    lax.fori_loop(0, STEPS, step, 0)
    for slot in range(2):
        arrived(o_ref.at[slot], sems.at[4 + slot])

    def finish(i, _):
        rows = pl.ds(pl.multiple_of(i * 128, 128), 128)
        halves = []
        squares = jnp.zeros((128, 1), jnp.float32)
        for h in range(2):
            lanes = slice(h * half, (h + 1) * half)
            total = output_sum(core, att_ref, rows, o_ref, h, x_ref[rows, lanes].astype(jnp.float32))
            middle = total.astype(jnp.bfloat16)
            mid_ref[rows, lanes] = middle
            middle = middle.astype(jnp.float32)
            squares = squares + jnp.sum(middle * middle, axis=-1, keepdims=True)
            halves.append(middle)
        inv = lax.rsqrt(squares / D + 1e-05)
        for h in range(2):
            lanes = slice(h * half, (h + 1) * half)
            next_ref[rows, lanes] = (halves[h] * inv * gain_ref[:, lanes]).astype(jnp.bfloat16)
        return 0

    lax.fori_loop(0, ROWS // 128, finish, 0)


def row_layer(place, x, hidden, gain, tables, pieces, kept):
    first = kept is None
    hbm = pl.BlockSpec(memory_space=pltpu.HBM)
    mine = lambda width: pl.BlockSpec((ROWS, width), lambda i: (0 if first else 1, 0), pipeline_mode=pl.Buffered(1))
    whole = lambda rows, width: pl.BlockSpec((rows, width), lambda i: (0, 0), pipeline_mode=pl.Buffered(1))
    state = whole(ROWS, WIDTH)
    wide = whole(ROWS, D)
    shape = lambda width: jax.ShapeDtypeStruct((ROWS, width), jnp.bfloat16)
    return pl.pallas_call(
        functools.partial(row_kernel, first),
        grid=(1,),
        out_shape=[shape(D), shape(D)] + [shape(WIDTH)] * (2 if first else 0),
        in_specs=[pl.BlockSpec(memory_space=pltpu.SMEM), mine(D), mine(D), whole(1, D), mine(HEAD), mine(HEAD)]
        + [hbm] * len(pieces)
        + ([] if first else [state, state]),
        out_specs=[wide, wide] + ([state, state] if first else []),
        scratch_shapes=[
            pltpu.VMEM((2, 2, 16, 2, 32, QKV_PART), jnp.bfloat16),
            pltpu.VMEM((2, 16, 2, 32, D // 2), jnp.bfloat16),
            pltpu.VMEM((ROWS, WIDTH), jnp.bfloat16),
            pltpu.SemaphoreType.DMA((6,)),
        ],
        compiler_params=pltpu.CompilerParams(vmem_limit_bytes=48 * MIB),
        cost_estimate=pl.CostEstimate(
            flops=C * D * 4 * WIDTH + 2 * C * C * WIDTH,
            bytes_accessed=2 * (2 * C * D + 4 * D * WIDTH),
            transcendentals=C * C * HEADS // 2,
        ),
    )(place, x, hidden, gain, *tables, *pieces, *([] if first else kept))


def column_kernel(core_ref, x_ref, cos_ref, sin_ref, own_plane, other_plane, out_ref, w_ref, hid_ref, sems):
    core = core_ref[0]
    half = D // 2
    triple = 3 * PAIR

    for g in range(STEPS):
        lanes = pl.ds(g * triple, triple)
        for slot, plane in enumerate((own_plane, other_plane)):
            for ylo in range(2):
                for yhi in range(2):
                    src = plane.at[:, :, ylo, yhi, :, lanes]
                    dst = w_ref.at[g, slot, ylo, :, yhi]
                    pltpu.make_async_copy(src, dst, sems.at[g]).start()

    def selection(transposed):
        a = lax.broadcasted_iota(jnp.int32, (ROWS, ROWS), 1 if transposed else 0)
        b = lax.broadcasted_iota(jnp.int32, (ROWS, ROWS), 0 if transposed else 1)
        same = (a // N_SEQ == lax.rem(b, COLS)) & (lax.rem(a, N_SEQ) == b // COLS)
        return jnp.where(same, 1.0, 0.0).astype(jnp.bfloat16)

    pick = selection(False)
    width = D // 4
    for block in range(4):
        lanes = pl.ds(pl.multiple_of(slot_of(block, core) * width, width), width)
        moved = dot(pick, x_ref[:, block * width : (block + 1) * width])
        hid_ref[:, lanes] = moved.astype(jnp.bfloat16)

    back = selection(True)
    size = 128
    row = lax.broadcasted_iota(jnp.int32, (size, size), 0)
    col = lax.broadcasted_iota(jnp.int32, (size, size), 1)
    keep = (row // N_SEQ == col // N_SEQ) & (col <= row)

    def step(g, _):
        pltpu.make_async_copy(w_ref.at[g], w_ref.at[g], sems.at[g]).wait()

        def weight(slot, kind):
            lanes = slice(kind * PAIR, (kind + 1) * PAIR)
            return w_ref[g, slot, :, :, :, :, :, lanes].reshape(half, PAIR)

        def projected(kind):
            return dot(hid_ref[:, :half], weight(0, kind)) + dot(hid_ref[:, half:], weight(1, kind))

        q2 = projected(0)
        k2 = projected(1)
        v2 = projected(2).astype(jnp.bfloat16)
        heads = []
        for h in range(2):
            lanes = slice(h * HEAD, (h + 1) * HEAD)
            q = rotate(q2[:, lanes], cos_ref[...], sin_ref[...]).astype(jnp.bfloat16)
            k = rotate(k2[:, lanes], cos_ref[...], sin_ref[...]).astype(jnp.bfloat16)
            v = v2[:, lanes]
            blocks = []
            for b in range(ROWS // size):
                rows = slice(b * size, (b + 1) * size)
                blocks.append(softmax_times(dot_t(q[rows], k[rows]), keep, v[rows]).astype(jnp.bfloat16))
            heads.append(jnp.concatenate(blocks, 0))
        attended = jnp.concatenate(heads, 1)
        lanes = pl.ds(pl.multiple_of(g * PAIR, PAIR), PAIR)
        out_ref[:, lanes] = dot(back, attended).astype(jnp.bfloat16)
        return 0

    lax.fori_loop(0, STEPS, step, 0)


def column_layer(core, x, tables, planes):
    vmem = pl.BlockSpec(memory_space=pltpu.VMEM)
    hbm = pl.BlockSpec(memory_space=pltpu.HBM)
    return pl.pallas_call(
        column_kernel,
        out_shape=jax.ShapeDtypeStruct((ROWS, WIDTH), jnp.bfloat16),
        in_specs=[pl.BlockSpec(memory_space=pltpu.SMEM)] + [vmem] * 3 + [hbm] * 2,
        out_specs=vmem,
        scratch_shapes=[
            pltpu.VMEM((STEPS, 2, 2, 4, 2, 4, 16, 3 * PAIR), jnp.bfloat16),
            pltpu.VMEM((ROWS, D), jnp.bfloat16),
            pltpu.SemaphoreType.DMA((STEPS,)),
        ],
        compiler_params=pltpu.CompilerParams(vmem_limit_bytes=56 * MIB),
        cost_estimate=pl.CostEstimate(
            flops=C * D * 3 * WIDTH + C * C * WIDTH,
            bytes_accessed=2 * (C * D + 3 * D * WIDTH + C * WIDTH),
            transcendentals=C * C * HEADS // 4,
        ),
    )(core, x, *tables, *planes)


def branch_sum(core, att_ref, own_ref, other_ref, resid_ref):
    width = WIDTH // 4
    total = resid_ref[...].astype(jnp.float32)
    for slot in range(4):
        block = jnp.where(slot < 2, core, 1 - core) + 2 * (slot % 2)
        lanes = pl.ds(pl.multiple_of(block * width, width), width)
        ref = own_ref if slot < 2 else other_ref
        rows = slice((slot % 2) * width, (slot % 2 + 1) * width)
        total = total + dot(att_ref[:, lanes], ref[rows, :])
    return total


def final_kernel(core_ref, att_ref, own_ref, other_ref, resid_ref, *refs):
    out_ref = refs[-1]
    out_ref[...] = branch_sum(core_ref[0], att_ref, own_ref, other_ref, resid_ref).astype(jnp.bfloat16)


def output_layer(core, attended, own, other, resid, out):
    size = 128
    second = out is not None
    start = ROWS // size if second else 0
    block = lambda width: pl.BlockSpec((size, width), lambda i: (i, 0))
    whole = lambda shape: pl.BlockSpec(shape, lambda i: (0, 0), pipeline_mode=pl.Buffered(1))
    return pl.pallas_call(
        final_kernel,
        grid=(ROWS // size,),
        out_shape=jax.ShapeDtypeStruct((C, D), jnp.bfloat16),
        in_specs=[
            pl.BlockSpec(memory_space=pltpu.SMEM),
            block(WIDTH),
            whole(own.shape),
            whole(other.shape),
            block(D),
        ]
        + ([pl.BlockSpec(memory_space=pl.ANY)] if second else []),
        out_specs=pl.BlockSpec((size, D), lambda i: (start + i, 0)),
        input_output_aliases={5: 0} if second else {},
        compiler_params=pltpu.CompilerParams(
            dimension_semantics=("arbitrary",), vmem_limit_bytes=54 * MIB
        ),
        cost_estimate=pl.CostEstimate(
            flops=C * D * WIDTH,
            bytes_accessed=2 * (C * D + D * WIDTH + C * WIDTH // 2),
            transcendentals=0,
        ),
    )(core, attended, own, other, resid, *([out] if second else []))


def shift(value, axis, by):
    if axis == "y":
        where = lambda y: (y % 2) * 2 + y // 2
        return lax.ppermute(value, ("ylo", "yhi"), [(where(y), where((y + by) % 4)) for y in range(4)])
    return lax.ppermute(value, axis, [(i, (i + by) % 4) for i in range(4)])


def first_hops(value, axis):
    return [value, shift(value, axis, 1), shift(value, axis, -1)]


def forwards(hops, axis):
    own, left, right = hops
    half = own.shape[-1] // 2
    return hops + [shift(left[..., :half], axis, 1), shift(right[..., half:], axis, -1)]


def stack(pieces):
    own, left, right, low, high = pieces
    return jnp.stack([own, left, right, jnp.concatenate([low, high], -1)])


def swap(value):
    return lax.ppermute(value, "core", [(0, 1), (1, 0)])


def fold_output(output):
    return jnp.concatenate([output[:, : D // 2], output[:, D // 2 :]], 0)


def by_step(inputs):
    return inputs.reshape(-1, 3, STEPS, PAIR).transpose(0, 2, 1, 3).reshape(-1, 3 * WIDTH)


def lines(inputs, output):
    shard = jnp.concatenate([by_step(inputs), fold_output(output)], 1)
    rows = lax.all_gather(shard, "z", axis=0)
    qkv = rows[:, :, : 3 * WIDTH].reshape(2, 32, 3 * WIDTH)
    out = rows[:, :, 3 * WIDTH :].reshape(4, 2, 8, WIDTH).transpose(1, 0, 2, 3).reshape(2, 32, WIDTH)
    parts = []
    for p in range(2):
        lanes = slice(p * QKV_PART, (p + 1) * QKV_PART)
        rest = slice(p * WIDTH // 2, (p + 1) * WIDTH // 2)
        parts.append(jnp.concatenate([qkv[:, :, lanes], out[:, :, rest]], -1))
    return parts


def inner_rings(parts):
    hops = [first_hops(part, axis) for part, axis in zip(parts, "xy")]
    return [stack(forwards(hop, axis)) for hop, axis in zip(hops, "xy")]


def outer_hops(stacks):
    return [first_hops(part, axis) for part, axis in zip(stacks, "yx")]


def outer_forwards(hops):
    return [forwards(hop, axis) for hop, axis in zip(hops, "yx")]


def both_cores(parts):
    own = [piece for part in parts for piece in part]
    return own + [swap(piece) for piece in own]


def column_line(inputs, output):
    shard = jnp.concatenate([by_step(inputs), fold_output(output)], 1)
    return lax.all_gather(jnp.concatenate([shard, shard], 1), ("ylo", "yhi"), axis=0)[:, :, : 4 * WIDTH]


def column_plane(line):
    return lax.all_gather(line, ("x", "z"), axis=0).reshape(4, 4, 2, 2, 16, 4 * WIDTH)


def column_output(plane):
    out = plane[..., 3 * WIDTH :].transpose(2, 0, 3, 1, 4, 5)
    return out.reshape(64, 2, 8, WIDTH).transpose(0, 2, 1, 3).reshape(WIDTH // 2, D)


def shards(tokens, gain_first, inputs_first, output_first, gain_second, inputs_second, output_second, starts, band_edges):
    residual = tokens[0]
    core = lax.axis_index("core").astype(jnp.int32)
    core_scalar = core.reshape(1)
    seq = lax.axis_index(SEQ)
    my_y = lax.axis_index("yhi") * 2 + lax.axis_index("ylo")
    place = jnp.stack([core, lax.axis_index("x").astype(jnp.int32), my_y.astype(jnp.int32)])

    frequency = frequencies(band_edges, HEAD // 2)
    block_starts = starts[0]
    own_start = lax.dynamic_index_in_dim(block_starts, seq, 0, keepdims=False)
    row_tables = rotary_tables(own_start + jnp.arange(C, dtype=jnp.int32), frequency)
    column_tables = []
    for half in range(2):
        columns = half * ROWS + seq.astype(jnp.int32) * COLS + jnp.arange(COLS, dtype=jnp.int32)
        positions = (columns[:, None] + block_starts[None, :]).reshape(ROWS)
        column_tables.append(rotary_tables(positions, frequency))
    hidden = normed_slots(core_scalar, residual, gain_first.reshape(1, D))

    line = column_line(inputs_second, output_second)
    first = inner_rings(lines(inputs_first, output_first))
    first, line = lax.optimization_barrier((first, line))
    plane = column_plane(line)
    hops = outer_hops(first)
    hops, hidden, row_tables, column_tables = lax.optimization_barrier((hops, hidden, row_tables, column_tables))
    pieces = both_cores(outer_forwards(hops))
    gain = gain_second.reshape(1, D)
    exchange = lambda value: lax.all_to_all(value, SEQ, split_axis=0, concat_axis=0, tiled=True)

    middle_a, next_a, *kept = row_layer(place, residual, hidden, gain, row_tables, pieces, None)
    plane, next_a = lax.optimization_barrier((plane, next_a))
    planes = (plane, swap(plane))
    middle_b, next_b = row_layer(place, residual, hidden, gain, row_tables, pieces, kept)
    next_a = exchange(next_a)
    next_b = exchange(next_b)
    attended_a = column_layer(core_scalar, next_a, column_tables[0], planes)
    attended_b = column_layer(core_scalar, next_b, column_tables[1], planes)
    attended_a = exchange(attended_a)
    attended_b = exchange(attended_b)
    output = [column_output(p) for p in planes]
    out = output_layer(core_scalar, attended_a, *output, middle_a, None)
    return output_layer(core_scalar, attended_b, *output, middle_b, out)[None]


def solution(mesh):
    split = Mesh(mesh.devices.reshape(2, 2, 4, 2, 4), ("ylo", "core") + SEQ)
    dp = ("ylo", "core")
    every = dp + SEQ
    return jax.shard_map(
        shards,
        mesh=split,
        in_specs=(
            P(dp, SEQ, None),
            P(),
            P(every, None),
            P(every, None),
            P(),
            P(every, None),
            P(every, None),
            P(dp, None),
            P(),
        ),
        out_specs=P(dp, SEQ, None),
        check_vma=False,
    )
```

```python
import math

import jax
import jax.numpy as jnp
from jax import lax
from jax.experimental import pallas as pl
from jax.experimental.pallas import tpu as pltpu
from jax.sharding import Mesh, PartitionSpec as P

HEADS = 8
HEAD = 128
C = 512
SCALE = 8
D = 2048
WIDTH = HEADS * HEAD
N_SEQ = 32
COLS = C // N_SEQ
PAIR = 2 * HEAD
STEPS = WIDTH // PAIR
SEQ = ("x", "yhi", "z")
QKV_HALF = 3 * WIDTH // 2
PART = 4 * WIDTH
RELATIVE = ((0, 0, PART), (3, 0, PART), (1, 0, PART), (2, 0, PART // 2), (2, PART // 2, PART))
RINGS = (0, 3, 1, 2)
LOG2E = 1.4426950408889634
MIB = 1 << 20


def frequencies(band_edges, half_size):
    dim_index = jnp.arange(half_size, dtype=jnp.float32)
    base_freq = jnp.power(10000.0, -dim_index / half_size)
    lower_edge = band_edges[0].astype(jnp.float32)
    upper_edge = band_edges[1].astype(jnp.float32)
    ramp_share = jnp.clip((dim_index - lower_edge) / (upper_edge - lower_edge), 0.0, 1.0)
    return base_freq * (1.0 - ramp_share) + base_freq * ramp_share / SCALE


def rotary_tables(positions, frequency):
    angles = positions.astype(jnp.float32)[:, None] * frequency
    mscale = 0.1 * math.log(SCALE) + 1.0
    cosine = jnp.cos(angles) * mscale
    sine = jnp.sin(angles) * mscale
    return jnp.concatenate([cosine, cosine], -1), jnp.concatenate([-sine, sine], -1)


def dot(a, b):
    return jnp.dot(a, b, preferred_element_type=jnp.float32)


def dot_t(a, b):
    return lax.dot_general(a, b, (((1,), (1,)), ((), ())), preferred_element_type=jnp.float32)


def slot_of(block, core):
    other = jnp.where(lax.rem(block, 2) == core, 0, 2)
    return other + block // 2


def rotate(heads, cos, sin):
    return heads * cos + pltpu.roll(heads, HEAD // 2, 1) * sin


def softmax_times(scores, keep, values):
    scores = jnp.where(keep, scores, -1e30)
    top = jnp.max(scores, axis=-1, keepdims=True)
    weights = jnp.exp2((scores - top) * (LOG2E / math.sqrt(HEAD)))
    total = jnp.sum(weights, axis=-1, keepdims=True)
    return dot(weights.astype(jnp.bfloat16), values) / total


def norm_kernel(core_ref, x_ref, gain_ref, hid_ref):
    core = core_ref[0]

    def chunk(i, _):
        rows = pl.ds(pl.multiple_of(i * 32, 32), 32)
        x = x_ref[rows, :].astype(jnp.float32)
        inv = lax.rsqrt(jnp.mean(x * x, axis=-1, keepdims=True) + 1e-05)
        hidden = (x * inv * gain_ref[...]).astype(jnp.bfloat16)
        width = D // 4
        for block in range(4):
            lanes = pl.ds(pl.multiple_of(slot_of(block, core) * width, width), width)
            hid_ref[rows, lanes] = hidden[:, block * width : (block + 1) * width]
        return 0

    lax.fori_loop(0, C // 32, chunk, 0)


def normed_slots(core, x, gain):
    vmem = pl.BlockSpec(memory_space=pltpu.VMEM)
    hbm = pl.BlockSpec(memory_space=pltpu.HBM)
    return pl.pallas_call(
        norm_kernel,
        out_shape=jax.ShapeDtypeStruct((C, D), jnp.bfloat16),
        in_specs=[pl.BlockSpec(memory_space=pltpu.SMEM), vmem, vmem],
        out_specs=vmem,
        compiler_params=pltpu.CompilerParams(vmem_limit_bytes=16 * MIB),
        cost_estimate=pl.CostEstimate(flops=4 * C * D, bytes_accessed=4 * C * D, transcendentals=C),
    )(core, x, gain)


def start_copies(place_ref, pieces, sems, w_ref, o_ref):
    my_x, my_y = place_ref[1], place_ref[2]

    def block_of(stacked, ring):
        x = lax.rem(my_x + stacked, 4)
        y = lax.rem(my_y + ring, 4)
        return lax.rem(y, 2) * 8 + x * 2 + y // 2

    def move(slot, first, last, dst_of, sem):
        for index, (ring, low, high) in enumerate(RELATIVE):
            begin, end = max(low, first), min(high, last)
            if begin >= end:
                continue
            src = pieces[slot * len(RELATIVE) + index]
            for k, stacked in enumerate(RINGS):
                dst = dst_of(block_of(stacked, ring)).at[:, :, pl.ds(begin - first, end - begin)]
                pltpu.make_async_copy(src.at[k, :, :, pl.ds(begin - low, end - begin)], dst, sem).start()

    for group in range(2):
        for slot in range(2):
            move(
                slot,
                group * QKV_HALF,
                (group + 1) * QKV_HALF,
                lambda block: w_ref.at[slot, group, block],
                sems.at[slot * 2 + group],
            )
    for slot in range(2):
        move(slot, 2 * QKV_HALF, PART, lambda block: o_ref.at[slot, block], sems.at[4 + slot])


def arrived(ref, sem):
    pltpu.make_async_copy(ref, ref, sem).wait()


def step_weights(w_ref, sems, g):
    part = g // 2
    for p in range(2):

        @pl.when(g == 2 * p)
        def _():
            for slot in range(2):
                arrived(w_ref.at[slot, p], sems.at[slot * 2 + p])

    base = lax.rem(g, 2) * (3 * PAIR)

    def weight(slot, kind):
        lanes = pl.ds(pl.multiple_of(base + kind * PAIR, PAIR), PAIR)
        return w_ref[slot, part, :, :, :, lanes].reshape(D // 2, PAIR)

    return weight


def output_sum(core, att_ref, rows, o_ref, h, total):
    for slot in range(2):
        for j in range(2):
            block = (core if slot == 0 else 1 - core) + 2 * j
            lanes = pl.ds(pl.multiple_of(block * PAIR, PAIR), PAIR)
            weight = o_ref[slot, j * 8 : (j + 1) * 8, h].reshape(PAIR, D // 2)
            total = total + dot(att_ref[rows, lanes], weight)
    return total


def row_kernel(place_ref, x_ref, hid_ref, gain_ref, cos_ref, sin_ref, *refs):
    pieces = refs[: 2 * len(RELATIVE)]
    mid_ref, next_ref, w_ref, o_ref, att_ref, sems = refs[2 * len(RELATIVE) :]
    core = place_ref[0]
    start_copies(place_ref, pieces, sems, w_ref, o_ref)
    half = D // 2

    def step(g, _):
        weight = step_weights(w_ref, sems, g)

        def projected(kind):
            return dot(hid_ref[:, :half], weight(0, kind)) + dot(hid_ref[:, half:], weight(1, kind))

        q2 = projected(0)
        k2 = projected(1)
        v2 = projected(2).astype(jnp.bfloat16)
        for h in range(2):
            lanes = slice(h * HEAD, (h + 1) * HEAD)
            q = rotate(q2[:, lanes], cos_ref[...], sin_ref[...]).astype(jnp.bfloat16)
            k = rotate(k2[:, lanes], cos_ref[...], sin_ref[...]).astype(jnp.bfloat16)
            v = v2[:, lanes]
            size = 256
            for b in range(C // size):
                end = (b + 1) * size
                scores = dot_t(q[b * size : end], k[:end])
                row = lax.broadcasted_iota(jnp.int32, scores.shape, 0) + b * size
                keep = lax.broadcasted_iota(jnp.int32, scores.shape, 1) <= row
                target = pl.ds(pl.multiple_of(g * PAIR + h * HEAD, HEAD), HEAD)
                att_ref[b * size : end, target] = softmax_times(scores, keep, v[:end]).astype(jnp.bfloat16)
        return 0

    lax.fori_loop(0, STEPS, step, 0)
    for slot in range(2):
        arrived(o_ref.at[slot], sems.at[4 + slot])

    def finish(i, _):
        rows = pl.ds(pl.multiple_of(i * 128, 128), 128)
        halves = []
        squares = jnp.zeros((128, 1), jnp.float32)
        for h in range(2):
            lanes = slice(h * half, (h + 1) * half)
            total = output_sum(core, att_ref, rows, o_ref, h, x_ref[rows, lanes].astype(jnp.float32))
            middle = total.astype(jnp.bfloat16)
            mid_ref[rows, lanes] = middle
            middle = middle.astype(jnp.float32)
            squares = squares + jnp.sum(middle * middle, axis=-1, keepdims=True)
            halves.append(middle)
        inv = lax.rsqrt(squares / D + 1e-05)
        for h in range(2):
            lanes = slice(h * half, (h + 1) * half)
            next_ref[rows, lanes] = (halves[h] * inv * gain_ref[:, lanes]).astype(jnp.bfloat16)
        return 0

    lax.fori_loop(0, C // 128, finish, 0)


def row_layer(place, x, hidden, gain, tables, pieces):
    vmem = pl.BlockSpec(memory_space=pltpu.VMEM)
    hbm = pl.BlockSpec(memory_space=pltpu.HBM)
    shape = jax.ShapeDtypeStruct((C, D), jnp.bfloat16)
    return pl.pallas_call(
        row_kernel,
        out_shape=[shape, shape],
        in_specs=[pl.BlockSpec(memory_space=pltpu.SMEM)]
        + [vmem] * 5
        + [hbm] * len(pieces),
        out_specs=[vmem, vmem],
        scratch_shapes=[
            pltpu.VMEM((2, 2, 16, 2, 32, QKV_HALF), jnp.bfloat16),
            pltpu.VMEM((2, 16, 2, 32, D // 2), jnp.bfloat16),
            pltpu.VMEM((C, WIDTH), jnp.bfloat16),
            pltpu.SemaphoreType.DMA((6,)),
        ],
        compiler_params=pltpu.CompilerParams(vmem_limit_bytes=48 * MIB),
        cost_estimate=pl.CostEstimate(
            flops=2 * C * D * 4 * WIDTH + 4 * C * C * WIDTH,
            bytes_accessed=2 * (4 * C * D + 4 * D * WIDTH),
            transcendentals=C * C * HEADS,
        ),
    )(place, x, hidden, gain, *tables, *pieces)


def column_kernel(core_ref, x_ref, cos_ref, sin_ref, own_plane, other_plane, out_ref, w_ref, hid_ref, sems):
    core = core_ref[0]
    half = D // 2
    triple = 3 * PAIR

    for g in range(STEPS):
        lanes = pl.ds(g * triple, triple)
        for slot, plane in enumerate((own_plane, other_plane)):
            for ylo in range(2):
                for yhi in range(2):
                    src = plane.at[:, :, ylo, yhi, :, lanes]
                    dst = w_ref.at[g, slot, ylo, :, yhi]
                    pltpu.make_async_copy(src, dst, sems.at[g]).start()

    def selection(transposed):
        a = lax.broadcasted_iota(jnp.int32, (C, C), 1 if transposed else 0)
        b = lax.broadcasted_iota(jnp.int32, (C, C), 0 if transposed else 1)
        same = (a // N_SEQ == lax.rem(b, COLS)) & (lax.rem(a, N_SEQ) == b // COLS)
        return jnp.where(same, 1.0, 0.0).astype(jnp.bfloat16)

    pick = selection(False)
    width = D // 4
    for block in range(4):
        lanes = pl.ds(pl.multiple_of(slot_of(block, core) * width, width), width)
        moved = dot(pick, x_ref[:, block * width : (block + 1) * width])
        hid_ref[:, lanes] = moved.astype(jnp.bfloat16)

    back = selection(True)
    size = 128
    row = lax.broadcasted_iota(jnp.int32, (size, size), 0)
    col = lax.broadcasted_iota(jnp.int32, (size, size), 1)
    keep = (row // N_SEQ == col // N_SEQ) & (col <= row)

    def step(g, _):
        pltpu.make_async_copy(w_ref.at[g], w_ref.at[g], sems.at[g]).wait()

        def weight(slot, kind):
            lanes = slice(kind * PAIR, (kind + 1) * PAIR)
            return w_ref[g, slot, :, :, :, :, :, lanes].reshape(half, PAIR)

        def projected(kind):
            return dot(hid_ref[:, :half], weight(0, kind)) + dot(hid_ref[:, half:], weight(1, kind))

        q2 = projected(0)
        k2 = projected(1)
        v2 = projected(2).astype(jnp.bfloat16)
        heads = []
        for h in range(2):
            lanes = slice(h * HEAD, (h + 1) * HEAD)
            q = rotate(q2[:, lanes], cos_ref[...], sin_ref[...]).astype(jnp.bfloat16)
            k = rotate(k2[:, lanes], cos_ref[...], sin_ref[...]).astype(jnp.bfloat16)
            v = v2[:, lanes]
            blocks = []
            for b in range(C // size):
                rows = slice(b * size, (b + 1) * size)
                blocks.append(softmax_times(dot_t(q[rows], k[rows]), keep, v[rows]).astype(jnp.bfloat16))
            heads.append(jnp.concatenate(blocks, 0))
        attended = jnp.concatenate(heads, 1)
        lanes = pl.ds(pl.multiple_of(g * PAIR, PAIR), PAIR)
        out_ref[:, lanes] = dot(back, attended).astype(jnp.bfloat16)
        return 0

    lax.fori_loop(0, STEPS, step, 0)


def column_layer(core, x, tables, planes):
    vmem = pl.BlockSpec(memory_space=pltpu.VMEM)
    hbm = pl.BlockSpec(memory_space=pltpu.HBM)
    return pl.pallas_call(
        column_kernel,
        out_shape=jax.ShapeDtypeStruct((C, WIDTH), jnp.bfloat16),
        in_specs=[pl.BlockSpec(memory_space=pltpu.SMEM)] + [vmem] * 3 + [hbm] * 2,
        out_specs=vmem,
        scratch_shapes=[
            pltpu.VMEM((STEPS, 2, 2, 4, 2, 4, 16, 3 * PAIR), jnp.bfloat16),
            pltpu.VMEM((C, D), jnp.bfloat16),
            pltpu.SemaphoreType.DMA((STEPS,)),
        ],
        compiler_params=pltpu.CompilerParams(vmem_limit_bytes=56 * MIB),
        cost_estimate=pl.CostEstimate(
            flops=2 * C * D * 3 * WIDTH + 4 * C * C * WIDTH,
            bytes_accessed=2 * (C * D + 3 * D * WIDTH + C * WIDTH),
            transcendentals=C * C * HEADS,
        ),
    )(core, x, *tables, *planes)


def branch_sum(core, att_ref, own_ref, other_ref, resid_ref):
    width = WIDTH // 4
    total = resid_ref[...].astype(jnp.float32)
    for slot in range(4):
        block = jnp.where(slot < 2, core, 1 - core) + 2 * (slot % 2)
        lanes = pl.ds(pl.multiple_of(block * width, width), width)
        ref = own_ref if slot < 2 else other_ref
        rows = slice((slot % 2) * width, (slot % 2 + 1) * width)
        total = total + dot(att_ref[:, lanes], ref[rows, :])
    return total


def final_kernel(core_ref, att_ref, own_ref, other_ref, resid_ref, out_ref):
    out_ref[...] = branch_sum(core_ref[0], att_ref, own_ref, other_ref, resid_ref).astype(jnp.bfloat16)


def output_layer(core, attended, own, other, resid):
    size = 128
    block = lambda width: pl.BlockSpec((size, width), lambda i: (i, 0))
    whole = lambda shape: pl.BlockSpec(shape, lambda i: (0, 0), pipeline_mode=pl.Buffered(1))
    return pl.pallas_call(
        final_kernel,
        grid=(C // size,),
        out_shape=jax.ShapeDtypeStruct((C, D), jnp.bfloat16),
        in_specs=[
            pl.BlockSpec(memory_space=pltpu.SMEM),
            block(WIDTH),
            whole(own.shape),
            whole(other.shape),
            block(D),
        ],
        out_specs=block(D),
        compiler_params=pltpu.CompilerParams(
            dimension_semantics=("arbitrary",), vmem_limit_bytes=40 * MIB
        ),
        cost_estimate=pl.CostEstimate(
            flops=2 * C * D * WIDTH,
            bytes_accessed=2 * (2 * C * D + D * WIDTH + C * WIDTH),
            transcendentals=0,
        ),
    )(core, attended, own, other, resid)


def shift(value, axis, by):
    if axis == "y":
        where = lambda y: (y % 2) * 2 + y // 2
        return lax.ppermute(value, ("ylo", "yhi"), [(where(y), where((y + by) % 4)) for y in range(4)])
    return lax.ppermute(value, axis, [(i, (i + by) % 4) for i in range(4)])


def first_hops(value, axis):
    return [value, shift(value, axis, 1), shift(value, axis, -1)]


def forwards(hops, axis):
    own, left, right = hops
    half = own.shape[-1] // 2
    return hops + [shift(left[..., :half], axis, 1), shift(right[..., half:], axis, -1)]


def stack(pieces):
    own, left, right, low, high = pieces
    return jnp.stack([own, left, right, jnp.concatenate([low, high], -1)])


def swap(value):
    return lax.ppermute(value, "core", [(0, 1), (1, 0)])


def fold_output(output):
    return jnp.concatenate([output[:, : D // 2], output[:, D // 2 :]], 0)


def by_step(inputs):
    return inputs.reshape(-1, 3, STEPS, PAIR).transpose(0, 2, 1, 3).reshape(-1, 3 * WIDTH)


def row_stack(inputs, output):
    shard = jnp.concatenate([by_step(inputs), fold_output(output)], 1)
    rows = lax.all_gather(shard, "z", axis=0)
    qkv = rows[:, :, : 3 * WIDTH].reshape(2, 32, 3 * WIDTH)
    out = rows[:, :, 3 * WIDTH :].reshape(4, 2, 8, WIDTH).transpose(1, 0, 2, 3).reshape(2, 32, WIDTH)
    return stack(forwards(first_hops(jnp.concatenate([qkv, out], -1), "x"), "x"))


def column_line(inputs, output):
    shard = jnp.concatenate([by_step(inputs), fold_output(output)], 1)
    return lax.all_gather(shard, ("ylo", "yhi"), axis=0)


def column_plane(line):
    return lax.all_gather(line, ("x", "z"), axis=0).reshape(4, 4, 2, 2, 16, 4 * WIDTH)


def column_output(plane):
    out = plane[..., 3 * WIDTH :].transpose(2, 0, 3, 1, 4, 5)
    return out.reshape(64, 2, 8, WIDTH).transpose(0, 2, 1, 3).reshape(WIDTH // 2, D)


def shards(tokens, gain_first, inputs_first, output_first, gain_second, inputs_second, output_second, starts, band_edges):
    residual = tokens[0]
    core = lax.axis_index("core").astype(jnp.int32)
    core_scalar = core.reshape(1)
    seq = lax.axis_index(SEQ)
    my_y = lax.axis_index("yhi") * 2 + lax.axis_index("ylo")
    place = jnp.stack([core, lax.axis_index("x").astype(jnp.int32), my_y.astype(jnp.int32)])

    frequency = frequencies(band_edges, HEAD // 2)
    block_starts = starts[0]
    own_start = lax.dynamic_index_in_dim(block_starts, seq, 0, keepdims=False)
    row_tables = rotary_tables(own_start + jnp.arange(C, dtype=jnp.int32), frequency)
    columns = seq.astype(jnp.int32) * COLS + jnp.arange(COLS, dtype=jnp.int32)
    column_positions = (columns[:, None] + block_starts[None, :]).reshape(C)
    column_tables = rotary_tables(column_positions, frequency)

    hidden = normed_slots(core_scalar, residual, gain_first.reshape(1, D))

    line = column_line(inputs_second, output_second)
    inputs_first, output_first, line = lax.optimization_barrier((inputs_first, output_first, line))
    plane = column_plane(line)
    own_stack = row_stack(inputs_first, output_first)
    pieces = forwards(first_hops(own_stack, "y"), "y")
    own_stack, hidden, row_tables, column_tables = lax.optimization_barrier(
        (own_stack, hidden, row_tables, column_tables)
    )
    pieces = pieces + [swap(own_stack)] + [swap(piece) for piece in pieces[1:]]

    middle, hidden = row_layer(place, residual, hidden, gain_second.reshape(1, D), row_tables, pieces)
    plane, hidden = lax.optimization_barrier((plane, hidden))
    planes = (plane, swap(plane))
    hidden = lax.all_to_all(hidden, SEQ, split_axis=0, concat_axis=0, tiled=True)
    attended = column_layer(core_scalar, hidden, column_tables, planes)
    attended = lax.all_to_all(attended, SEQ, split_axis=0, concat_axis=0, tiled=True)
    return output_layer(core_scalar, attended, *[column_output(p) for p in planes], middle)[None]


def solution(mesh):
    split = Mesh(mesh.devices.reshape(2, 2, 4, 2, 4), ("ylo", "core") + SEQ)
    dp = ("ylo", "core")
    every = dp + SEQ
    return jax.shard_map(
        shards,
        mesh=split,
        in_specs=(
            P(dp, SEQ, None),
            P(),
            P(every, None),
            P(every, None),
            P(),
            P(every, None),
            P(every, None),
            P(dp, None),
            P(),
        ),
        out_specs=P(dp, SEQ, None),
        check_vma=False,
    )
```

```python
import math

import jax
import jax.numpy as jnp
from jax import lax
from jax.experimental import pallas as pl
from jax.experimental.pallas import tpu as pltpu
from jax.sharding import Mesh, PartitionSpec as P

HEADS = 8
HEAD = 128
C = 512
SCALE = 8
D = 2048
WIDTH = HEADS * HEAD
N_SEQ = 32
COLS = C // N_SEQ
PAIR = 2 * HEAD
STEPS = WIDTH // PAIR
SEQ = ("x", "yhi", "z")
QKV_HALF = 3 * WIDTH // 2
PIECES = 2 * 5
RINGS = (0, 3, 1, 2)
LOG2E = 1.4426950408889634
MIB = 1 << 20


def frequencies(band_edges, half_size):
    dim_index = jnp.arange(half_size, dtype=jnp.float32)
    base_freq = jnp.power(10000.0, -dim_index / half_size)
    lower_edge = band_edges[0].astype(jnp.float32)
    upper_edge = band_edges[1].astype(jnp.float32)
    ramp_share = jnp.clip((dim_index - lower_edge) / (upper_edge - lower_edge), 0.0, 1.0)
    return base_freq * (1.0 - ramp_share) + base_freq * ramp_share / SCALE


def rotary_tables(positions, frequency):
    angles = positions.astype(jnp.float32)[:, None] * frequency
    mscale = 0.1 * math.log(SCALE) + 1.0
    cosine = jnp.cos(angles) * mscale
    sine = jnp.sin(angles) * mscale
    return jnp.concatenate([cosine, cosine], -1), jnp.concatenate([-sine, sine], -1)


def dot(a, b):
    return jnp.dot(a, b, preferred_element_type=jnp.float32)


def dot_t(a, b):
    return lax.dot_general(a, b, (((1,), (1,)), ((), ())), preferred_element_type=jnp.float32)


def slot_of(block, core):
    other = jnp.where(lax.rem(block, 2) == core, 0, 2)
    return other + block // 2


def rotate(heads, cos, sin):
    return heads * cos + pltpu.roll(heads, HEAD // 2, 1) * sin


def softmax_times(scores, keep, values):
    scores = jnp.where(keep, scores, -1e30)
    top = jnp.max(scores, axis=-1, keepdims=True)
    weights = jnp.exp2((scores - top) * (LOG2E / math.sqrt(HEAD)))
    total = jnp.sum(weights, axis=-1, keepdims=True)
    return dot(weights.astype(jnp.bfloat16), values) / total


def norm_kernel(core_ref, x_ref, gain_ref, hid_ref):
    core = core_ref[0]

    def chunk(i, _):
        rows = pl.ds(pl.multiple_of(i * 32, 32), 32)
        x = x_ref[rows, :].astype(jnp.float32)
        inv = lax.rsqrt(jnp.mean(x * x, axis=-1, keepdims=True) + 1e-05)
        hidden = (x * inv * gain_ref[...]).astype(jnp.bfloat16)
        width = D // 4
        for block in range(4):
            lanes = pl.ds(pl.multiple_of(slot_of(block, core) * width, width), width)
            hid_ref[rows, lanes] = hidden[:, block * width : (block + 1) * width]
        return 0

    lax.fori_loop(0, C // 32, chunk, 0)


def normed_slots(core, x, gain):
    vmem = pl.BlockSpec(memory_space=pltpu.VMEM)
    hbm = pl.BlockSpec(memory_space=pltpu.HBM)
    return pl.pallas_call(
        norm_kernel,
        out_shape=jax.ShapeDtypeStruct((C, D), jnp.bfloat16),
        in_specs=[pl.BlockSpec(memory_space=pltpu.SMEM), vmem, vmem],
        out_specs=vmem,
        compiler_params=pltpu.CompilerParams(vmem_limit_bytes=16 * MIB),
        cost_estimate=pl.CostEstimate(flops=4 * C * D, bytes_accessed=4 * C * D, transcendentals=C),
    )(core, x, gain)


def start_copies(place_ref, pieces, width, targets):
    my_x, my_y = place_ref[1], place_ref[2]
    held = (
        (0, 0, width),
        (3, 0, width),
        (1, 0, width),
        (2, 0, width // 2),
        (2, width // 2, width),
    )
    for slot, first, last, ref, sem in targets:
        for index, (ring, low, high) in enumerate(held):
            begin, end = max(low, first), min(high, last)
            if begin >= end:
                continue
            src = pieces[slot * len(held) + index]
            for k, stacked in enumerate(RINGS):
                x = lax.rem(my_x + stacked, 4)
                y = lax.rem(my_y + ring, 4)
                block = lax.rem(y, 2) * 8 + x * 2 + y // 2
                dst = ref.at[block, :, :, pl.ds(begin - first, end - begin)]
                pltpu.make_async_copy(src.at[k, :, :, pl.ds(begin - low, end - begin)], dst, sem).start()


def arrived(ref, sem):
    pltpu.make_async_copy(ref, ref, sem).wait()


def step_weights(w_ref, sems, g):
    part = g // 2
    for p in range(2):

        @pl.when(g == 2 * p)
        def _():
            for slot in range(2):
                arrived(w_ref.at[slot, p], sems.at[slot * 2 + p])

    base = lax.rem(g, 2) * (3 * PAIR)

    def weight(slot, kind):
        lanes = pl.ds(pl.multiple_of(base + kind * PAIR, PAIR), PAIR)
        return w_ref[slot, part, :, :, :, lanes].reshape(D // 2, PAIR)

    return weight


def output_sum(core, att_ref, rows, o_ref, h, total):
    for slot in range(2):
        for j in range(2):
            block = (core if slot == 0 else 1 - core) + 2 * j
            lanes = pl.ds(pl.multiple_of(block * PAIR, PAIR), PAIR)
            weight = o_ref[slot, j * 8 : (j + 1) * 8, h].reshape(PAIR, D // 2)
            total = total + dot(att_ref[rows, lanes], weight)
    return total


def row_kernel(hid_ref, cos_ref, sin_ref, own_plane, other_plane, out_ref, w_ref, sems):
    half = D // 2
    triple = 3 * PAIR
    for g in range(STEPS):
        lanes = pl.ds(g * triple, triple)
        for slot, plane in enumerate((own_plane, other_plane)):
            for ylo in range(2):
                for yhi in range(2):
                    src = plane.at[:, :, ylo, yhi, :, lanes]
                    dst = w_ref.at[g, slot, ylo, :, yhi]
                    pltpu.make_async_copy(src, dst, sems.at[g]).start()

    def step(g, _):
        arrived(w_ref.at[g], sems.at[g])

        def weight(slot, kind):
            lanes = slice(kind * PAIR, (kind + 1) * PAIR)
            return w_ref[g, slot, :, :, :, :, :, lanes].reshape(half, PAIR)

        def projected(kind):
            return dot(hid_ref[:, :half], weight(0, kind)) + dot(hid_ref[:, half:], weight(1, kind))

        q2 = projected(0)
        k2 = projected(1)
        v2 = projected(2).astype(jnp.bfloat16)
        for h in range(2):
            lanes = slice(h * HEAD, (h + 1) * HEAD)
            q = rotate(q2[:, lanes], cos_ref[...], sin_ref[...]).astype(jnp.bfloat16)
            k = rotate(k2[:, lanes], cos_ref[...], sin_ref[...]).astype(jnp.bfloat16)
            v = v2[:, lanes]
            size = 256
            for b in range(C // size):
                end = (b + 1) * size
                scores = dot_t(q[b * size : end], k[:end])
                row = lax.broadcasted_iota(jnp.int32, scores.shape, 0) + b * size
                keep = lax.broadcasted_iota(jnp.int32, scores.shape, 1) <= row
                target = pl.ds(pl.multiple_of(g * PAIR + h * HEAD, HEAD), HEAD)
                out_ref[b * size : end, target] = softmax_times(scores, keep, v[:end]).astype(jnp.bfloat16)
        return 0

    lax.fori_loop(0, STEPS, step, 0)


def row_layer(hidden, tables, planes):
    vmem = pl.BlockSpec(memory_space=pltpu.VMEM)
    hbm = pl.BlockSpec(memory_space=pltpu.HBM)
    return pl.pallas_call(
        row_kernel,
        out_shape=jax.ShapeDtypeStruct((C, WIDTH), jnp.bfloat16),
        in_specs=[vmem] * 3 + [hbm] * 2,
        out_specs=vmem,
        scratch_shapes=[
            pltpu.VMEM((STEPS, 2, 2, 4, 2, 4, 16, 3 * PAIR), jnp.bfloat16),
            pltpu.SemaphoreType.DMA((STEPS,)),
        ],
        compiler_params=pltpu.CompilerParams(vmem_limit_bytes=56 * MIB),
        cost_estimate=pl.CostEstimate(
            flops=2 * C * D * 3 * WIDTH + 4 * C * C * WIDTH,
            bytes_accessed=2 * (C * D + 3 * D * WIDTH + C * WIDTH),
            transcendentals=C * C * HEADS,
        ),
    )(hidden, *tables, *planes)


def middle_kernel(place_ref, att_ref, x_ref, gain_ref, *refs):
    pieces = refs[: PIECES]
    mid_ref, next_ref, o_ref, sems = refs[PIECES :]
    core = place_ref[0]
    half = D // 2
    targets = [(slot, WIDTH, 2 * WIDTH, o_ref.at[slot], sems.at[slot]) for slot in range(2)]
    start_copies(place_ref, pieces, 2 * WIDTH, targets)
    for slot in range(2):
        arrived(o_ref.at[slot], sems.at[slot])

    def finish(i, _):
        rows = pl.ds(pl.multiple_of(i * 128, 128), 128)
        halves = []
        squares = jnp.zeros((128, 1), jnp.float32)
        for h in range(2):
            lanes = slice(h * half, (h + 1) * half)
            total = output_sum(core, att_ref, rows, o_ref, h, x_ref[rows, lanes].astype(jnp.float32))
            middle = total.astype(jnp.bfloat16)
            mid_ref[rows, lanes] = middle
            middle = middle.astype(jnp.float32)
            squares = squares + jnp.sum(middle * middle, axis=-1, keepdims=True)
            halves.append(middle)
        inv = lax.rsqrt(squares / D + 1e-05)
        for h in range(2):
            lanes = slice(h * half, (h + 1) * half)
            next_ref[rows, lanes] = (halves[h] * inv * gain_ref[:, lanes]).astype(jnp.bfloat16)
        return 0

    lax.fori_loop(0, C // 128, finish, 0)


def middle_layer(place, attended, x, gain, pieces):
    vmem = pl.BlockSpec(memory_space=pltpu.VMEM)
    hbm = pl.BlockSpec(memory_space=pltpu.HBM)
    shape = jax.ShapeDtypeStruct((C, D), jnp.bfloat16)
    return pl.pallas_call(
        middle_kernel,
        out_shape=[shape, shape],
        in_specs=[pl.BlockSpec(memory_space=pltpu.SMEM)] + [vmem] * 3 + [hbm] * len(pieces),
        out_specs=[vmem, vmem],
        scratch_shapes=[
            pltpu.VMEM((2, 16, 2, 32, D // 2), jnp.bfloat16),
            pltpu.SemaphoreType.DMA((2,)),
        ],
        compiler_params=pltpu.CompilerParams(vmem_limit_bytes=54 * MIB),
        cost_estimate=pl.CostEstimate(
            flops=2 * C * D * WIDTH,
            bytes_accessed=2 * (3 * C * D + D * WIDTH + C * WIDTH),
            transcendentals=0,
        ),
    )(place, attended, x, gain, *pieces)


def column_kernel(place_ref, x_ref, cos_ref, sin_ref, *refs):
    pieces = refs[: PIECES]
    out_ref, w_ref, hid_ref, sems = refs[PIECES :]
    core = place_ref[0]
    half = D // 2
    targets = [
        (slot, group * QKV_HALF, (group + 1) * QKV_HALF, w_ref.at[slot, group], sems.at[slot * 2 + group])
        for group in range(2)
        for slot in range(2)
    ]
    start_copies(place_ref, pieces, 3 * WIDTH, targets)

    def selection(transposed):
        a = lax.broadcasted_iota(jnp.int32, (C, C), 1 if transposed else 0)
        b = lax.broadcasted_iota(jnp.int32, (C, C), 0 if transposed else 1)
        same = (a // N_SEQ == lax.rem(b, COLS)) & (lax.rem(a, N_SEQ) == b // COLS)
        return jnp.where(same, 1.0, 0.0).astype(jnp.bfloat16)

    pick = selection(False)
    width = D // 4
    for block in range(4):
        lanes = pl.ds(pl.multiple_of(slot_of(block, core) * width, width), width)
        moved = dot(pick, x_ref[:, block * width : (block + 1) * width])
        hid_ref[:, lanes] = moved.astype(jnp.bfloat16)

    back = selection(True)
    size = 128
    row = lax.broadcasted_iota(jnp.int32, (size, size), 0)
    col = lax.broadcasted_iota(jnp.int32, (size, size), 1)
    keep = (row // N_SEQ == col // N_SEQ) & (col <= row)

    def step(g, _):
        weight = step_weights(w_ref, sems, g)

        def projected(kind):
            return dot(hid_ref[:, :half], weight(0, kind)) + dot(hid_ref[:, half:], weight(1, kind))

        q2 = projected(0)
        k2 = projected(1)
        v2 = projected(2).astype(jnp.bfloat16)
        heads = []
        for h in range(2):
            lanes = slice(h * HEAD, (h + 1) * HEAD)
            q = rotate(q2[:, lanes], cos_ref[...], sin_ref[...]).astype(jnp.bfloat16)
            k = rotate(k2[:, lanes], cos_ref[...], sin_ref[...]).astype(jnp.bfloat16)
            v = v2[:, lanes]
            blocks = []
            for b in range(C // size):
                rows = slice(b * size, (b + 1) * size)
                blocks.append(softmax_times(dot_t(q[rows], k[rows]), keep, v[rows]).astype(jnp.bfloat16))
            heads.append(jnp.concatenate(blocks, 0))
        attended = jnp.concatenate(heads, 1)
        lanes = pl.ds(pl.multiple_of(g * PAIR, PAIR), PAIR)
        out_ref[:, lanes] = dot(back, attended).astype(jnp.bfloat16)
        return 0

    lax.fori_loop(0, STEPS, step, 0)


def column_layer(place, x, tables, pieces):
    vmem = pl.BlockSpec(memory_space=pltpu.VMEM)
    hbm = pl.BlockSpec(memory_space=pltpu.HBM)
    return pl.pallas_call(
        column_kernel,
        out_shape=jax.ShapeDtypeStruct((C, WIDTH), jnp.bfloat16),
        in_specs=[pl.BlockSpec(memory_space=pltpu.SMEM)] + [vmem] * 3 + [hbm] * len(pieces),
        out_specs=vmem,
        scratch_shapes=[
            pltpu.VMEM((2, 2, 16, 2, 32, QKV_HALF), jnp.bfloat16),
            pltpu.VMEM((C, D), jnp.bfloat16),
            pltpu.SemaphoreType.DMA((4,)),
        ],
        compiler_params=pltpu.CompilerParams(vmem_limit_bytes=56 * MIB),
        cost_estimate=pl.CostEstimate(
            flops=2 * C * D * 3 * WIDTH + 4 * C * C * WIDTH,
            bytes_accessed=2 * (C * D + 3 * D * WIDTH + C * WIDTH),
            transcendentals=C * C * HEADS,
        ),
    )(place, x, *tables, *pieces)


def final_kernel(place_ref, att_ref, x_ref, *refs):
    pieces = refs[: PIECES]
    out_ref, o_ref, sems = refs[PIECES :]
    core = place_ref[0]
    half = D // 2

    @pl.when(pl.program_id(0) == 0)
    def _():
        targets = [(slot, 0, WIDTH, o_ref.at[slot], sems.at[slot]) for slot in range(2)]
        start_copies(place_ref, pieces, 2 * WIDTH, targets)
        for slot in range(2):
            arrived(o_ref.at[slot], sems.at[slot])

    for h in range(2):
        lanes = slice(h * half, (h + 1) * half)
        total = x_ref[:, lanes].astype(jnp.float32)
        out_ref[:, lanes] = output_sum(core, att_ref, slice(None), o_ref, h, total).astype(jnp.bfloat16)


def final_layer(place, attended, x, pieces):
    size = 128
    block = lambda width: pl.BlockSpec((size, width), lambda i: (i, 0))
    hbm = pl.BlockSpec(memory_space=pltpu.HBM)
    return pl.pallas_call(
        final_kernel,
        grid=(C // size,),
        out_shape=jax.ShapeDtypeStruct((C, D), jnp.bfloat16),
        in_specs=[pl.BlockSpec(memory_space=pltpu.SMEM), block(WIDTH), block(D)] + [hbm] * len(pieces),
        out_specs=block(D),
        scratch_shapes=[
            pltpu.VMEM((2, 16, 2, 32, D // 2), jnp.bfloat16),
            pltpu.SemaphoreType.DMA((2,)),
        ],
        compiler_params=pltpu.CompilerParams(
            dimension_semantics=("arbitrary",), vmem_limit_bytes=54 * MIB
        ),
        cost_estimate=pl.CostEstimate(
            flops=2 * C * D * WIDTH,
            bytes_accessed=2 * (2 * C * D + D * WIDTH + C * WIDTH),
            transcendentals=0,
        ),
    )(place, attended, x, *pieces)


def shift(value, axis, by):
    if axis == "y":
        where = lambda y: (y % 2) * 2 + y // 2
        return lax.ppermute(value, ("ylo", "yhi"), [(where(y), where((y + by) % 4)) for y in range(4)])
    return lax.ppermute(value, axis, [(i, (i + by) % 4) for i in range(4)])


def first_hops(value, axis):
    return [value, shift(value, axis, 1), shift(value, axis, -1)]


def forwards(hops, axis):
    own, left, right = hops
    half = own.shape[-1] // 2
    return hops + [shift(left[..., :half], axis, 1), shift(right[..., half:], axis, -1)]


def stack(pieces):
    own, left, right, low, high = pieces
    return jnp.stack([own, left, right, jnp.concatenate([low, high], -1)])


def swap(value):
    return lax.ppermute(value, "core", [(0, 1), (1, 0)])


def fold_output(output):
    return jnp.concatenate([output[:, : D // 2], output[:, D // 2 :]], 0)


def by_step(inputs):
    return inputs.reshape(-1, 3, STEPS, PAIR).transpose(0, 2, 1, 3).reshape(-1, 3 * WIDTH)


def line_stack(inputs, *outputs):
    shard = jnp.concatenate([by_step(inputs)] + [fold_output(output) for output in outputs], 1)
    rows = lax.all_gather(shard, "z", axis=0)
    qkv = rows[:, :, : 3 * WIDTH].reshape(2, 32, 3 * WIDTH)
    outs = rows[:, :, 3 * WIDTH :].reshape(4, 2, 8, len(outputs) * WIDTH).transpose(1, 0, 2, 3)
    outs = outs.reshape(2, 32, len(outputs) * WIDTH)
    return stack(forwards(first_hops(jnp.concatenate([qkv, outs], -1), "x"), "x"))


def row_plane(inputs):
    line = lax.all_gather(by_step(inputs), ("ylo", "yhi"), axis=0)
    return line, lax.all_gather(line, ("x", "z"), axis=0).reshape(4, 4, 2, 2, 16, 3 * WIDTH)


def shards(tokens, gain_first, inputs_first, output_first, gain_second, inputs_second, output_second, starts, band_edges):
    residual = tokens[0]
    core = lax.axis_index("core").astype(jnp.int32)
    core_scalar = core.reshape(1)
    seq = lax.axis_index(SEQ)
    my_y = lax.axis_index("yhi") * 2 + lax.axis_index("ylo")
    place = jnp.stack([core, lax.axis_index("x").astype(jnp.int32), my_y.astype(jnp.int32)])

    frequency = frequencies(band_edges, HEAD // 2)
    block_starts = starts[0]
    own_start = lax.dynamic_index_in_dim(block_starts, seq, 0, keepdims=False)
    row_tables = rotary_tables(own_start + jnp.arange(C, dtype=jnp.int32), frequency)
    columns = seq.astype(jnp.int32) * COLS + jnp.arange(COLS, dtype=jnp.int32)
    column_positions = (columns[:, None] + block_starts[None, :]).reshape(C)
    column_tables = rotary_tables(column_positions, frequency)

    hidden = normed_slots(core_scalar, residual, gain_first.reshape(1, D))

    line, plane = row_plane(inputs_first)
    output_first, output_second, inputs_second, line = lax.optimization_barrier(
        (output_first, output_second, inputs_second, line)
    )
    gathered = line_stack(inputs_second, output_second, output_first)
    second, small = gathered[..., : 3 * WIDTH], gathered[..., 3 * WIDTH :]
    small_hop = first_hops(small, "y")
    plane, hidden, row_tables, column_tables, _ = lax.optimization_barrier(
        (plane, hidden, row_tables, column_tables, small_hop)
    )
    planes = (plane, swap(plane))
    small = forwards(small_hop, "y")
    small = small + [swap(piece) for piece in small]
    second, small = lax.optimization_barrier((second, small))
    second_hop = first_hops(second, "y")

    attended = row_layer(hidden, row_tables, planes)
    middle, hidden = middle_layer(place, attended, residual, gain_second.reshape(1, D), small)
    second_hop, _ = lax.optimization_barrier((second_hop, hidden))
    pieces = forwards(second_hop, "y")
    pieces = pieces + [swap(piece) for piece in pieces]
    hidden = lax.all_to_all(hidden, SEQ, split_axis=0, concat_axis=0, tiled=True)
    attended = column_layer(place, hidden, column_tables, pieces)
    attended = lax.all_to_all(attended, SEQ, split_axis=0, concat_axis=0, tiled=True)
    return final_layer(place, attended, middle, small)[None]


def solution(mesh):
    split = Mesh(mesh.devices.reshape(2, 2, 4, 2, 4), ("ylo", "core") + SEQ)
    dp = ("ylo", "core")
    every = dp + SEQ
    return jax.shard_map(
        shards,
        mesh=split,
        in_specs=(
            P(dp, SEQ, None),
            P(),
            P(every, None),
            P(every, None),
            P(),
            P(every, None),
            P(every, None),
            P(dp, None),
            P(),
        ),
        out_specs=P(dp, SEQ, None),
        check_vma=False,
    )
```

```python
import math

import jax
import jax.numpy as jnp
from jax import lax
from jax.experimental import pallas as pl
from jax.experimental.pallas import tpu as pltpu
from jax.sharding import Mesh, PartitionSpec as P

HEADS = 8
HEAD = 128
C = 512
SCALE = 8
D = 2048
WIDTH = HEADS * HEAD
N_SEQ = 32
COLS = C // N_SEQ
PAIR = 2 * HEAD
STEPS = WIDTH // PAIR
SEQ = ("x", "yhi", "z")
QKV_PART = 3 * WIDTH // 2
PART = 2 * WIDTH
RELATIVE = ((0, 0, PART), (3, 0, PART), (1, 0, PART), (2, 0, PART // 2), (2, PART // 2, PART))
STACKED = (0, 3, 1, 2)
LOG2E = 1.4426950408889634
MIB = 1 << 20


def frequencies(band_edges, half_size):
    dim_index = jnp.arange(half_size, dtype=jnp.float32)
    base_freq = jnp.power(10000.0, -dim_index / half_size)
    lower_edge = band_edges[0].astype(jnp.float32)
    upper_edge = band_edges[1].astype(jnp.float32)
    ramp_share = jnp.clip((dim_index - lower_edge) / (upper_edge - lower_edge), 0.0, 1.0)
    return base_freq * (1.0 - ramp_share) + base_freq * ramp_share / SCALE


def rotary_tables(positions, frequency):
    angles = positions.astype(jnp.float32)[:, None] * frequency
    mscale = 0.1 * math.log(SCALE) + 1.0
    cosine = jnp.cos(angles) * mscale
    sine = jnp.sin(angles) * mscale
    return jnp.concatenate([cosine, cosine], -1), jnp.concatenate([-sine, sine], -1)


def dot(a, b):
    return jnp.dot(a, b, preferred_element_type=jnp.float32)


def dot_t(a, b):
    return lax.dot_general(a, b, (((1,), (1,)), ((), ())), preferred_element_type=jnp.float32)


def slot_of(block, core):
    other = jnp.where(lax.rem(block, 2) == core, 0, 2)
    return other + block // 2


def rotate(heads, cos, sin):
    return heads * cos + pltpu.roll(heads, HEAD // 2, 1) * sin


def softmax_times(scores, keep, values):
    scores = jnp.where(keep, scores, -1e30)
    top = jnp.max(scores, axis=-1, keepdims=True)
    weights = jnp.exp2((scores - top) * (LOG2E / math.sqrt(HEAD)))
    total = jnp.sum(weights, axis=-1, keepdims=True)
    return dot(weights.astype(jnp.bfloat16), values) / total


def norm_kernel(core_ref, x_ref, gain_ref, hid_ref):
    core = core_ref[0]

    def chunk(i, _):
        rows = pl.ds(pl.multiple_of(i * 32, 32), 32)
        x = x_ref[rows, :].astype(jnp.float32)
        inv = lax.rsqrt(jnp.mean(x * x, axis=-1, keepdims=True) + 1e-05)
        hidden = (x * inv * gain_ref[...]).astype(jnp.bfloat16)
        width = D // 4
        for block in range(4):
            lanes = pl.ds(pl.multiple_of(slot_of(block, core) * width, width), width)
            hid_ref[rows, lanes] = hidden[:, block * width : (block + 1) * width]
        return 0

    lax.fori_loop(0, C // 32, chunk, 0)


def normed_slots(core, x, gain):
    vmem = pl.BlockSpec(memory_space=pltpu.VMEM)
    return pl.pallas_call(
        norm_kernel,
        out_shape=jax.ShapeDtypeStruct((C, D), jnp.bfloat16),
        in_specs=[pl.BlockSpec(memory_space=pltpu.SMEM), vmem, vmem],
        out_specs=vmem,
        compiler_params=pltpu.CompilerParams(vmem_limit_bytes=16 * MIB),
        cost_estimate=pl.CostEstimate(flops=4 * C * D, bytes_accessed=4 * C * D, transcendentals=C),
    )(core, x, gain)


def row_kernel(place_ref, x_ref, hid_ref, gain_ref, cos_ref, sin_ref, *refs):
    pieces = refs[: 4 * len(RELATIVE)]
    mid_ref, next_ref, w_ref, o_ref, att_ref, sems = refs[4 * len(RELATIVE) :]
    core, my_x, my_y = place_ref[0], place_ref[1], place_ref[2]

    def block_of(part, stacked, ring):
        x, y = (stacked, ring) if part == 0 else (ring, stacked)
        x = lax.rem(my_x + x, 4)
        y = lax.rem(my_y + y, 4)
        return lax.rem(y, 2) * 8 + x * 2 + y // 2

    def copies(slot, part, outputs):
        first = (slot * 2 + part) * len(RELATIVE)
        for index, (ring, low, high) in enumerate(RELATIVE):
            src = pieces[first + index]
            if outputs:
                if high < PART:
                    continue
                lanes, target = pl.ds(QKV_PART - low, PART - QKV_PART), None
            else:
                end = min(high, QKV_PART)
                lanes, target = pl.ds(0, end - low), pl.ds(low, end - low)
            for k, stacked in enumerate(STACKED):
                block = block_of(part, stacked, ring)
                if outputs:
                    width = PART - QKV_PART
                    dst = o_ref.at[slot, block, :, :, pl.ds(part * width, width)]
                else:
                    dst = w_ref.at[slot, part, block, :, :, target]
                sem = sems.at[4 + slot if outputs else slot * 2 + part]
                pltpu.make_async_copy(src.at[k, :, :, lanes], dst, sem).start()

    for part in range(2):
        for slot in range(2):
            copies(slot, part, False)
    for part in range(2):
        for slot in range(2):
            copies(slot, part, True)

    def arrived(ref, sem):
        pltpu.make_async_copy(ref, ref, sem).wait()

    half = D // 2

    def step(g, _):
        part = g // 2
        for p in range(2):

            @pl.when(g == 2 * p)
            def _():
                for slot in range(2):
                    arrived(w_ref.at[slot, p], sems.at[slot * 2 + p])

        base = lax.rem(g, 2) * (3 * PAIR)

        def weight(slot, kind):
            lanes = pl.ds(pl.multiple_of(base + kind * PAIR, PAIR), PAIR)
            return w_ref[slot, part, :, :, :, lanes].reshape(half, PAIR)

        def projected(kind):
            return dot(hid_ref[:, :half], weight(0, kind)) + dot(hid_ref[:, half:], weight(1, kind))

        q2 = projected(0)
        k2 = projected(1)
        v2 = projected(2).astype(jnp.bfloat16)
        for h in range(2):
            lanes = slice(h * HEAD, (h + 1) * HEAD)
            q = rotate(q2[:, lanes], cos_ref[...], sin_ref[...]).astype(jnp.bfloat16)
            k = rotate(k2[:, lanes], cos_ref[...], sin_ref[...]).astype(jnp.bfloat16)
            v = v2[:, lanes]
            size = 256
            for b in range(C // size):
                end = (b + 1) * size
                scores = dot_t(q[b * size : end], k[:end])
                row = lax.broadcasted_iota(jnp.int32, scores.shape, 0) + b * size
                keep = lax.broadcasted_iota(jnp.int32, scores.shape, 1) <= row
                att_ref[g, b * size : end, lanes] = softmax_times(scores, keep, v[:end]).astype(jnp.bfloat16)
        return 0

    lax.fori_loop(0, STEPS, step, 0)
    for slot in range(2):
        arrived(o_ref.at[slot], sems.at[4 + slot])

    def finish(i, _):
        rows = pl.ds(pl.multiple_of(i * 128, 128), 128)
        halves = []
        squares = jnp.zeros((128, 1), jnp.float32)
        for h in range(2):
            lanes = slice(h * half, (h + 1) * half)
            total = x_ref[rows, lanes].astype(jnp.float32)
            for slot in range(2):
                for j in range(2):
                    block = (core if slot == 0 else 1 - core) + 2 * j
                    weight = o_ref[slot, j * 8 : (j + 1) * 8, h].reshape(PAIR, half)
                    total = total + dot(att_ref[block, rows, :], weight)
            middle = total.astype(jnp.bfloat16)
            mid_ref[rows, lanes] = middle
            middle = middle.astype(jnp.float32)
            squares = squares + jnp.sum(middle * middle, axis=-1, keepdims=True)
            halves.append(middle)
        inv = lax.rsqrt(squares / D + 1e-05)
        for h in range(2):
            lanes = slice(h * half, (h + 1) * half)
            next_ref[rows, lanes] = (halves[h] * inv * gain_ref[:, lanes]).astype(jnp.bfloat16)
        return 0

    lax.fori_loop(0, C // 128, finish, 0)


def row_layer(place, x, hidden, gain, tables, pieces):
    vmem = pl.BlockSpec(memory_space=pltpu.VMEM)
    shape = jax.ShapeDtypeStruct((C, D), jnp.bfloat16)
    return pl.pallas_call(
        row_kernel,
        out_shape=[shape, shape],
        in_specs=[pl.BlockSpec(memory_space=pltpu.SMEM)]
        + [vmem] * 5
        + [pl.BlockSpec(memory_space=pl.ANY)] * len(pieces),
        out_specs=[vmem, vmem],
        scratch_shapes=[
            pltpu.VMEM((2, 2, 16, 2, 32, QKV_PART), jnp.bfloat16),
            pltpu.VMEM((2, 16, 2, 32, D // 2), jnp.bfloat16),
            pltpu.VMEM((STEPS, C, PAIR), jnp.bfloat16),
            pltpu.SemaphoreType.DMA((6,)),
        ],
        compiler_params=pltpu.CompilerParams(vmem_limit_bytes=48 * MIB),
        cost_estimate=pl.CostEstimate(
            flops=2 * C * D * 4 * WIDTH + 4 * C * C * WIDTH,
            bytes_accessed=2 * (4 * C * D + 4 * D * WIDTH),
            transcendentals=C * C * HEADS,
        ),
    )(place, x, hidden, gain, *tables, *pieces)


def column_kernel(core_ref, x_ref, cos_ref, sin_ref, own_plane, other_plane, out_ref, w_ref, hid_ref, sems):
    core = core_ref[0]
    half = D // 2
    triple = 3 * PAIR

    for g in range(STEPS):
        lanes = pl.ds(g * triple, triple)
        for slot, plane in enumerate((own_plane, other_plane)):
            for ylo in range(2):
                for yhi in range(2):
                    src = plane.at[:, :, ylo, yhi, :, lanes]
                    dst = w_ref.at[g, slot, ylo, :, yhi]
                    pltpu.make_async_copy(src, dst, sems.at[g]).start()

    def selection(transposed):
        a = lax.broadcasted_iota(jnp.int32, (C, C), 1 if transposed else 0)
        b = lax.broadcasted_iota(jnp.int32, (C, C), 0 if transposed else 1)
        same = (a // N_SEQ == lax.rem(b, COLS)) & (lax.rem(a, N_SEQ) == b // COLS)
        return jnp.where(same, 1.0, 0.0).astype(jnp.bfloat16)

    pick = selection(False)
    width = D // 4
    for block in range(4):
        lanes = pl.ds(pl.multiple_of(slot_of(block, core) * width, width), width)
        moved = dot(pick, x_ref[:, block * width : (block + 1) * width])
        hid_ref[:, lanes] = moved.astype(jnp.bfloat16)

    back = selection(True)
    size = 128
    row = lax.broadcasted_iota(jnp.int32, (size, size), 0)
    col = lax.broadcasted_iota(jnp.int32, (size, size), 1)
    keep = (row // N_SEQ == col // N_SEQ) & (col <= row)

    def step(g, _):
        pltpu.make_async_copy(w_ref.at[g], w_ref.at[g], sems.at[g]).wait()

        def weight(slot, kind):
            lanes = slice(kind * PAIR, (kind + 1) * PAIR)
            return w_ref[g, slot, :, :, :, :, :, lanes].reshape(half, PAIR)

        def projected(kind):
            return dot(hid_ref[:, :half], weight(0, kind)) + dot(hid_ref[:, half:], weight(1, kind))

        q2 = projected(0)
        k2 = projected(1)
        v2 = projected(2).astype(jnp.bfloat16)
        heads = []
        for h in range(2):
            lanes = slice(h * HEAD, (h + 1) * HEAD)
            q = rotate(q2[:, lanes], cos_ref[...], sin_ref[...]).astype(jnp.bfloat16)
            k = rotate(k2[:, lanes], cos_ref[...], sin_ref[...]).astype(jnp.bfloat16)
            v = v2[:, lanes]
            blocks = []
            for b in range(C // size):
                rows = slice(b * size, (b + 1) * size)
                blocks.append(softmax_times(dot_t(q[rows], k[rows]), keep, v[rows]).astype(jnp.bfloat16))
            heads.append(jnp.concatenate(blocks, 0))
        attended = jnp.concatenate(heads, 1)
        lanes = pl.ds(pl.multiple_of(g * PAIR, PAIR), PAIR)
        out_ref[:, lanes] = dot(back, attended).astype(jnp.bfloat16)
        return 0

    lax.fori_loop(0, STEPS, step, 0)


def column_layer(core, x, tables, planes):
    vmem = pl.BlockSpec(memory_space=pltpu.VMEM)
    return pl.pallas_call(
        column_kernel,
        out_shape=jax.ShapeDtypeStruct((C, WIDTH), jnp.bfloat16),
        in_specs=[pl.BlockSpec(memory_space=pltpu.SMEM)] + [vmem] * 3 + [pl.BlockSpec(memory_space=pltpu.HBM)] * 2,
        out_specs=vmem,
        scratch_shapes=[
            pltpu.VMEM((STEPS, 2, 2, 4, 2, 4, 16, 3 * PAIR), jnp.bfloat16),
            pltpu.VMEM((C, D), jnp.bfloat16),
            pltpu.SemaphoreType.DMA((STEPS,)),
        ],
        compiler_params=pltpu.CompilerParams(vmem_limit_bytes=56 * MIB),
        cost_estimate=pl.CostEstimate(
            flops=2 * C * D * 3 * WIDTH + 4 * C * C * WIDTH,
            bytes_accessed=2 * (C * D + 3 * D * WIDTH + C * WIDTH),
            transcendentals=C * C * HEADS,
        ),
    )(core, x, *tables, *planes)


def branch_sum(core, att_ref, own_ref, other_ref, resid_ref):
    width = WIDTH // 4
    total = resid_ref[...].astype(jnp.float32)
    for slot in range(4):
        block = jnp.where(slot < 2, core, 1 - core) + 2 * (slot % 2)
        lanes = pl.ds(pl.multiple_of(block * width, width), width)
        ref = own_ref if slot < 2 else other_ref
        rows = slice((slot % 2) * width, (slot % 2 + 1) * width)
        total = total + dot(att_ref[:, lanes], ref[rows, :])
    return total


def final_kernel(core_ref, att_ref, own_ref, other_ref, resid_ref, out_ref):
    out_ref[...] = branch_sum(core_ref[0], att_ref, own_ref, other_ref, resid_ref).astype(jnp.bfloat16)


def output_layer(core, attended, own, other, resid):
    size = 128
    block = lambda width: pl.BlockSpec((size, width), lambda i: (i, 0))
    whole = lambda shape: pl.BlockSpec(shape, lambda i: (0, 0), pipeline_mode=pl.Buffered(1))
    return pl.pallas_call(
        final_kernel,
        grid=(C // size,),
        out_shape=jax.ShapeDtypeStruct((C, D), jnp.bfloat16),
        in_specs=[
            pl.BlockSpec(memory_space=pltpu.SMEM),
            block(WIDTH),
            whole(own.shape),
            whole(other.shape),
            block(D),
        ],
        out_specs=block(D),
        compiler_params=pltpu.CompilerParams(
            dimension_semantics=("arbitrary",), vmem_limit_bytes=40 * MIB
        ),
        cost_estimate=pl.CostEstimate(
            flops=2 * C * D * WIDTH,
            bytes_accessed=2 * (2 * C * D + D * WIDTH + C * WIDTH),
            transcendentals=0,
        ),
    )(core, attended, own, other, resid)


def shift(value, axis, by):
    if axis == "y":
        where = lambda y: (y % 2) * 2 + y // 2
        return lax.ppermute(value, ("ylo", "yhi"), [(where(y), where((y + by) % 4)) for y in range(4)])
    return lax.ppermute(value, axis, [(i, (i + by) % 4) for i in range(4)])


def ring(value, axis):
    half = value.shape[-1] // 2
    left = shift(value, axis, 1)
    right = shift(value, axis, -1)
    return [value, left, right, shift(left[..., :half], axis, 1), shift(right[..., half:], axis, -1)]


def stack(pieces):
    own, left, right, low, high = pieces
    return jnp.stack([own, left, right, jnp.concatenate([low, high], -1)])


def swap(value):
    return lax.ppermute(value, "core", [(0, 1), (1, 0)])


def fold_output(output):
    return jnp.concatenate([output[:, : D // 2], output[:, D // 2 :]], 0)


def by_step(inputs):
    return inputs.reshape(-1, 3, STEPS, PAIR).transpose(0, 2, 1, 3).reshape(-1, 3 * WIDTH)


def row_weights(inputs, output, line):
    shard = jnp.concatenate([by_step(inputs), fold_output(output)], 1)
    rows = lax.all_gather(shard, "z", axis=0)
    qkv = rows[:, :, : 3 * WIDTH].reshape(2, 32, 3 * WIDTH)
    out = rows[:, :, 3 * WIDTH :].reshape(4, 2, 8, WIDTH).transpose(1, 0, 2, 3).reshape(2, 32, WIDTH)
    parts = []
    for p in range(2):
        lanes = slice(p * QKV_PART, (p + 1) * QKV_PART)
        rest = slice(p * WIDTH // 2, (p + 1) * WIDTH // 2)
        parts.append(jnp.concatenate([qkv[:, :, lanes], out[:, :, rest]], -1))
    stacks = [stack(ring(parts[0], "x")), stack(ring(parts[1], "y"))]
    stacks, line = lax.optimization_barrier((stacks, line))
    own = [ring(stacks[0], "y"), ring(stacks[1], "x")]
    return own, line


def column_line(inputs, output):
    shard = jnp.concatenate([by_step(inputs), fold_output(output)], 1)
    return lax.all_gather(jnp.concatenate([shard, shard], 1), ("ylo", "yhi"), axis=0)


def column_plane(line):
    return lax.all_gather(line[:, :, : 4 * WIDTH], ("x", "z"), axis=0).reshape(4, 4, 2, 2, 16, 4 * WIDTH)


def column_output(plane):
    out = plane[..., 3 * WIDTH :].transpose(2, 0, 3, 1, 4, 5)
    return out.reshape(64, 2, 8, WIDTH).transpose(0, 2, 1, 3).reshape(WIDTH // 2, D)


def shards(tokens, gain_first, inputs_first, output_first, gain_second, inputs_second, output_second, starts, band_edges):
    residual = tokens[0]
    core = lax.axis_index("core").astype(jnp.int32)
    core_scalar = core.reshape(1)
    seq = lax.axis_index(SEQ)
    my_y = lax.axis_index("yhi") * 2 + lax.axis_index("ylo")
    place = jnp.stack([core, lax.axis_index("x").astype(jnp.int32), my_y.astype(jnp.int32)])

    line = column_line(inputs_second, output_second)
    frequency = frequencies(band_edges, HEAD // 2)
    block_starts = starts[0]
    own_start = lax.dynamic_index_in_dim(block_starts, seq, 0, keepdims=False)
    row_tables = rotary_tables(own_start + jnp.arange(C, dtype=jnp.int32), frequency)
    columns = seq.astype(jnp.int32) * COLS + jnp.arange(COLS, dtype=jnp.int32)
    column_positions = (columns[:, None] + block_starts[None, :]).reshape(C)
    column_tables = rotary_tables(column_positions, frequency)

    hidden = normed_slots(core_scalar, residual, gain_first.reshape(1, D))
    own, line = row_weights(inputs_first, output_first, line)
    plane = column_plane(line)
    pieces = [piece for part in own for piece in part]
    early, hidden, row_tables, column_tables = lax.optimization_barrier(
        (own[0][1], hidden, row_tables, column_tables)
    )
    other = [swap(early if index == 1 else piece) for index, piece in enumerate(pieces)]
    pieces = pieces + other
    middle, hidden = row_layer(place, residual, hidden, gain_second.reshape(1, D), row_tables, pieces)
    plane, hidden = lax.optimization_barrier((plane, hidden))
    planes = (plane, swap(plane))
    hidden = lax.all_to_all(hidden, SEQ, split_axis=0, concat_axis=0, tiled=True)
    attended = column_layer(core_scalar, hidden, column_tables, planes)
    attended = lax.all_to_all(attended, SEQ, split_axis=0, concat_axis=0, tiled=True)
    return output_layer(core_scalar, attended, *[column_output(p) for p in planes], middle)[None]


def solution(mesh):
    split = Mesh(mesh.devices.reshape(2, 2, 4, 2, 4), ("ylo", "core") + SEQ)
    dp = ("ylo", "core")
    every = dp + SEQ
    return jax.shard_map(
        shards,
        mesh=split,
        in_specs=(
            P(dp, SEQ, None),
            P(),
            P(every, None),
            P(every, None),
            P(),
            P(every, None),
            P(every, None),
            P(dp, None),
            P(),
        ),
        out_specs=P(dp, SEQ, None),
        check_vma=False,
    )
```

```python
import math

import jax
import jax.numpy as jnp
from jax import lax
from jax.experimental import pallas as pl
from jax.experimental.pallas import tpu as pltpu
from jax.sharding import Mesh, PartitionSpec as P

HEADS = 8
HEAD = 128
C = 512
SCALE = 8
D = 2048
WIDTH = HEADS * HEAD
N_SEQ = 32
COLS = C // N_SEQ
PAIR = 2 * HEAD
STEPS = WIDTH // PAIR
SEQ = ("x", "yhi", "z")
QKV_HALF = 3 * WIDTH // 2
PART = 4 * WIDTH
RELATIVE = ((0, 0, PART), (3, 0, PART), (1, 0, PART), (2, 0, PART // 2), (2, PART // 2, PART))
RINGS = (0, 3, 1, 2)
LOG2E = 1.4426950408889634
MIB = 1 << 20


def frequencies(band_edges, half_size):
    dim_index = jnp.arange(half_size, dtype=jnp.float32)
    base_freq = jnp.power(10000.0, -dim_index / half_size)
    lower_edge = band_edges[0].astype(jnp.float32)
    upper_edge = band_edges[1].astype(jnp.float32)
    ramp_share = jnp.clip((dim_index - lower_edge) / (upper_edge - lower_edge), 0.0, 1.0)
    return base_freq * (1.0 - ramp_share) + base_freq * ramp_share / SCALE


def rotary_tables(positions, frequency):
    angles = positions.astype(jnp.float32)[:, None] * frequency
    mscale = 0.1 * math.log(SCALE) + 1.0
    cosine = jnp.cos(angles) * mscale
    sine = jnp.sin(angles) * mscale
    return jnp.concatenate([cosine, cosine], -1), jnp.concatenate([-sine, sine], -1)


def dot(a, b):
    return jnp.dot(a, b, preferred_element_type=jnp.float32)


def dot_t(a, b):
    return lax.dot_general(a, b, (((1,), (1,)), ((), ())), preferred_element_type=jnp.float32)


def slot_of(block, core):
    other = jnp.where(lax.rem(block, 2) == core, 0, 2)
    return other + block // 2


def rotate(heads, cos, sin):
    return heads * cos + pltpu.roll(heads, HEAD // 2, 1) * sin


def softmax_times(scores, keep, values):
    scores = jnp.where(keep, scores, -1e30)
    top = jnp.max(scores, axis=-1, keepdims=True)
    weights = jnp.exp2((scores - top) * (LOG2E / math.sqrt(HEAD)))
    total = jnp.sum(weights, axis=-1, keepdims=True)
    return dot(weights.astype(jnp.bfloat16), values) / total


def norm_kernel(core_ref, x_ref, gain_ref, hid_ref):
    core = core_ref[0]

    def chunk(i, _):
        rows = pl.ds(pl.multiple_of(i * 32, 32), 32)
        x = x_ref[rows, :].astype(jnp.float32)
        inv = lax.rsqrt(jnp.mean(x * x, axis=-1, keepdims=True) + 1e-05)
        hidden = (x * inv * gain_ref[...]).astype(jnp.bfloat16)
        width = D // 4
        for block in range(4):
            lanes = pl.ds(pl.multiple_of(slot_of(block, core) * width, width), width)
            hid_ref[rows, lanes] = hidden[:, block * width : (block + 1) * width]
        return 0

    lax.fori_loop(0, C // 32, chunk, 0)


def normed_slots(core, x, gain):
    vmem = pl.BlockSpec(memory_space=pltpu.VMEM)
    hbm = pl.BlockSpec(memory_space=pltpu.HBM)
    return pl.pallas_call(
        norm_kernel,
        out_shape=jax.ShapeDtypeStruct((C, D), jnp.bfloat16),
        in_specs=[pl.BlockSpec(memory_space=pltpu.SMEM), vmem, vmem],
        out_specs=vmem,
        compiler_params=pltpu.CompilerParams(vmem_limit_bytes=16 * MIB),
        cost_estimate=pl.CostEstimate(flops=4 * C * D, bytes_accessed=4 * C * D, transcendentals=C),
    )(core, x, gain)


def start_copies(place_ref, pieces, sems, w_ref, o_ref):
    my_x, my_y = place_ref[1], place_ref[2]

    def block_of(stacked, ring):
        x = lax.rem(my_x + stacked, 4)
        y = lax.rem(my_y + ring, 4)
        return lax.rem(y, 2) * 8 + x * 2 + y // 2

    def move(slot, first, last, dst_of, sem):
        for index, (ring, low, high) in enumerate(RELATIVE):
            begin, end = max(low, first), min(high, last)
            if begin >= end:
                continue
            src = pieces[slot * len(RELATIVE) + index]
            for k, stacked in enumerate(RINGS):
                dst = dst_of(block_of(stacked, ring)).at[:, :, pl.ds(begin - first, end - begin)]
                pltpu.make_async_copy(src.at[k, :, :, pl.ds(begin - low, end - begin)], dst, sem).start()

    for group in range(2):
        for slot in range(2):
            move(
                slot,
                group * QKV_HALF,
                (group + 1) * QKV_HALF,
                lambda block: w_ref.at[slot, group, block],
                sems.at[slot * 2 + group],
            )
    for slot in range(2):
        move(slot, 2 * QKV_HALF, PART, lambda block: o_ref.at[slot, block], sems.at[4 + slot])


def arrived(ref, sem):
    pltpu.make_async_copy(ref, ref, sem).wait()


def step_weights(w_ref, sems, g):
    part = g // 2
    for p in range(2):

        @pl.when(g == 2 * p)
        def _():
            for slot in range(2):
                arrived(w_ref.at[slot, p], sems.at[slot * 2 + p])

    base = lax.rem(g, 2) * (3 * PAIR)

    def weight(slot, kind):
        lanes = pl.ds(pl.multiple_of(base + kind * PAIR, PAIR), PAIR)
        return w_ref[slot, part, :, :, :, lanes].reshape(D // 2, PAIR)

    return weight


def output_sum(core, att_ref, rows, o_ref, h, total):
    for slot in range(2):
        for j in range(2):
            block = (core if slot == 0 else 1 - core) + 2 * j
            lanes = pl.ds(pl.multiple_of(block * PAIR, PAIR), PAIR)
            weight = o_ref[slot, j * 8 : (j + 1) * 8, h].reshape(PAIR, D // 2)
            total = total + dot(att_ref[rows, lanes], weight)
    return total


def row_kernel(place_ref, x_ref, hid_ref, gain_ref, cos_ref, sin_ref, *refs):
    pieces = refs[: 2 * len(RELATIVE)]
    mid_ref, next_ref, w_ref, o_ref, att_ref, sems = refs[2 * len(RELATIVE) :]
    core = place_ref[0]
    start_copies(place_ref, pieces, sems, w_ref, o_ref)
    half = D // 2

    def step(g, _):
        weight = step_weights(w_ref, sems, g)

        def projected(kind):
            return dot(hid_ref[:, :half], weight(0, kind)) + dot(hid_ref[:, half:], weight(1, kind))

        q2 = projected(0)
        k2 = projected(1)
        v2 = projected(2).astype(jnp.bfloat16)
        for h in range(2):
            lanes = slice(h * HEAD, (h + 1) * HEAD)
            q = rotate(q2[:, lanes], cos_ref[...], sin_ref[...]).astype(jnp.bfloat16)
            k = rotate(k2[:, lanes], cos_ref[...], sin_ref[...]).astype(jnp.bfloat16)
            v = v2[:, lanes]
            size = 256
            for b in range(C // size):
                end = (b + 1) * size
                scores = dot_t(q[b * size : end], k[:end])
                row = lax.broadcasted_iota(jnp.int32, scores.shape, 0) + b * size
                keep = lax.broadcasted_iota(jnp.int32, scores.shape, 1) <= row
                target = pl.ds(pl.multiple_of(g * PAIR + h * HEAD, HEAD), HEAD)
                att_ref[b * size : end, target] = softmax_times(scores, keep, v[:end]).astype(jnp.bfloat16)
        return 0

    lax.fori_loop(0, STEPS, step, 0)
    for slot in range(2):
        arrived(o_ref.at[slot], sems.at[4 + slot])

    def finish(i, _):
        rows = pl.ds(pl.multiple_of(i * 128, 128), 128)
        halves = []
        squares = jnp.zeros((128, 1), jnp.float32)
        for h in range(2):
            lanes = slice(h * half, (h + 1) * half)
            total = output_sum(core, att_ref, rows, o_ref, h, x_ref[rows, lanes].astype(jnp.float32))
            middle = total.astype(jnp.bfloat16)
            mid_ref[rows, lanes] = middle
            middle = middle.astype(jnp.float32)
            squares = squares + jnp.sum(middle * middle, axis=-1, keepdims=True)
            halves.append(middle)
        inv = lax.rsqrt(squares / D + 1e-05)
        for h in range(2):
            lanes = slice(h * half, (h + 1) * half)
            next_ref[rows, lanes] = (halves[h] * inv * gain_ref[:, lanes]).astype(jnp.bfloat16)
        return 0

    lax.fori_loop(0, C // 128, finish, 0)


def row_layer(place, x, hidden, gain, tables, pieces):
    vmem = pl.BlockSpec(memory_space=pltpu.VMEM)
    hbm = pl.BlockSpec(memory_space=pltpu.HBM)
    shape = jax.ShapeDtypeStruct((C, D), jnp.bfloat16)
    return pl.pallas_call(
        row_kernel,
        out_shape=[shape, shape],
        in_specs=[pl.BlockSpec(memory_space=pltpu.SMEM)]
        + [vmem] * 5
        + [hbm] * len(pieces),
        out_specs=[vmem, vmem],
        scratch_shapes=[
            pltpu.VMEM((2, 2, 16, 2, 32, QKV_HALF), jnp.bfloat16),
            pltpu.VMEM((2, 16, 2, 32, D // 2), jnp.bfloat16),
            pltpu.VMEM((C, WIDTH), jnp.bfloat16),
            pltpu.SemaphoreType.DMA((6,)),
        ],
        compiler_params=pltpu.CompilerParams(vmem_limit_bytes=48 * MIB),
        cost_estimate=pl.CostEstimate(
            flops=2 * C * D * 4 * WIDTH + 4 * C * C * WIDTH,
            bytes_accessed=2 * (4 * C * D + 4 * D * WIDTH),
            transcendentals=C * C * HEADS,
        ),
    )(place, x, hidden, gain, *tables, *pieces)


def column_kernel(core_ref, x_ref, cos_ref, sin_ref, own_plane, other_plane, out_ref, w_ref, hid_ref, sems):
    core = core_ref[0]
    half = D // 2
    triple = 3 * PAIR

    for g in range(STEPS):
        lanes = pl.ds(g * triple, triple)
        for slot, plane in enumerate((own_plane, other_plane)):
            for ylo in range(2):
                for yhi in range(2):
                    src = plane.at[:, :, ylo, yhi, :, lanes]
                    dst = w_ref.at[g, slot, ylo, :, yhi]
                    pltpu.make_async_copy(src, dst, sems.at[g]).start()

    def selection(transposed):
        a = lax.broadcasted_iota(jnp.int32, (C, C), 1 if transposed else 0)
        b = lax.broadcasted_iota(jnp.int32, (C, C), 0 if transposed else 1)
        same = (a // N_SEQ == lax.rem(b, COLS)) & (lax.rem(a, N_SEQ) == b // COLS)
        return jnp.where(same, 1.0, 0.0).astype(jnp.bfloat16)

    pick = selection(False)
    width = D // 4
    for block in range(4):
        lanes = pl.ds(pl.multiple_of(slot_of(block, core) * width, width), width)
        moved = dot(pick, x_ref[:, block * width : (block + 1) * width])
        hid_ref[:, lanes] = moved.astype(jnp.bfloat16)

    back = selection(True)
    size = 128
    row = lax.broadcasted_iota(jnp.int32, (size, size), 0)
    col = lax.broadcasted_iota(jnp.int32, (size, size), 1)
    keep = (row // N_SEQ == col // N_SEQ) & (col <= row)

    def step(g, _):
        pltpu.make_async_copy(w_ref.at[g], w_ref.at[g], sems.at[g]).wait()

        def weight(slot, kind):
            lanes = slice(kind * PAIR, (kind + 1) * PAIR)
            return w_ref[g, slot, :, :, :, :, :, lanes].reshape(half, PAIR)

        def projected(kind):
            return dot(hid_ref[:, :half], weight(0, kind)) + dot(hid_ref[:, half:], weight(1, kind))

        q2 = projected(0)
        k2 = projected(1)
        v2 = projected(2).astype(jnp.bfloat16)
        heads = []
        for h in range(2):
            lanes = slice(h * HEAD, (h + 1) * HEAD)
            q = rotate(q2[:, lanes], cos_ref[...], sin_ref[...]).astype(jnp.bfloat16)
            k = rotate(k2[:, lanes], cos_ref[...], sin_ref[...]).astype(jnp.bfloat16)
            v = v2[:, lanes]
            blocks = []
            for b in range(C // size):
                rows = slice(b * size, (b + 1) * size)
                blocks.append(softmax_times(dot_t(q[rows], k[rows]), keep, v[rows]).astype(jnp.bfloat16))
            heads.append(jnp.concatenate(blocks, 0))
        attended = jnp.concatenate(heads, 1)
        lanes = pl.ds(pl.multiple_of(g * PAIR, PAIR), PAIR)
        out_ref[:, lanes] = dot(back, attended).astype(jnp.bfloat16)
        return 0

    lax.fori_loop(0, STEPS, step, 0)


def column_layer(core, x, tables, planes):
    vmem = pl.BlockSpec(memory_space=pltpu.VMEM)
    hbm = pl.BlockSpec(memory_space=pltpu.HBM)
    return pl.pallas_call(
        column_kernel,
        out_shape=jax.ShapeDtypeStruct((C, WIDTH), jnp.bfloat16),
        in_specs=[pl.BlockSpec(memory_space=pltpu.SMEM)] + [vmem] * 3 + [hbm] * 2,
        out_specs=vmem,
        scratch_shapes=[
            pltpu.VMEM((STEPS, 2, 2, 4, 2, 4, 16, 3 * PAIR), jnp.bfloat16),
            pltpu.VMEM((C, D), jnp.bfloat16),
            pltpu.SemaphoreType.DMA((STEPS,)),
        ],
        compiler_params=pltpu.CompilerParams(vmem_limit_bytes=56 * MIB),
        cost_estimate=pl.CostEstimate(
            flops=2 * C * D * 3 * WIDTH + 4 * C * C * WIDTH,
            bytes_accessed=2 * (C * D + 3 * D * WIDTH + C * WIDTH),
            transcendentals=C * C * HEADS,
        ),
    )(core, x, *tables, *planes)


def branch_sum(core, att_ref, own_ref, other_ref, resid_ref):
    width = WIDTH // 4
    total = resid_ref[...].astype(jnp.float32)
    for slot in range(4):
        block = jnp.where(slot < 2, core, 1 - core) + 2 * (slot % 2)
        lanes = pl.ds(pl.multiple_of(block * width, width), width)
        ref = own_ref if slot < 2 else other_ref
        rows = slice((slot % 2) * width, (slot % 2 + 1) * width)
        total = total + dot(att_ref[:, lanes], ref[rows, :])
    return total


def final_kernel(core_ref, att_ref, own_ref, other_ref, resid_ref, out_ref):
    out_ref[...] = branch_sum(core_ref[0], att_ref, own_ref, other_ref, resid_ref).astype(jnp.bfloat16)


def output_layer(core, attended, own, other, resid):
    size = 128
    block = lambda width: pl.BlockSpec((size, width), lambda i: (i, 0))
    whole = lambda shape: pl.BlockSpec(shape, lambda i: (0, 0), pipeline_mode=pl.Buffered(1))
    return pl.pallas_call(
        final_kernel,
        grid=(C // size,),
        out_shape=jax.ShapeDtypeStruct((C, D), jnp.bfloat16),
        in_specs=[
            pl.BlockSpec(memory_space=pltpu.SMEM),
            block(WIDTH),
            whole(own.shape),
            whole(other.shape),
            block(D),
        ],
        out_specs=block(D),
        compiler_params=pltpu.CompilerParams(
            dimension_semantics=("arbitrary",), vmem_limit_bytes=40 * MIB
        ),
        cost_estimate=pl.CostEstimate(
            flops=2 * C * D * WIDTH,
            bytes_accessed=2 * (2 * C * D + D * WIDTH + C * WIDTH),
            transcendentals=0,
        ),
    )(core, attended, own, other, resid)


def shift(value, axis, by):
    if axis == "y":
        where = lambda y: (y % 2) * 2 + y // 2
        return lax.ppermute(value, ("ylo", "yhi"), [(where(y), where((y + by) % 4)) for y in range(4)])
    return lax.ppermute(value, axis, [(i, (i + by) % 4) for i in range(4)])


def first_hops(value, axis):
    return [value, shift(value, axis, 1), shift(value, axis, -1)]


def forwards(hops, axis):
    own, left, right = hops
    half = own.shape[-1] // 2
    return hops + [shift(left[..., :half], axis, 1), shift(right[..., half:], axis, -1)]


def stack(pieces):
    own, left, right, low, high = pieces
    return jnp.stack([own, left, right, jnp.concatenate([low, high], -1)])


def swap(value):
    return lax.ppermute(value, "core", [(0, 1), (1, 0)])


def fold_output(output):
    return jnp.concatenate([output[:, : D // 2], output[:, D // 2 :]], 0)


def by_step(inputs):
    return inputs.reshape(-1, 3, STEPS, PAIR).transpose(0, 2, 1, 3).reshape(-1, 3 * WIDTH)


def row_stack(inputs, output):
    shard = jnp.concatenate([by_step(inputs), fold_output(output)], 1)
    rows = lax.all_gather(shard, "z", axis=0)
    qkv = rows[:, :, : 3 * WIDTH].reshape(2, 32, 3 * WIDTH)
    out = rows[:, :, 3 * WIDTH :].reshape(4, 2, 8, WIDTH).transpose(1, 0, 2, 3).reshape(2, 32, WIDTH)
    return stack(forwards(first_hops(jnp.concatenate([qkv, out], -1), "x"), "x"))


def column_line(inputs, output):
    shard = jnp.concatenate([by_step(inputs), fold_output(output)], 1)
    return lax.all_gather(shard, ("ylo", "yhi"), axis=0)


def column_plane(line):
    return lax.all_gather(line, ("x", "z"), axis=0).reshape(4, 4, 2, 2, 16, 4 * WIDTH)


def column_output(plane):
    out = plane[..., 3 * WIDTH :].transpose(2, 0, 3, 1, 4, 5)
    return out.reshape(64, 2, 8, WIDTH).transpose(0, 2, 1, 3).reshape(WIDTH // 2, D)


def shards(tokens, gain_first, inputs_first, output_first, gain_second, inputs_second, output_second, starts, band_edges):
    residual = tokens[0]
    core = lax.axis_index("core").astype(jnp.int32)
    core_scalar = core.reshape(1)
    seq = lax.axis_index(SEQ)
    my_y = lax.axis_index("yhi") * 2 + lax.axis_index("ylo")
    place = jnp.stack([core, lax.axis_index("x").astype(jnp.int32), my_y.astype(jnp.int32)])

    frequency = frequencies(band_edges, HEAD // 2)
    block_starts = starts[0]
    own_start = lax.dynamic_index_in_dim(block_starts, seq, 0, keepdims=False)
    row_tables = rotary_tables(own_start + jnp.arange(C, dtype=jnp.int32), frequency)
    columns = seq.astype(jnp.int32) * COLS + jnp.arange(COLS, dtype=jnp.int32)
    column_positions = (columns[:, None] + block_starts[None, :]).reshape(C)
    column_tables = rotary_tables(column_positions, frequency)

    hidden = normed_slots(core_scalar, residual, gain_first.reshape(1, D))

    own_stack = row_stack(inputs_first, output_first)
    inputs_second, output_second, own_stack = lax.optimization_barrier((inputs_second, output_second, own_stack))
    plane = column_plane(column_line(inputs_second, output_second))
    pieces = forwards(first_hops(own_stack, "y"), "y")
    own_stack, hidden, row_tables, column_tables = lax.optimization_barrier(
        (own_stack, hidden, row_tables, column_tables)
    )
    pieces = pieces + [swap(own_stack)] + [swap(piece) for piece in pieces[1:]]

    middle, hidden = row_layer(place, residual, hidden, gain_second.reshape(1, D), row_tables, pieces)
    plane, hidden = lax.optimization_barrier((plane, hidden))
    planes = (plane, swap(plane))
    hidden = lax.all_to_all(hidden, SEQ, split_axis=0, concat_axis=0, tiled=True)
    attended = column_layer(core_scalar, hidden, column_tables, planes)
    attended = lax.all_to_all(attended, SEQ, split_axis=0, concat_axis=0, tiled=True)
    return output_layer(core_scalar, attended, *[column_output(p) for p in planes], middle)[None]


def solution(mesh):
    split = Mesh(mesh.devices.reshape(2, 2, 4, 2, 4), ("ylo", "core") + SEQ)
    dp = ("ylo", "core")
    every = dp + SEQ
    return jax.shard_map(
        shards,
        mesh=split,
        in_specs=(
            P(dp, SEQ, None),
            P(),
            P(every, None),
            P(every, None),
            P(),
            P(every, None),
            P(every, None),
            P(dp, None),
            P(),
        ),
        out_specs=P(dp, SEQ, None),
        check_vma=False,
    )
```

```python
import math

import jax
import jax.numpy as jnp
from jax import lax
from jax.experimental import pallas as pl
from jax.experimental.pallas import tpu as pltpu
from jax.sharding import Mesh, PartitionSpec as P

HEADS = 8
HEAD = 128
C = 512
SCALE = 8
D = 2048
WIDTH = HEADS * HEAD
N_SEQ = 32
COLS = C // N_SEQ
PAIR = 2 * HEAD
STEPS = WIDTH // PAIR
SEQ = ("x", "yhi", "z")
QKV_HALF = 3 * WIDTH // 2
PART = 4 * WIDTH
RELATIVE = ((0, 0, PART), (3, 0, PART), (1, 0, PART), (2, 0, PART // 2), (2, PART // 2, PART))
RINGS = (0, 3, 1, 2)
LOG2E = 1.4426950408889634
MIB = 1 << 20


def frequencies(band_edges, half_size):
    dim_index = jnp.arange(half_size, dtype=jnp.float32)
    base_freq = jnp.power(10000.0, -dim_index / half_size)
    lower_edge = band_edges[0].astype(jnp.float32)
    upper_edge = band_edges[1].astype(jnp.float32)
    ramp_share = jnp.clip((dim_index - lower_edge) / (upper_edge - lower_edge), 0.0, 1.0)
    return base_freq * (1.0 - ramp_share) + base_freq * ramp_share / SCALE


def rotary_tables(positions, frequency):
    angles = positions.astype(jnp.float32)[:, None] * frequency
    mscale = 0.1 * math.log(SCALE) + 1.0
    cosine = jnp.cos(angles) * mscale
    sine = jnp.sin(angles) * mscale
    return jnp.concatenate([cosine, cosine], -1), jnp.concatenate([-sine, sine], -1)


def dot(a, b):
    return jnp.dot(a, b, preferred_element_type=jnp.float32)


def dot_t(a, b):
    return lax.dot_general(a, b, (((1,), (1,)), ((), ())), preferred_element_type=jnp.float32)


def slot_of(block, core):
    other = jnp.where(lax.rem(block, 2) == core, 0, 2)
    return other + block // 2


def rotate(heads, cos, sin):
    return heads * cos + pltpu.roll(heads, HEAD // 2, 1) * sin


def softmax_times(scores, keep, values):
    scores = jnp.where(keep, scores, -1e30)
    top = jnp.max(scores, axis=-1, keepdims=True)
    weights = jnp.exp2((scores - top) * (LOG2E / math.sqrt(HEAD)))
    total = jnp.sum(weights, axis=-1, keepdims=True)
    return dot(weights.astype(jnp.bfloat16), values) / total


def norm_kernel(core_ref, x_ref, gain_ref, hid_ref):
    core = core_ref[0]

    def chunk(i, _):
        rows = pl.ds(pl.multiple_of(i * 32, 32), 32)
        x = x_ref[rows, :].astype(jnp.float32)
        inv = lax.rsqrt(jnp.mean(x * x, axis=-1, keepdims=True) + 1e-05)
        hidden = (x * inv * gain_ref[...]).astype(jnp.bfloat16)
        width = D // 4
        for block in range(4):
            lanes = pl.ds(pl.multiple_of(slot_of(block, core) * width, width), width)
            hid_ref[rows, lanes] = hidden[:, block * width : (block + 1) * width]
        return 0

    lax.fori_loop(0, C // 32, chunk, 0)


def normed_slots(core, x, gain):
    vmem = pl.BlockSpec(memory_space=pltpu.VMEM)
    hbm = pl.BlockSpec(memory_space=pltpu.HBM)
    return pl.pallas_call(
        norm_kernel,
        out_shape=jax.ShapeDtypeStruct((C, D), jnp.bfloat16),
        in_specs=[pl.BlockSpec(memory_space=pltpu.SMEM), vmem, vmem],
        out_specs=vmem,
        compiler_params=pltpu.CompilerParams(vmem_limit_bytes=16 * MIB),
        cost_estimate=pl.CostEstimate(flops=4 * C * D, bytes_accessed=4 * C * D, transcendentals=C),
    )(core, x, gain)


def start_copies(place_ref, pieces, sems, w_ref, o_ref):
    my_x, my_y = place_ref[1], place_ref[2]

    def block_of(stacked, ring):
        x = lax.rem(my_x + stacked, 4)
        y = lax.rem(my_y + ring, 4)
        return lax.rem(y, 2) * 8 + x * 2 + y // 2

    def move(slot, first, last, dst_of, sem):
        for index, (ring, low, high) in enumerate(RELATIVE):
            begin, end = max(low, first), min(high, last)
            if begin >= end:
                continue
            src = pieces[slot * len(RELATIVE) + index]
            for k, stacked in enumerate(RINGS):
                dst = dst_of(block_of(stacked, ring)).at[:, :, pl.ds(begin - first, end - begin)]
                pltpu.make_async_copy(src.at[k, :, :, pl.ds(begin - low, end - begin)], dst, sem).start()

    for group in range(2):
        for slot in range(2):
            move(
                slot,
                group * QKV_HALF,
                (group + 1) * QKV_HALF,
                lambda block: w_ref.at[slot, group, block],
                sems.at[slot * 2 + group],
            )
    for slot in range(2):
        move(slot, 2 * QKV_HALF, PART, lambda block: o_ref.at[slot, block], sems.at[4 + slot])


def arrived(ref, sem):
    pltpu.make_async_copy(ref, ref, sem).wait()


def step_weights(w_ref, sems, g):
    part = g // 2
    for p in range(2):

        @pl.when(g == 2 * p)
        def _():
            for slot in range(2):
                arrived(w_ref.at[slot, p], sems.at[slot * 2 + p])

    base = lax.rem(g, 2) * (3 * PAIR)

    def weight(slot, kind):
        lanes = pl.ds(pl.multiple_of(base + kind * PAIR, PAIR), PAIR)
        return w_ref[slot, part, :, :, :, lanes].reshape(D // 2, PAIR)

    return weight


def output_sum(core, att_ref, rows, o_ref, h, total):
    for slot in range(2):
        for j in range(2):
            block = (core if slot == 0 else 1 - core) + 2 * j
            lanes = pl.ds(pl.multiple_of(block * PAIR, PAIR), PAIR)
            weight = o_ref[slot, j * 8 : (j + 1) * 8, h].reshape(PAIR, D // 2)
            total = total + dot(att_ref[rows, lanes], weight)
    return total


def row_kernel(place_ref, x_ref, hid_ref, gain_ref, cos_ref, sin_ref, *refs):
    pieces = refs[: 2 * len(RELATIVE)]
    mid_ref, next_ref, w_ref, o_ref, att_ref, sems = refs[2 * len(RELATIVE) :]
    core = place_ref[0]
    start_copies(place_ref, pieces, sems, w_ref, o_ref)
    half = D // 2

    def step(g, _):
        weight = step_weights(w_ref, sems, g)

        def projected(kind):
            return dot(hid_ref[:, :half], weight(0, kind)) + dot(hid_ref[:, half:], weight(1, kind))

        q2 = projected(0)
        k2 = projected(1)
        v2 = projected(2).astype(jnp.bfloat16)
        for h in range(2):
            lanes = slice(h * HEAD, (h + 1) * HEAD)
            q = rotate(q2[:, lanes], cos_ref[...], sin_ref[...]).astype(jnp.bfloat16)
            k = rotate(k2[:, lanes], cos_ref[...], sin_ref[...]).astype(jnp.bfloat16)
            v = v2[:, lanes]
            size = 256
            for b in range(C // size):
                end = (b + 1) * size
                scores = dot_t(q[b * size : end], k[:end])
                row = lax.broadcasted_iota(jnp.int32, scores.shape, 0) + b * size
                keep = lax.broadcasted_iota(jnp.int32, scores.shape, 1) <= row
                target = pl.ds(pl.multiple_of(g * PAIR + h * HEAD, HEAD), HEAD)
                att_ref[b * size : end, target] = softmax_times(scores, keep, v[:end]).astype(jnp.bfloat16)
        return 0

    lax.fori_loop(0, STEPS, step, 0)
    for slot in range(2):
        arrived(o_ref.at[slot], sems.at[4 + slot])

    def finish(i, _):
        rows = pl.ds(pl.multiple_of(i * 128, 128), 128)
        halves = []
        squares = jnp.zeros((128, 1), jnp.float32)
        for h in range(2):
            lanes = slice(h * half, (h + 1) * half)
            total = output_sum(core, att_ref, rows, o_ref, h, x_ref[rows, lanes].astype(jnp.float32))
            middle = total.astype(jnp.bfloat16)
            mid_ref[rows, lanes] = middle
            middle = middle.astype(jnp.float32)
            squares = squares + jnp.sum(middle * middle, axis=-1, keepdims=True)
            halves.append(middle)
        inv = lax.rsqrt(squares / D + 1e-05)
        for h in range(2):
            lanes = slice(h * half, (h + 1) * half)
            next_ref[rows, lanes] = (halves[h] * inv * gain_ref[:, lanes]).astype(jnp.bfloat16)
        return 0

    lax.fori_loop(0, C // 128, finish, 0)


def row_layer(place, x, hidden, gain, tables, pieces):
    vmem = pl.BlockSpec(memory_space=pltpu.VMEM)
    hbm = pl.BlockSpec(memory_space=pltpu.HBM)
    shape = jax.ShapeDtypeStruct((C, D), jnp.bfloat16)
    return pl.pallas_call(
        row_kernel,
        out_shape=[shape, shape],
        in_specs=[pl.BlockSpec(memory_space=pltpu.SMEM)]
        + [vmem] * 5
        + [hbm] * len(pieces),
        out_specs=[vmem, vmem],
        scratch_shapes=[
            pltpu.VMEM((2, 2, 16, 2, 32, QKV_HALF), jnp.bfloat16),
            pltpu.VMEM((2, 16, 2, 32, D // 2), jnp.bfloat16),
            pltpu.VMEM((C, WIDTH), jnp.bfloat16),
            pltpu.SemaphoreType.DMA((6,)),
        ],
        compiler_params=pltpu.CompilerParams(vmem_limit_bytes=48 * MIB),
        cost_estimate=pl.CostEstimate(
            flops=2 * C * D * 4 * WIDTH + 4 * C * C * WIDTH,
            bytes_accessed=2 * (4 * C * D + 4 * D * WIDTH),
            transcendentals=C * C * HEADS,
        ),
    )(place, x, hidden, gain, *tables, *pieces)


def column_kernel(core_ref, x_ref, cos_ref, sin_ref, own_plane, other_plane, out_ref, w_ref, hid_ref, sems):
    core = core_ref[0]
    half = D // 2
    triple = 3 * PAIR

    for g in range(STEPS):
        lanes = pl.ds(g * triple, triple)
        for slot, plane in enumerate((own_plane, other_plane)):
            for ylo in range(2):
                for yhi in range(2):
                    src = plane.at[:, :, ylo, yhi, :, lanes]
                    dst = w_ref.at[g, slot, ylo, :, yhi]
                    pltpu.make_async_copy(src, dst, sems.at[g]).start()

    def selection(transposed):
        a = lax.broadcasted_iota(jnp.int32, (C, C), 1 if transposed else 0)
        b = lax.broadcasted_iota(jnp.int32, (C, C), 0 if transposed else 1)
        same = (a // N_SEQ == lax.rem(b, COLS)) & (lax.rem(a, N_SEQ) == b // COLS)
        return jnp.where(same, 1.0, 0.0).astype(jnp.bfloat16)

    pick = selection(False)
    width = D // 4
    for block in range(4):
        lanes = pl.ds(pl.multiple_of(slot_of(block, core) * width, width), width)
        moved = dot(pick, x_ref[:, block * width : (block + 1) * width])
        hid_ref[:, lanes] = moved.astype(jnp.bfloat16)

    back = selection(True)
    size = 128
    row = lax.broadcasted_iota(jnp.int32, (size, size), 0)
    col = lax.broadcasted_iota(jnp.int32, (size, size), 1)
    keep = (row // N_SEQ == col // N_SEQ) & (col <= row)

    def step(g, _):
        pltpu.make_async_copy(w_ref.at[g], w_ref.at[g], sems.at[g]).wait()

        def weight(slot, kind):
            lanes = slice(kind * PAIR, (kind + 1) * PAIR)
            return w_ref[g, slot, :, :, :, :, :, lanes].reshape(half, PAIR)

        def projected(kind):
            return dot(hid_ref[:, :half], weight(0, kind)) + dot(hid_ref[:, half:], weight(1, kind))

        q2 = projected(0)
        k2 = projected(1)
        v2 = projected(2).astype(jnp.bfloat16)
        heads = []
        for h in range(2):
            lanes = slice(h * HEAD, (h + 1) * HEAD)
            q = rotate(q2[:, lanes], cos_ref[...], sin_ref[...]).astype(jnp.bfloat16)
            k = rotate(k2[:, lanes], cos_ref[...], sin_ref[...]).astype(jnp.bfloat16)
            v = v2[:, lanes]
            blocks = []
            for b in range(C // size):
                rows = slice(b * size, (b + 1) * size)
                blocks.append(softmax_times(dot_t(q[rows], k[rows]), keep, v[rows]).astype(jnp.bfloat16))
            heads.append(jnp.concatenate(blocks, 0))
        attended = jnp.concatenate(heads, 1)
        lanes = pl.ds(pl.multiple_of(g * PAIR, PAIR), PAIR)
        out_ref[:, lanes] = dot(back, attended).astype(jnp.bfloat16)
        return 0

    lax.fori_loop(0, STEPS, step, 0)


def column_layer(core, x, tables, planes):
    vmem = pl.BlockSpec(memory_space=pltpu.VMEM)
    hbm = pl.BlockSpec(memory_space=pltpu.HBM)
    return pl.pallas_call(
        column_kernel,
        out_shape=jax.ShapeDtypeStruct((C, WIDTH), jnp.bfloat16),
        in_specs=[pl.BlockSpec(memory_space=pltpu.SMEM)] + [vmem] * 3 + [hbm] * 2,
        out_specs=vmem,
        scratch_shapes=[
            pltpu.VMEM((STEPS, 2, 2, 4, 2, 4, 16, 3 * PAIR), jnp.bfloat16),
            pltpu.VMEM((C, D), jnp.bfloat16),
            pltpu.SemaphoreType.DMA((STEPS,)),
        ],
        compiler_params=pltpu.CompilerParams(vmem_limit_bytes=56 * MIB),
        cost_estimate=pl.CostEstimate(
            flops=2 * C * D * 3 * WIDTH + 4 * C * C * WIDTH,
            bytes_accessed=2 * (C * D + 3 * D * WIDTH + C * WIDTH),
            transcendentals=C * C * HEADS,
        ),
    )(core, x, *tables, *planes)


def branch_sum(core, att_ref, own_ref, other_ref, resid_ref):
    width = WIDTH // 4
    total = resid_ref[...].astype(jnp.float32)
    for slot in range(4):
        block = jnp.where(slot < 2, core, 1 - core) + 2 * (slot % 2)
        lanes = pl.ds(pl.multiple_of(block * width, width), width)
        ref = own_ref if slot < 2 else other_ref
        rows = slice((slot % 2) * width, (slot % 2 + 1) * width)
        total = total + dot(att_ref[:, lanes], ref[rows, :])
    return total


def final_kernel(core_ref, att_ref, own_ref, other_ref, resid_ref, out_ref):
    out_ref[...] = branch_sum(core_ref[0], att_ref, own_ref, other_ref, resid_ref).astype(jnp.bfloat16)


def output_layer(core, attended, own, other, resid):
    size = 128
    block = lambda width: pl.BlockSpec((size, width), lambda i: (i, 0))
    whole = lambda shape: pl.BlockSpec(shape, lambda i: (0, 0), pipeline_mode=pl.Buffered(1))
    return pl.pallas_call(
        final_kernel,
        grid=(C // size,),
        out_shape=jax.ShapeDtypeStruct((C, D), jnp.bfloat16),
        in_specs=[
            pl.BlockSpec(memory_space=pltpu.SMEM),
            block(WIDTH),
            whole(own.shape),
            whole(other.shape),
            block(D),
        ],
        out_specs=block(D),
        compiler_params=pltpu.CompilerParams(
            dimension_semantics=("arbitrary",), vmem_limit_bytes=40 * MIB
        ),
        cost_estimate=pl.CostEstimate(
            flops=2 * C * D * WIDTH,
            bytes_accessed=2 * (2 * C * D + D * WIDTH + C * WIDTH),
            transcendentals=0,
        ),
    )(core, attended, own, other, resid)


def shift(value, axis, by):
    if axis == "y":
        where = lambda y: (y % 2) * 2 + y // 2
        return lax.ppermute(value, ("ylo", "yhi"), [(where(y), where((y + by) % 4)) for y in range(4)])
    return lax.ppermute(value, axis, [(i, (i + by) % 4) for i in range(4)])


def first_hops(value, axis):
    return [value, shift(value, axis, 1), shift(value, axis, -1)]


def forwards(hops, axis):
    own, left, right = hops
    half = own.shape[-1] // 2
    return hops + [shift(left[..., :half], axis, 1), shift(right[..., half:], axis, -1)]


def stack(pieces):
    own, left, right, low, high = pieces
    return jnp.stack([own, left, right, jnp.concatenate([low, high], -1)])


def swap(value):
    return lax.ppermute(value, "core", [(0, 1), (1, 0)])


def fold_output(output):
    return jnp.concatenate([output[:, : D // 2], output[:, D // 2 :]], 0)


def by_step(inputs):
    return inputs.reshape(-1, 3, STEPS, PAIR).transpose(0, 2, 1, 3).reshape(-1, 3 * WIDTH)


def row_stack(inputs, output):
    shard = jnp.concatenate([by_step(inputs), fold_output(output)], 1)
    rows = lax.all_gather(shard, "z", axis=0)
    qkv = rows[:, :, : 3 * WIDTH].reshape(2, 32, 3 * WIDTH)
    out = rows[:, :, 3 * WIDTH :].reshape(4, 2, 8, WIDTH).transpose(1, 0, 2, 3).reshape(2, 32, WIDTH)
    hops = first_hops(jnp.concatenate([qkv, out], -1), "x")
    return hops, stack(forwards(hops, "x"))


def column_line(inputs, output):
    shard = jnp.concatenate([by_step(inputs), fold_output(output)], 1)
    return lax.all_gather(shard, ("ylo", "yhi"), axis=0)


def column_plane(line):
    return lax.all_gather(line, ("x", "z"), axis=0).reshape(4, 4, 2, 2, 16, 4 * WIDTH)


def column_output(plane):
    out = plane[..., 3 * WIDTH :].transpose(2, 0, 3, 1, 4, 5)
    return out.reshape(64, 2, 8, WIDTH).transpose(0, 2, 1, 3).reshape(WIDTH // 2, D)


def shards(tokens, gain_first, inputs_first, output_first, gain_second, inputs_second, output_second, starts, band_edges):
    residual = tokens[0]
    core = lax.axis_index("core").astype(jnp.int32)
    core_scalar = core.reshape(1)
    seq = lax.axis_index(SEQ)
    my_y = lax.axis_index("yhi") * 2 + lax.axis_index("ylo")
    place = jnp.stack([core, lax.axis_index("x").astype(jnp.int32), my_y.astype(jnp.int32)])

    frequency = frequencies(band_edges, HEAD // 2)
    block_starts = starts[0]
    own_start = lax.dynamic_index_in_dim(block_starts, seq, 0, keepdims=False)
    row_tables = rotary_tables(own_start + jnp.arange(C, dtype=jnp.int32), frequency)
    columns = seq.astype(jnp.int32) * COLS + jnp.arange(COLS, dtype=jnp.int32)
    column_positions = (columns[:, None] + block_starts[None, :]).reshape(C)
    column_tables = rotary_tables(column_positions, frequency)

    hidden = normed_slots(core_scalar, residual, gain_first.reshape(1, D))

    inner_hops, own_stack = row_stack(inputs_first, output_first)
    line, _ = lax.optimization_barrier((column_line(inputs_second, output_second), inner_hops))
    plane = column_plane(line)
    pieces = forwards(first_hops(own_stack, "y"), "y")
    own_stack, hidden, row_tables, column_tables = lax.optimization_barrier(
        (own_stack, hidden, row_tables, column_tables)
    )
    pieces = pieces + [swap(own_stack)] + [swap(piece) for piece in pieces[1:]]

    middle, hidden = row_layer(place, residual, hidden, gain_second.reshape(1, D), row_tables, pieces)
    plane, hidden = lax.optimization_barrier((plane, hidden))
    planes = (plane, swap(plane))
    hidden = lax.all_to_all(hidden, SEQ, split_axis=0, concat_axis=0, tiled=True)
    attended = column_layer(core_scalar, hidden, column_tables, planes)
    attended = lax.all_to_all(attended, SEQ, split_axis=0, concat_axis=0, tiled=True)
    return output_layer(core_scalar, attended, *[column_output(p) for p in planes], middle)[None]


def solution(mesh):
    split = Mesh(mesh.devices.reshape(2, 2, 4, 2, 4), ("ylo", "core") + SEQ)
    dp = ("ylo", "core")
    every = dp + SEQ
    return jax.shard_map(
        shards,
        mesh=split,
        in_specs=(
            P(dp, SEQ, None),
            P(),
            P(every, None),
            P(every, None),
            P(),
            P(every, None),
            P(every, None),
            P(dp, None),
            P(),
        ),
        out_specs=P(dp, SEQ, None),
        check_vma=False,
    )
```

```python
import math

import jax
import jax.numpy as jnp
from jax import lax
from jax.experimental import pallas as pl
from jax.experimental.pallas import tpu as pltpu
from jax.sharding import Mesh, PartitionSpec as P

HEADS = 8
HEAD = 128
C = 512
SCALE = 8
D = 2048
WIDTH = HEADS * HEAD
N_SEQ = 32
COLS = C // N_SEQ
PAIR = 2 * HEAD
STEPS = WIDTH // PAIR
SEQ = ("x", "yhi", "z")
QKV_HALF = 3 * WIDTH // 2
PART = 4 * WIDTH
RELATIVE = tuple((ring, half * PART // 2, (half + 1) * PART // 2) for half in range(2) for ring in (0, 3, 1, 2))
RINGS = (0, 3, 1, 2)
LOG2E = 1.4426950408889634
MIB = 1 << 20


def frequencies(band_edges, half_size):
    dim_index = jnp.arange(half_size, dtype=jnp.float32)
    base_freq = jnp.power(10000.0, -dim_index / half_size)
    lower_edge = band_edges[0].astype(jnp.float32)
    upper_edge = band_edges[1].astype(jnp.float32)
    ramp_share = jnp.clip((dim_index - lower_edge) / (upper_edge - lower_edge), 0.0, 1.0)
    return base_freq * (1.0 - ramp_share) + base_freq * ramp_share / SCALE


def rotary_tables(positions, frequency):
    angles = positions.astype(jnp.float32)[:, None] * frequency
    mscale = 0.1 * math.log(SCALE) + 1.0
    cosine = jnp.cos(angles) * mscale
    sine = jnp.sin(angles) * mscale
    return jnp.concatenate([cosine, cosine], -1), jnp.concatenate([-sine, sine], -1)


def dot(a, b):
    return jnp.dot(a, b, preferred_element_type=jnp.float32)


def dot_t(a, b):
    return lax.dot_general(a, b, (((1,), (1,)), ((), ())), preferred_element_type=jnp.float32)


def slot_of(block, core):
    other = jnp.where(lax.rem(block, 2) == core, 0, 2)
    return other + block // 2


def rotate(heads, cos, sin):
    return heads * cos + pltpu.roll(heads, HEAD // 2, 1) * sin


def softmax_times(scores, keep, values):
    scores = jnp.where(keep, scores, -1e30)
    top = jnp.max(scores, axis=-1, keepdims=True)
    weights = jnp.exp2((scores - top) * (LOG2E / math.sqrt(HEAD)))
    total = jnp.sum(weights, axis=-1, keepdims=True)
    return dot(weights.astype(jnp.bfloat16), values) / total


def norm_kernel(core_ref, x_ref, gain_ref, hid_ref):
    core = core_ref[0]

    def chunk(i, _):
        rows = pl.ds(pl.multiple_of(i * 32, 32), 32)
        x = x_ref[rows, :].astype(jnp.float32)
        inv = lax.rsqrt(jnp.mean(x * x, axis=-1, keepdims=True) + 1e-05)
        hidden = (x * inv * gain_ref[...]).astype(jnp.bfloat16)
        width = D // 4
        for block in range(4):
            lanes = pl.ds(pl.multiple_of(slot_of(block, core) * width, width), width)
            hid_ref[rows, lanes] = hidden[:, block * width : (block + 1) * width]
        return 0

    lax.fori_loop(0, C // 32, chunk, 0)


def normed_slots(core, x, gain):
    vmem = pl.BlockSpec(memory_space=pltpu.VMEM)
    hbm = pl.BlockSpec(memory_space=pltpu.HBM)
    return pl.pallas_call(
        norm_kernel,
        out_shape=jax.ShapeDtypeStruct((C, D), jnp.bfloat16),
        in_specs=[pl.BlockSpec(memory_space=pltpu.SMEM), vmem, vmem],
        out_specs=vmem,
        compiler_params=pltpu.CompilerParams(vmem_limit_bytes=16 * MIB),
        cost_estimate=pl.CostEstimate(flops=4 * C * D, bytes_accessed=4 * C * D, transcendentals=C),
    )(core, x, gain)


def start_copies(place_ref, pieces, sems, w_ref, o_ref):
    my_x, my_y = place_ref[1], place_ref[2]

    def block_of(stacked, ring):
        x = lax.rem(my_x + stacked, 4)
        y = lax.rem(my_y + ring, 4)
        return lax.rem(y, 2) * 8 + x * 2 + y // 2

    def move(slot, first, last, dst_of, sem):
        for index, (ring, low, high) in enumerate(RELATIVE):
            begin, end = max(low, first), min(high, last)
            if begin >= end:
                continue
            src = pieces[slot * len(RELATIVE) + index]
            for k, stacked in enumerate(RINGS):
                dst = dst_of(block_of(stacked, ring)).at[:, :, pl.ds(begin - first, end - begin)]
                pltpu.make_async_copy(src.at[k, :, :, pl.ds(begin - low, end - begin)], dst, sem).start()

    for group in range(2):
        for slot in range(2):
            move(
                slot,
                group * QKV_HALF,
                (group + 1) * QKV_HALF,
                lambda block: w_ref.at[slot, group, block],
                sems.at[slot * 2 + group],
            )
    for slot in range(2):
        move(slot, 2 * QKV_HALF, PART, lambda block: o_ref.at[slot, block], sems.at[4 + slot])


def arrived(ref, sem):
    pltpu.make_async_copy(ref, ref, sem).wait()


def step_weights(w_ref, sems, g):
    part = g // 2
    for p in range(2):

        @pl.when(g == 2 * p)
        def _():
            for slot in range(2):
                arrived(w_ref.at[slot, p], sems.at[slot * 2 + p])

    base = lax.rem(g, 2) * (3 * PAIR)

    def weight(slot, kind):
        lanes = pl.ds(pl.multiple_of(base + kind * PAIR, PAIR), PAIR)
        return w_ref[slot, part, :, :, :, lanes].reshape(D // 2, PAIR)

    return weight


def output_sum(core, att_ref, rows, o_ref, h, total):
    for slot in range(2):
        for j in range(2):
            block = (core if slot == 0 else 1 - core) + 2 * j
            lanes = pl.ds(pl.multiple_of(block * PAIR, PAIR), PAIR)
            weight = o_ref[slot, j * 8 : (j + 1) * 8, h].reshape(PAIR, D // 2)
            total = total + dot(att_ref[rows, lanes], weight)
    return total


def row_kernel(place_ref, x_ref, hid_ref, gain_ref, cos_ref, sin_ref, *refs):
    pieces = refs[: 2 * len(RELATIVE)]
    mid_ref, next_ref, w_ref, o_ref, att_ref, sems = refs[2 * len(RELATIVE) :]
    core = place_ref[0]
    start_copies(place_ref, pieces, sems, w_ref, o_ref)
    half = D // 2

    def step(g, _):
        weight = step_weights(w_ref, sems, g)

        def projected(kind):
            return dot(hid_ref[:, :half], weight(0, kind)) + dot(hid_ref[:, half:], weight(1, kind))

        q2 = projected(0)
        k2 = projected(1)
        v2 = projected(2).astype(jnp.bfloat16)
        for h in range(2):
            lanes = slice(h * HEAD, (h + 1) * HEAD)
            q = rotate(q2[:, lanes], cos_ref[...], sin_ref[...]).astype(jnp.bfloat16)
            k = rotate(k2[:, lanes], cos_ref[...], sin_ref[...]).astype(jnp.bfloat16)
            v = v2[:, lanes]
            size = 256
            for b in range(C // size):
                end = (b + 1) * size
                scores = dot_t(q[b * size : end], k[:end])
                row = lax.broadcasted_iota(jnp.int32, scores.shape, 0) + b * size
                keep = lax.broadcasted_iota(jnp.int32, scores.shape, 1) <= row
                target = pl.ds(pl.multiple_of(g * PAIR + h * HEAD, HEAD), HEAD)
                att_ref[b * size : end, target] = softmax_times(scores, keep, v[:end]).astype(jnp.bfloat16)
        return 0

    lax.fori_loop(0, STEPS, step, 0)
    for slot in range(2):
        arrived(o_ref.at[slot], sems.at[4 + slot])

    def finish(i, _):
        rows = pl.ds(pl.multiple_of(i * 128, 128), 128)
        halves = []
        squares = jnp.zeros((128, 1), jnp.float32)
        for h in range(2):
            lanes = slice(h * half, (h + 1) * half)
            total = output_sum(core, att_ref, rows, o_ref, h, x_ref[rows, lanes].astype(jnp.float32))
            middle = total.astype(jnp.bfloat16)
            mid_ref[rows, lanes] = middle
            middle = middle.astype(jnp.float32)
            squares = squares + jnp.sum(middle * middle, axis=-1, keepdims=True)
            halves.append(middle)
        inv = lax.rsqrt(squares / D + 1e-05)
        for h in range(2):
            lanes = slice(h * half, (h + 1) * half)
            next_ref[rows, lanes] = (halves[h] * inv * gain_ref[:, lanes]).astype(jnp.bfloat16)
        return 0

    lax.fori_loop(0, C // 128, finish, 0)


def row_layer(place, x, hidden, gain, tables, pieces):
    vmem = pl.BlockSpec(memory_space=pltpu.VMEM)
    hbm = pl.BlockSpec(memory_space=pltpu.HBM)
    shape = jax.ShapeDtypeStruct((C, D), jnp.bfloat16)
    return pl.pallas_call(
        row_kernel,
        out_shape=[shape, shape],
        in_specs=[pl.BlockSpec(memory_space=pltpu.SMEM)]
        + [vmem] * 5
        + [hbm] * len(pieces),
        out_specs=[vmem, vmem],
        scratch_shapes=[
            pltpu.VMEM((2, 2, 16, 2, 32, QKV_HALF), jnp.bfloat16),
            pltpu.VMEM((2, 16, 2, 32, D // 2), jnp.bfloat16),
            pltpu.VMEM((C, WIDTH), jnp.bfloat16),
            pltpu.SemaphoreType.DMA((6,)),
        ],
        compiler_params=pltpu.CompilerParams(vmem_limit_bytes=48 * MIB),
        cost_estimate=pl.CostEstimate(
            flops=2 * C * D * 4 * WIDTH + 4 * C * C * WIDTH,
            bytes_accessed=2 * (4 * C * D + 4 * D * WIDTH),
            transcendentals=C * C * HEADS,
        ),
    )(place, x, hidden, gain, *tables, *pieces)


def column_kernel(core_ref, x_ref, cos_ref, sin_ref, own_plane, other_plane, out_ref, w_ref, hid_ref, sems):
    core = core_ref[0]
    half = D // 2
    triple = 3 * PAIR

    for g in range(STEPS):
        lanes = pl.ds(g * triple, triple)
        for slot, plane in enumerate((own_plane, other_plane)):
            for ylo in range(2):
                for yhi in range(2):
                    src = plane.at[:, :, ylo, yhi, :, lanes]
                    dst = w_ref.at[g, slot, ylo, :, yhi]
                    pltpu.make_async_copy(src, dst, sems.at[g]).start()

    def selection(transposed):
        a = lax.broadcasted_iota(jnp.int32, (C, C), 1 if transposed else 0)
        b = lax.broadcasted_iota(jnp.int32, (C, C), 0 if transposed else 1)
        same = (a // N_SEQ == lax.rem(b, COLS)) & (lax.rem(a, N_SEQ) == b // COLS)
        return jnp.where(same, 1.0, 0.0).astype(jnp.bfloat16)

    pick = selection(False)
    width = D // 4
    for block in range(4):
        lanes = pl.ds(pl.multiple_of(slot_of(block, core) * width, width), width)
        moved = dot(pick, x_ref[:, block * width : (block + 1) * width])
        hid_ref[:, lanes] = moved.astype(jnp.bfloat16)

    back = selection(True)
    size = 128
    row = lax.broadcasted_iota(jnp.int32, (size, size), 0)
    col = lax.broadcasted_iota(jnp.int32, (size, size), 1)
    keep = (row // N_SEQ == col // N_SEQ) & (col <= row)

    def step(g, _):
        pltpu.make_async_copy(w_ref.at[g], w_ref.at[g], sems.at[g]).wait()

        def weight(slot, kind):
            lanes = slice(kind * PAIR, (kind + 1) * PAIR)
            return w_ref[g, slot, :, :, :, :, :, lanes].reshape(half, PAIR)

        def projected(kind):
            return dot(hid_ref[:, :half], weight(0, kind)) + dot(hid_ref[:, half:], weight(1, kind))

        q2 = projected(0)
        k2 = projected(1)
        v2 = projected(2).astype(jnp.bfloat16)
        heads = []
        for h in range(2):
            lanes = slice(h * HEAD, (h + 1) * HEAD)
            q = rotate(q2[:, lanes], cos_ref[...], sin_ref[...]).astype(jnp.bfloat16)
            k = rotate(k2[:, lanes], cos_ref[...], sin_ref[...]).astype(jnp.bfloat16)
            v = v2[:, lanes]
            blocks = []
            for b in range(C // size):
                rows = slice(b * size, (b + 1) * size)
                blocks.append(softmax_times(dot_t(q[rows], k[rows]), keep, v[rows]).astype(jnp.bfloat16))
            heads.append(jnp.concatenate(blocks, 0))
        attended = jnp.concatenate(heads, 1)
        lanes = pl.ds(pl.multiple_of(g * PAIR, PAIR), PAIR)
        out_ref[:, lanes] = dot(back, attended).astype(jnp.bfloat16)
        return 0

    lax.fori_loop(0, STEPS, step, 0)


def column_layer(core, x, tables, planes):
    vmem = pl.BlockSpec(memory_space=pltpu.VMEM)
    hbm = pl.BlockSpec(memory_space=pltpu.HBM)
    return pl.pallas_call(
        column_kernel,
        out_shape=jax.ShapeDtypeStruct((C, WIDTH), jnp.bfloat16),
        in_specs=[pl.BlockSpec(memory_space=pltpu.SMEM)] + [vmem] * 3 + [hbm] * 2,
        out_specs=vmem,
        scratch_shapes=[
            pltpu.VMEM((STEPS, 2, 2, 4, 2, 4, 16, 3 * PAIR), jnp.bfloat16),
            pltpu.VMEM((C, D), jnp.bfloat16),
            pltpu.SemaphoreType.DMA((STEPS,)),
        ],
        compiler_params=pltpu.CompilerParams(vmem_limit_bytes=56 * MIB),
        cost_estimate=pl.CostEstimate(
            flops=2 * C * D * 3 * WIDTH + 4 * C * C * WIDTH,
            bytes_accessed=2 * (C * D + 3 * D * WIDTH + C * WIDTH),
            transcendentals=C * C * HEADS,
        ),
    )(core, x, *tables, *planes)


def branch_sum(core, att_ref, own_ref, other_ref, resid_ref):
    width = WIDTH // 4
    total = resid_ref[...].astype(jnp.float32)
    for slot in range(4):
        block = jnp.where(slot < 2, core, 1 - core) + 2 * (slot % 2)
        lanes = pl.ds(pl.multiple_of(block * width, width), width)
        ref = own_ref if slot < 2 else other_ref
        rows = slice((slot % 2) * width, (slot % 2 + 1) * width)
        total = total + dot(att_ref[:, lanes], ref[rows, :])
    return total


def final_kernel(core_ref, att_ref, own_ref, other_ref, resid_ref, out_ref):
    out_ref[...] = branch_sum(core_ref[0], att_ref, own_ref, other_ref, resid_ref).astype(jnp.bfloat16)


def output_layer(core, attended, own, other, resid):
    size = 128
    block = lambda width: pl.BlockSpec((size, width), lambda i: (i, 0))
    whole = lambda shape: pl.BlockSpec(shape, lambda i: (0, 0), pipeline_mode=pl.Buffered(1))
    return pl.pallas_call(
        final_kernel,
        grid=(C // size,),
        out_shape=jax.ShapeDtypeStruct((C, D), jnp.bfloat16),
        in_specs=[
            pl.BlockSpec(memory_space=pltpu.SMEM),
            block(WIDTH),
            whole(own.shape),
            whole(other.shape),
            block(D),
        ],
        out_specs=block(D),
        compiler_params=pltpu.CompilerParams(
            dimension_semantics=("arbitrary",), vmem_limit_bytes=40 * MIB
        ),
        cost_estimate=pl.CostEstimate(
            flops=2 * C * D * WIDTH,
            bytes_accessed=2 * (2 * C * D + D * WIDTH + C * WIDTH),
            transcendentals=0,
        ),
    )(core, attended, own, other, resid)


def shift(value, axis, by):
    if axis == "y":
        where = lambda y: (y % 2) * 2 + y // 2
        return lax.ppermute(value, ("ylo", "yhi"), [(where(y), where((y + by) % 4)) for y in range(4)])
    return lax.ppermute(value, axis, [(i, (i + by) % 4) for i in range(4)])


def first_hops(value, axis):
    return [value, shift(value, axis, 1), shift(value, axis, -1)]


def forwards(hops, axis):
    own, left, right = hops
    half = own.shape[-1] // 2
    return hops + [shift(left[..., :half], axis, 1), shift(right[..., half:], axis, -1)]


def stack(pieces):
    own, left, right, low, high = pieces
    return jnp.stack([own, left, right, jnp.concatenate([low, high], -1)])


def outer_ring(value):
    half = value.shape[-1] // 2
    low, high = value[..., :half], value[..., half:]
    pieces = []
    hops = [(part, shift(part, "y", 1), shift(part, "y", -1)) for part in (low, high)]
    for index, (own, left, right) in enumerate(hops):
        far = shift(right, "y", -1) if index else shift(left, "y", 1)
        pieces += [own, left, right, far]
    return pieces


def swap(value):
    return lax.ppermute(value, "core", [(0, 1), (1, 0)])


def fold_output(output):
    return jnp.concatenate([output[:, : D // 2], output[:, D // 2 :]], 0)


def by_step(inputs):
    return inputs.reshape(-1, 3, STEPS, PAIR).transpose(0, 2, 1, 3).reshape(-1, 3 * WIDTH)


def row_stack(inputs, output):
    shard = jnp.concatenate([by_step(inputs), fold_output(output)], 1)
    rows = lax.all_gather(shard, "z", axis=0)
    qkv = rows[:, :, : 3 * WIDTH].reshape(2, 32, 3 * WIDTH)
    out = rows[:, :, 3 * WIDTH :].reshape(4, 2, 8, WIDTH).transpose(1, 0, 2, 3).reshape(2, 32, WIDTH)
    hops = first_hops(jnp.concatenate([qkv, out], -1), "x")
    return hops, stack(forwards(hops, "x"))


def column_line(inputs, output):
    shard = jnp.concatenate([by_step(inputs), fold_output(output)], 1)
    return lax.all_gather(shard, ("ylo", "yhi"), axis=0)


def column_plane(line):
    return lax.all_gather(line, ("x", "z"), axis=0).reshape(4, 4, 2, 2, 16, 4 * WIDTH)


def column_output(plane):
    out = plane[..., 3 * WIDTH :].transpose(2, 0, 3, 1, 4, 5)
    return out.reshape(64, 2, 8, WIDTH).transpose(0, 2, 1, 3).reshape(WIDTH // 2, D)


def shards(tokens, gain_first, inputs_first, output_first, gain_second, inputs_second, output_second, starts, band_edges):
    residual = tokens[0]
    core = lax.axis_index("core").astype(jnp.int32)
    core_scalar = core.reshape(1)
    seq = lax.axis_index(SEQ)
    my_y = lax.axis_index("yhi") * 2 + lax.axis_index("ylo")
    place = jnp.stack([core, lax.axis_index("x").astype(jnp.int32), my_y.astype(jnp.int32)])

    frequency = frequencies(band_edges, HEAD // 2)
    block_starts = starts[0]
    own_start = lax.dynamic_index_in_dim(block_starts, seq, 0, keepdims=False)
    row_tables = rotary_tables(own_start + jnp.arange(C, dtype=jnp.int32), frequency)
    columns = seq.astype(jnp.int32) * COLS + jnp.arange(COLS, dtype=jnp.int32)
    column_positions = (columns[:, None] + block_starts[None, :]).reshape(C)
    column_tables = rotary_tables(column_positions, frequency)

    hidden = normed_slots(core_scalar, residual, gain_first.reshape(1, D))

    inner_hops, own_stack = row_stack(inputs_first, output_first)
    line, _ = lax.optimization_barrier((column_line(inputs_second, output_second), inner_hops))
    plane = column_plane(line)
    pieces = outer_ring(own_stack)
    early, hidden, row_tables, column_tables = lax.optimization_barrier(
        (pieces[0], hidden, row_tables, column_tables)
    )
    pieces = pieces + [swap(early)] + [swap(piece) for piece in pieces[1:]]

    middle, hidden = row_layer(place, residual, hidden, gain_second.reshape(1, D), row_tables, pieces)
    plane, hidden = lax.optimization_barrier((plane, hidden))
    planes = (plane, swap(plane))
    hidden = lax.all_to_all(hidden, SEQ, split_axis=0, concat_axis=0, tiled=True)
    attended = column_layer(core_scalar, hidden, column_tables, planes)
    attended = lax.all_to_all(attended, SEQ, split_axis=0, concat_axis=0, tiled=True)
    return output_layer(core_scalar, attended, *[column_output(p) for p in planes], middle)[None]


def solution(mesh):
    split = Mesh(mesh.devices.reshape(2, 2, 4, 2, 4), ("ylo", "core") + SEQ)
    dp = ("ylo", "core")
    every = dp + SEQ
    return jax.shard_map(
        shards,
        mesh=split,
        in_specs=(
            P(dp, SEQ, None),
            P(),
            P(every, None),
            P(every, None),
            P(),
            P(every, None),
            P(every, None),
            P(dp, None),
            P(),
        ),
        out_specs=P(dp, SEQ, None),
        check_vma=False,
    )
```

```python
import math

import jax
import jax.numpy as jnp
from jax import lax
from jax.experimental import pallas as pl
from jax.experimental.pallas import tpu as pltpu
from jax.sharding import Mesh, PartitionSpec as P

HEADS = 8
HEAD = 128
C = 512
SCALE = 8
D = 2048
WIDTH = HEADS * HEAD
N_SEQ = 32
COLS = C // N_SEQ
PAIR = 2 * HEAD
STEPS = WIDTH // PAIR
SEQ = ("x", "yhi", "z")
QKV_HALF = 3 * WIDTH // 2
PART = 4 * WIDTH
RELATIVE = ((0, 0, PART), (3, 0, PART), (1, 0, PART), (2, 0, PART // 2), (2, PART // 2, PART))
RINGS = (0, 3, 1, 2)
LOG2E = 1.4426950408889634
MIB = 1 << 20


def frequencies(band_edges, half_size):
    dim_index = jnp.arange(half_size, dtype=jnp.float32)
    base_freq = jnp.power(10000.0, -dim_index / half_size)
    lower_edge = band_edges[0].astype(jnp.float32)
    upper_edge = band_edges[1].astype(jnp.float32)
    ramp_share = jnp.clip((dim_index - lower_edge) / (upper_edge - lower_edge), 0.0, 1.0)
    return base_freq * (1.0 - ramp_share) + base_freq * ramp_share / SCALE


def rotary_tables(positions, frequency):
    angles = positions.astype(jnp.float32)[:, None] * frequency
    mscale = 0.1 * math.log(SCALE) + 1.0
    cosine = jnp.cos(angles) * mscale
    sine = jnp.sin(angles) * mscale
    return jnp.concatenate([cosine, cosine], -1), jnp.concatenate([-sine, sine], -1)


def dot(a, b):
    return jnp.dot(a, b, preferred_element_type=jnp.float32)


def dot_t(a, b):
    return lax.dot_general(a, b, (((1,), (1,)), ((), ())), preferred_element_type=jnp.float32)


def slot_of(block, core):
    other = jnp.where(lax.rem(block, 2) == core, 0, 2)
    return other + block // 2


def rotate(heads, cos, sin):
    return heads * cos + pltpu.roll(heads, HEAD // 2, 1) * sin


def softmax_times(scores, keep, values):
    scores = jnp.where(keep, scores, -1e30)
    top = jnp.max(scores, axis=-1, keepdims=True)
    weights = jnp.exp2((scores - top) * (LOG2E / math.sqrt(HEAD)))
    total = jnp.sum(weights, axis=-1, keepdims=True)
    return dot(weights.astype(jnp.bfloat16), values) / total


def norm_kernel(core_ref, x_ref, gain_ref, hid_ref):
    core = core_ref[0]

    def chunk(i, _):
        rows = pl.ds(pl.multiple_of(i * 32, 32), 32)
        x = x_ref[rows, :].astype(jnp.float32)
        inv = lax.rsqrt(jnp.mean(x * x, axis=-1, keepdims=True) + 1e-05)
        hidden = (x * inv * gain_ref[...]).astype(jnp.bfloat16)
        width = D // 4
        for block in range(4):
            lanes = pl.ds(pl.multiple_of(slot_of(block, core) * width, width), width)
            hid_ref[rows, lanes] = hidden[:, block * width : (block + 1) * width]
        return 0

    lax.fori_loop(0, C // 32, chunk, 0)


def normed_slots(core, x, gain):
    vmem = pl.BlockSpec(memory_space=pltpu.VMEM)
    hbm = pl.BlockSpec(memory_space=pltpu.HBM)
    return pl.pallas_call(
        norm_kernel,
        out_shape=jax.ShapeDtypeStruct((C, D), jnp.bfloat16),
        in_specs=[pl.BlockSpec(memory_space=pltpu.SMEM), vmem, vmem],
        out_specs=vmem,
        compiler_params=pltpu.CompilerParams(vmem_limit_bytes=16 * MIB),
        cost_estimate=pl.CostEstimate(flops=4 * C * D, bytes_accessed=4 * C * D, transcendentals=C),
    )(core, x, gain)


def start_copies(place_ref, pieces, sems, w_ref, o_ref):
    my_x, my_y = place_ref[1], place_ref[2]

    def block_of(stacked, ring):
        x = lax.rem(my_x + stacked, 4)
        y = lax.rem(my_y + ring, 4)
        return lax.rem(y, 2) * 8 + x * 2 + y // 2

    def move(slot, first, last, dst_of, sem):
        for index, (ring, low, high) in enumerate(RELATIVE):
            begin, end = max(low, first), min(high, last)
            if begin >= end:
                continue
            src = pieces[slot * len(RELATIVE) + index]
            for k, stacked in enumerate(RINGS):
                dst = dst_of(block_of(stacked, ring)).at[:, :, pl.ds(begin - first, end - begin)]
                pltpu.make_async_copy(src.at[k, :, :, pl.ds(begin - low, end - begin)], dst, sem).start()

    for group in range(2):
        for slot in range(2):
            move(
                slot,
                group * QKV_HALF,
                (group + 1) * QKV_HALF,
                lambda block: w_ref.at[slot, group, block],
                sems.at[slot * 2 + group],
            )
    for slot in range(2):
        move(slot, 2 * QKV_HALF, PART, lambda block: o_ref.at[slot, block], sems.at[4 + slot])


def arrived(ref, sem):
    pltpu.make_async_copy(ref, ref, sem).wait()


def step_weights(w_ref, sems, g):
    part = g // 2
    for p in range(2):

        @pl.when(g == 2 * p)
        def _():
            for slot in range(2):
                arrived(w_ref.at[slot, p], sems.at[slot * 2 + p])

    base = lax.rem(g, 2) * (3 * PAIR)

    def weight(slot, kind):
        lanes = pl.ds(pl.multiple_of(base + kind * PAIR, PAIR), PAIR)
        return w_ref[slot, part, :, :, :, lanes].reshape(D // 2, PAIR)

    return weight


def output_sum(core, att_ref, rows, o_ref, h, total):
    for slot in range(2):
        for j in range(2):
            block = (core if slot == 0 else 1 - core) + 2 * j
            lanes = pl.ds(pl.multiple_of(block * PAIR, PAIR), PAIR)
            weight = o_ref[slot, j * 8 : (j + 1) * 8, h].reshape(PAIR, D // 2)
            total = total + dot(att_ref[rows, lanes], weight)
    return total


def row_kernel(place_ref, x_ref, hid_ref, gain_ref, cos_ref, sin_ref, *refs):
    pieces = refs[: 2 * len(RELATIVE)]
    mid_ref, next_ref, w_ref, o_ref, att_ref, sems = refs[2 * len(RELATIVE) :]
    core = place_ref[0]
    start_copies(place_ref, pieces, sems, w_ref, o_ref)
    half = D // 2

    def step(g, _):
        weight = step_weights(w_ref, sems, g)

        def projected(kind):
            return dot(hid_ref[:, :half], weight(0, kind)) + dot(hid_ref[:, half:], weight(1, kind))

        q2 = projected(0)
        k2 = projected(1)
        v2 = projected(2).astype(jnp.bfloat16)
        for h in range(2):
            lanes = slice(h * HEAD, (h + 1) * HEAD)
            q = rotate(q2[:, lanes], cos_ref[...], sin_ref[...]).astype(jnp.bfloat16)
            k = rotate(k2[:, lanes], cos_ref[...], sin_ref[...]).astype(jnp.bfloat16)
            v = v2[:, lanes]
            size = 128
            for b in range(C // size):
                end = (b + 1) * size
                scores = dot_t(q[b * size : end], k[:end])
                row = lax.broadcasted_iota(jnp.int32, scores.shape, 0) + b * size
                keep = lax.broadcasted_iota(jnp.int32, scores.shape, 1) <= row
                target = pl.ds(pl.multiple_of(g * PAIR + h * HEAD, HEAD), HEAD)
                att_ref[b * size : end, target] = softmax_times(scores, keep, v[:end]).astype(jnp.bfloat16)
        return 0

    lax.fori_loop(0, STEPS, step, 0)
    for slot in range(2):
        arrived(o_ref.at[slot], sems.at[4 + slot])

    def finish(i, _):
        rows = pl.ds(pl.multiple_of(i * 128, 128), 128)
        halves = []
        squares = jnp.zeros((128, 1), jnp.float32)
        for h in range(2):
            lanes = slice(h * half, (h + 1) * half)
            total = output_sum(core, att_ref, rows, o_ref, h, x_ref[rows, lanes].astype(jnp.float32))
            middle = total.astype(jnp.bfloat16)
            mid_ref[rows, lanes] = middle
            middle = middle.astype(jnp.float32)
            squares = squares + jnp.sum(middle * middle, axis=-1, keepdims=True)
            halves.append(middle)
        inv = lax.rsqrt(squares / D + 1e-05)
        for h in range(2):
            lanes = slice(h * half, (h + 1) * half)
            next_ref[rows, lanes] = (halves[h] * inv * gain_ref[:, lanes]).astype(jnp.bfloat16)
        return 0

    lax.fori_loop(0, C // 128, finish, 0)


def row_layer(place, x, hidden, gain, tables, pieces):
    vmem = pl.BlockSpec(memory_space=pltpu.VMEM)
    hbm = pl.BlockSpec(memory_space=pltpu.HBM)
    shape = jax.ShapeDtypeStruct((C, D), jnp.bfloat16)
    return pl.pallas_call(
        row_kernel,
        out_shape=[shape, shape],
        in_specs=[pl.BlockSpec(memory_space=pltpu.SMEM)]
        + [vmem] * 5
        + [hbm] * len(pieces),
        out_specs=[vmem, vmem],
        scratch_shapes=[
            pltpu.VMEM((2, 2, 16, 2, 32, QKV_HALF), jnp.bfloat16),
            pltpu.VMEM((2, 16, 2, 32, D // 2), jnp.bfloat16),
            pltpu.VMEM((C, WIDTH), jnp.bfloat16),
            pltpu.SemaphoreType.DMA((6,)),
        ],
        compiler_params=pltpu.CompilerParams(vmem_limit_bytes=48 * MIB),
        cost_estimate=pl.CostEstimate(
            flops=2 * C * D * 4 * WIDTH + 4 * C * C * WIDTH,
            bytes_accessed=2 * (4 * C * D + 4 * D * WIDTH),
            transcendentals=C * C * HEADS,
        ),
    )(place, x, hidden, gain, *tables, *pieces)


def column_kernel(core_ref, x_ref, cos_ref, sin_ref, own_plane, other_plane, out_ref, w_ref, hid_ref, sems):
    core = core_ref[0]
    half = D // 2
    triple = 3 * PAIR

    for g in range(STEPS):
        lanes = pl.ds(g * triple, triple)
        for slot, plane in enumerate((own_plane, other_plane)):
            for ylo in range(2):
                for yhi in range(2):
                    src = plane.at[:, :, ylo, yhi, :, lanes]
                    dst = w_ref.at[g, slot, ylo, :, yhi]
                    pltpu.make_async_copy(src, dst, sems.at[g]).start()

    def selection(transposed):
        a = lax.broadcasted_iota(jnp.int32, (C, C), 1 if transposed else 0)
        b = lax.broadcasted_iota(jnp.int32, (C, C), 0 if transposed else 1)
        same = (a // N_SEQ == lax.rem(b, COLS)) & (lax.rem(a, N_SEQ) == b // COLS)
        return jnp.where(same, 1.0, 0.0).astype(jnp.bfloat16)

    pick = selection(False)
    width = D // 4
    for block in range(4):
        lanes = pl.ds(pl.multiple_of(slot_of(block, core) * width, width), width)
        moved = dot(pick, x_ref[:, block * width : (block + 1) * width])
        hid_ref[:, lanes] = moved.astype(jnp.bfloat16)

    back = selection(True)
    size = 128
    row = lax.broadcasted_iota(jnp.int32, (size, size), 0)
    col = lax.broadcasted_iota(jnp.int32, (size, size), 1)
    keep = (row // N_SEQ == col // N_SEQ) & (col <= row)

    def step(g, _):
        pltpu.make_async_copy(w_ref.at[g], w_ref.at[g], sems.at[g]).wait()

        def weight(slot, kind):
            lanes = slice(kind * PAIR, (kind + 1) * PAIR)
            return w_ref[g, slot, :, :, :, :, :, lanes].reshape(half, PAIR)

        def projected(kind):
            return dot(hid_ref[:, :half], weight(0, kind)) + dot(hid_ref[:, half:], weight(1, kind))

        q2 = projected(0)
        k2 = projected(1)
        v2 = projected(2).astype(jnp.bfloat16)
        heads = []
        for h in range(2):
            lanes = slice(h * HEAD, (h + 1) * HEAD)
            q = rotate(q2[:, lanes], cos_ref[...], sin_ref[...]).astype(jnp.bfloat16)
            k = rotate(k2[:, lanes], cos_ref[...], sin_ref[...]).astype(jnp.bfloat16)
            v = v2[:, lanes]
            blocks = []
            for b in range(C // size):
                rows = slice(b * size, (b + 1) * size)
                blocks.append(softmax_times(dot_t(q[rows], k[rows]), keep, v[rows]).astype(jnp.bfloat16))
            heads.append(jnp.concatenate(blocks, 0))
        attended = jnp.concatenate(heads, 1)
        lanes = pl.ds(pl.multiple_of(g * PAIR, PAIR), PAIR)
        out_ref[:, lanes] = dot(back, attended).astype(jnp.bfloat16)
        return 0

    lax.fori_loop(0, STEPS, step, 0)


def column_layer(core, x, tables, planes):
    vmem = pl.BlockSpec(memory_space=pltpu.VMEM)
    hbm = pl.BlockSpec(memory_space=pltpu.HBM)
    return pl.pallas_call(
        column_kernel,
        out_shape=jax.ShapeDtypeStruct((C, WIDTH), jnp.bfloat16),
        in_specs=[pl.BlockSpec(memory_space=pltpu.SMEM)] + [vmem] * 3 + [hbm] * 2,
        out_specs=vmem,
        scratch_shapes=[
            pltpu.VMEM((STEPS, 2, 2, 4, 2, 4, 16, 3 * PAIR), jnp.bfloat16),
            pltpu.VMEM((C, D), jnp.bfloat16),
            pltpu.SemaphoreType.DMA((STEPS,)),
        ],
        compiler_params=pltpu.CompilerParams(vmem_limit_bytes=56 * MIB),
        cost_estimate=pl.CostEstimate(
            flops=2 * C * D * 3 * WIDTH + 4 * C * C * WIDTH,
            bytes_accessed=2 * (C * D + 3 * D * WIDTH + C * WIDTH),
            transcendentals=C * C * HEADS,
        ),
    )(core, x, *tables, *planes)


def branch_sum(core, att_ref, own_ref, other_ref, resid_ref):
    width = WIDTH // 4
    total = resid_ref[...].astype(jnp.float32)
    for slot in range(4):
        block = jnp.where(slot < 2, core, 1 - core) + 2 * (slot % 2)
        lanes = pl.ds(pl.multiple_of(block * width, width), width)
        ref = own_ref if slot < 2 else other_ref
        rows = slice((slot % 2) * width, (slot % 2 + 1) * width)
        total = total + dot(att_ref[:, lanes], ref[rows, :])
    return total


def final_kernel(core_ref, att_ref, own_ref, other_ref, resid_ref, out_ref):
    out_ref[...] = branch_sum(core_ref[0], att_ref, own_ref, other_ref, resid_ref).astype(jnp.bfloat16)


def output_layer(core, attended, own, other, resid):
    size = 128
    block = lambda width: pl.BlockSpec((size, width), lambda i: (i, 0))
    whole = lambda shape: pl.BlockSpec(shape, lambda i: (0, 0), pipeline_mode=pl.Buffered(1))
    return pl.pallas_call(
        final_kernel,
        grid=(C // size,),
        out_shape=jax.ShapeDtypeStruct((C, D), jnp.bfloat16),
        in_specs=[
            pl.BlockSpec(memory_space=pltpu.SMEM),
            block(WIDTH),
            whole(own.shape),
            whole(other.shape),
            block(D),
        ],
        out_specs=block(D),
        compiler_params=pltpu.CompilerParams(
            dimension_semantics=("arbitrary",), vmem_limit_bytes=40 * MIB
        ),
        cost_estimate=pl.CostEstimate(
            flops=2 * C * D * WIDTH,
            bytes_accessed=2 * (2 * C * D + D * WIDTH + C * WIDTH),
            transcendentals=0,
        ),
    )(core, attended, own, other, resid)


def shift(value, axis, by):
    if axis == "y":
        where = lambda y: (y % 2) * 2 + y // 2
        return lax.ppermute(value, ("ylo", "yhi"), [(where(y), where((y + by) % 4)) for y in range(4)])
    return lax.ppermute(value, axis, [(i, (i + by) % 4) for i in range(4)])


def first_hops(value, axis):
    return [value, shift(value, axis, 1), shift(value, axis, -1)]


def forwards(hops, axis):
    own, left, right = hops
    half = own.shape[-1] // 2
    return hops + [shift(left[..., :half], axis, 1), shift(right[..., half:], axis, -1)]


def stack(pieces):
    own, left, right, low, high = pieces
    return jnp.stack([own, left, right, jnp.concatenate([low, high], -1)])


def swap(value):
    return lax.ppermute(value, "core", [(0, 1), (1, 0)])


def fold_output(output):
    return jnp.concatenate([output[:, : D // 2], output[:, D // 2 :]], 0)


def by_step(inputs):
    return inputs.reshape(-1, 3, STEPS, PAIR).transpose(0, 2, 1, 3).reshape(-1, 3 * WIDTH)


def row_stack(inputs, output):
    shard = jnp.concatenate([by_step(inputs), fold_output(output)], 1)
    rows = lax.all_gather(shard, "z", axis=0)
    qkv = rows[:, :, : 3 * WIDTH].reshape(2, 32, 3 * WIDTH)
    out = rows[:, :, 3 * WIDTH :].reshape(4, 2, 8, WIDTH).transpose(1, 0, 2, 3).reshape(2, 32, WIDTH)
    hops = first_hops(jnp.concatenate([qkv, out], -1), "x")
    return hops, stack(forwards(hops, "x"))


def column_line(inputs, output):
    shard = jnp.concatenate([by_step(inputs), fold_output(output)], 1)
    return lax.all_gather(shard, ("ylo", "yhi"), axis=0)


def column_plane(line):
    return lax.all_gather(line, ("x", "z"), axis=0).reshape(4, 4, 2, 2, 16, 4 * WIDTH)


def column_output(plane):
    out = plane[..., 3 * WIDTH :].transpose(2, 0, 3, 1, 4, 5)
    return out.reshape(64, 2, 8, WIDTH).transpose(0, 2, 1, 3).reshape(WIDTH // 2, D)


def shards(tokens, gain_first, inputs_first, output_first, gain_second, inputs_second, output_second, starts, band_edges):
    residual = tokens[0]
    core = lax.axis_index("core").astype(jnp.int32)
    core_scalar = core.reshape(1)
    seq = lax.axis_index(SEQ)
    my_y = lax.axis_index("yhi") * 2 + lax.axis_index("ylo")
    place = jnp.stack([core, lax.axis_index("x").astype(jnp.int32), my_y.astype(jnp.int32)])

    frequency = frequencies(band_edges, HEAD // 2)
    block_starts = starts[0]
    own_start = lax.dynamic_index_in_dim(block_starts, seq, 0, keepdims=False)
    row_tables = rotary_tables(own_start + jnp.arange(C, dtype=jnp.int32), frequency)
    columns = seq.astype(jnp.int32) * COLS + jnp.arange(COLS, dtype=jnp.int32)
    column_positions = (columns[:, None] + block_starts[None, :]).reshape(C)
    column_tables = rotary_tables(column_positions, frequency)

    hidden = normed_slots(core_scalar, residual, gain_first.reshape(1, D))

    inner_hops, own_stack = row_stack(inputs_first, output_first)
    line, _ = lax.optimization_barrier((column_line(inputs_second, output_second), inner_hops))
    plane = column_plane(line)
    pieces = forwards(first_hops(own_stack, "y"), "y")
    own_stack, hidden, row_tables, column_tables = lax.optimization_barrier(
        (own_stack, hidden, row_tables, column_tables)
    )
    pieces = pieces + [swap(own_stack)] + [swap(piece) for piece in pieces[1:]]

    middle, hidden = row_layer(place, residual, hidden, gain_second.reshape(1, D), row_tables, pieces)
    plane, hidden = lax.optimization_barrier((plane, hidden))
    planes = (plane, swap(plane))
    hidden = lax.all_to_all(hidden, SEQ, split_axis=0, concat_axis=0, tiled=True)
    attended = column_layer(core_scalar, hidden, column_tables, planes)
    attended = lax.all_to_all(attended, SEQ, split_axis=0, concat_axis=0, tiled=True)
    return output_layer(core_scalar, attended, *[column_output(p) for p in planes], middle)[None]


def solution(mesh):
    split = Mesh(mesh.devices.reshape(2, 2, 4, 2, 4), ("ylo", "core") + SEQ)
    dp = ("ylo", "core")
    every = dp + SEQ
    return jax.shard_map(
        shards,
        mesh=split,
        in_specs=(
            P(dp, SEQ, None),
            P(),
            P(every, None),
            P(every, None),
            P(),
            P(every, None),
            P(every, None),
            P(dp, None),
            P(),
        ),
        out_specs=P(dp, SEQ, None),
        check_vma=False,
    )
```
